512 devices in a mesh: dp: 16 (over y, z_lo), tensor: 32 (over z_hi, x, core).
Axes of the slice: x: 4, y: 8, z: 8 (z_hi: 4, z_lo: 2; z = z_hi * 2 + z_lo), core: 2. Of those that a mesh axis runs over, the one named last changes fastest.
Arguments:
- hidden_in: bfloat16 [16, 32, 1, 64, 1536], P('dp', 'tensor'), may hold values from -6 to 6
- rotated_queries: bfloat16 [16, 32, 1, 64, 1536], P('dp', 'tensor'), may hold values from -8 to 8
- fresh_key_values: bfloat16 [16, 32, 1, 64, 1024], P('dp', 'tensor'), may hold values from -6 to 6
- cached_key_values: bfloat16 [16, 1024, 1024], P('dp', 'tensor'), may hold values from -8 to 8
- cached_len: int32 [16], P('dp'), may hold values from 8 to 1024, as said below
- expert_ids: int32 [16, 32, 1, 64, 8], P('dp', 'tensor'), may hold values from 0 to 31, all different within a row; in each aligned block of 64 rows (0 to 63, 64 to 127, ..., all dimensions but the last counted through in order) at most 17 rows name the same one
- route_gates: float32 [16, 32, 1, 64, 8], P('dp', 'tensor'), may hold values from 0.1 to 0.4
- output_weight: bfloat16 [1536, 1536], P('tensor'), may hold values from -3 to 3
- norm_gain: float32 [1536], replicated, may hold values from 0.1 to 1.9
- gate_up: bfloat16 [32, 1536, 1024], P('tensor', 'dp'), may hold values from -0.15625 to 0.15625
- down_weight: bfloat16 [32, 512, 1536], P('tensor', 'dp'), may hold values from -0.25 to 0.25
Outputs:
- hidden_out: bfloat16 [16, 32, 1, 64, 1536], P('dp', 'tensor')
- cache_out: bfloat16 [16, 3072, 1024], P('dp', None, 'tensor')
The draws below stay inside these ranges and needn't reach their ends.
Inputs may be any that keep to these rules, and one draw needn't show every extreme that they name: `cached_len`: some request has exactly 1024 valid slots. `expert_ids`: among the 64 tokens of one device no expert is chosen more than 17 times, and on some device some expert is chosen exactly 17 times.
All inputs are finite; a program needn't handle non-finite values.
Results may differ from the reference program's by a relative error of at most 0.006.
Values may be sent and summed in bfloat16 or wider, within the bound.
No kernel may reach another device: no remote copies, remote signals or barrier semaphores. Data moves between devices by JAX's collectives and lax.ppermute only.
A program may use at most 64 MiB of HBM per device.

```python
import math
import jax
import jax.numpy as jnp
import numpy as np
from jax import lax

MODEL_WIDTH = 1536
QUERY_HEADS = 24
KEY_VALUE_HEADS = 8
HEAD_WIDTH = 64
FFE = 512
TOPK = 8
REQ_GRP = 1
NEW_DEV = 64
REQUEST_COUNT = 16
FRESH_POSITIONS = 2048
CACHE_SLOT_LIMIT = 1024
TOK_DEV = 64
KVW = 1024
EXPERTS = 32
CAP = 17
N_DP = 16
N_TENSOR = 32


def draw_rotated_queries(key, part):
    rows_all = N_DP * N_TENSOR * REQ_GRP * NEW_DEV
    sampled_values = jnp.clip(jax.random.normal(jax.random.fold_in(key, 11), (rows_all, QUERY_HEADS, HEAD_WIDTH), jnp.float32), -8.0, 8.0)
    return sampled_values.reshape(N_DP, N_TENSOR, REQ_GRP, NEW_DEV, QUERY_HEADS * HEAD_WIDTH).astype(jnp.bfloat16)


def draw_cached_key_values(key, part):
    complete_shape = (REQUEST_COUNT, CACHE_SLOT_LIMIT, KEY_VALUE_HEADS, 2 * HEAD_WIDTH)
    sampled_values = jnp.clip(jax.random.normal(jax.random.fold_in(key, 12), complete_shape, jnp.float32), -8.0, 8.0)
    return sampled_values.reshape(REQUEST_COUNT, CACHE_SLOT_LIMIT, 2 * KEY_VALUE_HEADS * HEAD_WIDTH).astype(jnp.bfloat16)


def draw_cached_len(key, part):
    lengths = jax.random.randint(jax.random.fold_in(key, 21), (REQUEST_COUNT,), 8, CACHE_SLOT_LIMIT + 1)
    picked = jax.random.randint(jax.random.fold_in(key, 22), (), 0, REQUEST_COUNT)
    return jnp.where(jnp.arange(REQUEST_COUNT) == picked, CACHE_SLOT_LIMIT, lengths).astype(jnp.int32)


def block_levels(key, shape, split, least, largest):
    gain = 1.0
    for position, parts in split:
        draws = jax.random.uniform(jax.random.fold_in(jax.random.fold_in(key, 6), position), (parts,), jnp.float32, least / len(split), largest / len(split))
        gain = gain * jnp.repeat(jnp.exp(draws), shape[position] // parts).reshape((-1,) + (1,) * (len(shape) - 1 - position))
    return gain


def deal_out(own_key, own, number, rows, number_of, top, limit, lean):
    order = jax.random.permutation(own_key, number_of)
    crowded, common = load_shares(number_of, rows * top, limit, lean, True), load_shares(number_of, rows * top, limit, lean, False)
    places = jnp.arange(number_of)

    def named(sizes, turn):
        used = int((sizes > 0).sum())
        fixed = max(1, used // 4)
        shifted = fixed + (places - fixed + turn * (used - fixed)) % max(1, number_of - fixed)
        return jnp.zeros((number_of,), jnp.int32).at[order[jnp.where(places < fixed, places, shifted)]].set(jnp.asarray(sizes, jnp.int32))

    sizes = jnp.where(number % 4 == 0, named(crowded, number // 4), named(common, number - number // 4 - 1))
    mixed = jax.random.permutation(jax.random.fold_in(own, 3), number_of)
    source_of, taker = mixed[0:number_of // 2 * 2:2], mixed[1:number_of // 2 * 2:2]
    margin = jnp.minimum(sizes[source_of] - 1, limit - sizes[taker]) // 2
    margin = jnp.where((source_of == order[0]) | (taker == order[0]) | (sizes[taker] == 0), 0, jnp.maximum(margin, 0))
    shifted = jax.random.randint(jax.random.fold_in(own, 4), (number_of // 2,), 0, 1 << 20) % (margin + 1)
    sizes = sizes.at[source_of].add(-shifted).at[taker].add(shifted)
    members = jnp.searchsorted(jnp.cumsum(sizes), jnp.arange(rows * top), side="right").astype(jnp.int32)
    grid = members.reshape(top, rows).T
    grid = grid[jax.random.permutation(jax.random.fold_in(own, 1), rows)]
    turn = jax.random.randint(jax.random.fold_in(own, 2), (rows, 1), 0, top)
    return jnp.take_along_axis(grid, (jnp.arange(top)[None, :] + turn) % top, axis=1)


def load_shares(amount, total, bound, lean, full):
    portions = [(1 << 20) // math.isqrt(standing ** lean) + 1 for standing in range(1, amount + 1)]
    largest = bound if full else min(bound, max(-(-total // amount), total * portions[0] // sum(portions)))
    least = 1 if total - largest >= amount - 1 else 0
    given, rest = [largest] + [least] * (amount - 1), total - largest - least * (amount - 1)
    while rest > 0:
        free = [i for i in range(1, amount) if given[i] < largest] or [i for i in range(1, amount) if given[i] < bound]
        whole, left = sum([portions[i] for i in free]), rest
        for i in free:
            addition = min(bound - given[i], max(1, left * portions[i] // whole), rest)
            given[i] = given[i] + addition
            rest = rest - addition
    return np.array(given)


def noise(stream_key, dims, width, most, pieces=(), held_as=jnp.bfloat16):
    drawn = jax.random.normal(stream_key, dims, jnp.float32) * width
    if len(pieces) > 0:
        drawn = block_levels(stream_key, dims, pieces, -0.22, 0.18) * drawn
    return jnp.clip(drawn, min=-most, max=most).astype(held_as)


def setup_inputs(seed: int = 0) -> dict:
    keys = jax.random.split(jax.random.key(seed), 12)
    hidden_in = noise(keys[0], (N_DP, N_TENSOR, REQ_GRP, NEW_DEV, MODEL_WIDTH), 1.0, 6.0, ((0, 16), (1, 32)))
    rotated_queries = draw_rotated_queries(jax.random.fold_in(keys[11], 71), 0)
    fresh_key_values = noise(keys[2], (N_DP, N_TENSOR, REQ_GRP, NEW_DEV, KVW), 1.0, 6.0, ((0, 16), (1, 32)))
    cached_key_values = draw_cached_key_values(jax.random.fold_in(keys[11], 71), 0)
    cached_len = draw_cached_len(jax.random.fold_in(keys[11], 71), 0)
    expert_ids_keys = jax.random.split(jax.random.fold_in(keys[5], 1), N_DP * N_TENSOR * REQ_GRP * NEW_DEV // TOK_DEV)
    expert_ids_turns = jax.random.permutation(jax.random.fold_in(keys[5], 3), N_DP * N_TENSOR * REQ_GRP * NEW_DEV // TOK_DEV)
    expert_ids = jax.vmap(lambda own, number: deal_out(jax.random.fold_in(keys[5], 2), own, number, TOK_DEV, EXPERTS, TOPK, CAP, 0))(expert_ids_keys, expert_ids_turns).reshape((N_DP, N_TENSOR, REQ_GRP, NEW_DEV, TOPK))
    route_gates = jnp.clip(0.1 + 0.3 * jax.random.uniform(keys[6], (N_DP, N_TENSOR, REQ_GRP, NEW_DEV, TOPK), jnp.float32) ** block_levels(keys[6], (N_DP, N_TENSOR, REQ_GRP, NEW_DEV, TOPK), ((0, 16), (1, 32)), -0.2, 0.2), 0.1, 0.4)
    output_weight = noise(keys[7], (QUERY_HEADS * HEAD_WIDTH, MODEL_WIDTH), 0.5, 3.0, ((0, 32),))
    norm_gain = jnp.clip(1.0 + 0.18 * jax.random.normal(keys[8], (MODEL_WIDTH,), jnp.float32), 0.1, 1.9)
    gate_up = noise(keys[9], (EXPERTS, MODEL_WIDTH, 2 * FFE), MODEL_WIDTH ** -0.5, 0.15625, ((0, 32), (1, 16)))
    down_weight = noise(keys[10], (EXPERTS, FFE, MODEL_WIDTH), FFE ** -0.5, 0.25, ((0, 32), (1, 16)))
    return {"hidden_in": hidden_in, "rotated_queries": rotated_queries, "fresh_key_values": fresh_key_values, "cached_key_values": cached_key_values, "cached_len": cached_len, "expert_ids": expert_ids, "route_gates": route_gates, "output_weight": output_weight, "norm_gain": norm_gain, "gate_up": gate_up, "down_weight": down_weight}


epsilon = 1e-05

def by_request(blocked):
    last_width = blocked.shape[-1]
    return jnp.transpose(blocked, (0, 2, 1, 3, 4)).reshape(N_DP * REQ_GRP, N_TENSOR * NEW_DEV, last_width)

def request_attention(single_query, single_fresh, single_cache, length, output_weight):
    query_groups = QUERY_HEADS // KEY_VALUE_HEADS
    query_matrix = jnp.transpose(single_query.reshape(FRESH_POSITIONS, KEY_VALUE_HEADS, query_groups, HEAD_WIDTH), (1, 0, 2, 3))
    key_value_part = jnp.concatenate([single_cache.reshape(CACHE_SLOT_LIMIT, KEY_VALUE_HEADS, 2 * HEAD_WIDTH), single_fresh.reshape(FRESH_POSITIONS, KEY_VALUE_HEADS, 2 * HEAD_WIDTH)], 0)
    key_value_part = jnp.transpose(key_value_part, (1, 0, 2))
    key_pos = jnp.arange(CACHE_SLOT_LIMIT + FRESH_POSITIONS, dtype=jnp.int32)
    query_pos = jnp.arange(FRESH_POSITIONS, dtype=jnp.int32)
    visible = jnp.where(key_pos[None, :] < CACHE_SLOT_LIMIT, key_pos[None, :] < length, key_pos[None, :] - CACHE_SLOT_LIMIT <= query_pos[:, None])
    visible = visible[:, None, :]

    def one_head(packed):
        query_head, pair_head = packed
        keys_all = pair_head[:, :HEAD_WIDTH].astype(jnp.float32)
        values_all = pair_head[:, HEAD_WIDTH:].astype(jnp.float32)
        scores = jnp.einsum('pgd,kd->pgk', query_head.astype(jnp.float32), keys_all) * (1.0 / math.sqrt(HEAD_WIDTH))
        scores = jnp.where(visible, scores, -1e+30)
        highest = lax.optimization_barrier(jnp.max(scores, -1, keepdims=True))
        weights = jnp.where(visible, jnp.exp(scores - highest), 0.0)
        denoms = lax.optimization_barrier(jnp.sum(weights, -1, keepdims=True))
        rounded = lax.optimization_barrier(weights.astype(jnp.bfloat16)).astype(jnp.float32)
        return jnp.einsum('pgk,kd->pgd', rounded, values_all) / denoms
    mixed_output = lax.map(one_head, (query_matrix, key_value_part))
    attention_result = jnp.transpose(mixed_output, (1, 0, 2, 3)).astype(jnp.bfloat16).reshape(FRESH_POSITIONS, KEY_VALUE_HEADS, query_groups * HEAD_WIDTH)
    output_projected = output_weight.reshape(KEY_VALUE_HEADS, query_groups * HEAD_WIDTH, MODEL_WIDTH).astype(jnp.float32)
    head_sums = jnp.einsum('phc,hcd->phd', attention_result.astype(jnp.float32), output_projected)
    head_sums = lax.optimization_barrier(head_sums.astype(jnp.bfloat16)).astype(jnp.float32)
    return lax.optimization_barrier(jnp.sum(head_sums, 1))

def appended_cache(single_cache, single_fresh, length):
    context = jnp.arange(CACHE_SLOT_LIMIT + FRESH_POSITIONS, dtype=jnp.int32)
    old_rows = single_cache[jnp.clip(context, 0, CACHE_SLOT_LIMIT - 1)]
    new_rows = single_fresh[jnp.clip(context - length, 0, FRESH_POSITIONS - 1)]
    later = jnp.where((context < length + FRESH_POSITIONS)[:, None], new_rows, jnp.zeros_like(new_rows))
    return jnp.where((context < length)[:, None], old_rows, later)

def reference(hidden_in, rotated_queries, fresh_key_values, cached_key_values, cached_len, expert_ids, route_gates, output_weight, norm_gain, gate_up, down_weight):
    query_req = by_request(rotated_queries)
    fresh_req = by_request(fresh_key_values)

    def one_request(packed):
        single_query, single_fresh, single_cache, length = packed
        return (request_attention(single_query, single_fresh, single_cache, length, output_weight), appended_cache(single_cache, single_fresh, length))
    attention_sum, cache_out = lax.map(one_request, (query_req, fresh_req, cached_key_values, cached_len))
    attention_dev = jnp.transpose(attention_sum.reshape(N_DP, REQ_GRP, N_TENSOR, NEW_DEV, MODEL_WIDTH), (0, 2, 1, 3, 4))
    residual = hidden_in.astype(jnp.float32) + attention_dev
    meansq = lax.optimization_barrier(jnp.mean(residual * residual, -1, keepdims=True))
    normed = (residual * lax.rsqrt(meansq + epsilon) * norm_gain).astype(jnp.bfloat16)
    blocks = N_DP * N_TENSOR
    tokens_all = blocks * TOK_DEV
    normed_flat = normed.reshape(tokens_all, MODEL_WIDTH)
    ids_block = expert_ids.reshape(blocks, TOK_DEV * TOPK)
    onehot = (ids_block[:, :, None] == jnp.arange(EXPERTS, dtype=jnp.int32)[None, None, :]).astype(jnp.int32)
    slot_rank = lax.optimization_barrier(jnp.sum(onehot * (jnp.cumsum(onehot, 1) - onehot), 2))
    slot_index = (ids_block * (blocks * CAP) + jnp.arange(blocks, dtype=jnp.int32)[:, None] * CAP + slot_rank).reshape(-1)
    token_index = jnp.arange(tokens_all * TOPK, dtype=jnp.int32) // TOPK
    slot_tokens = jnp.full((EXPERTS * blocks * CAP,), tokens_all, jnp.int32).at[slot_index].set(token_index).reshape(EXPERTS, blocks * CAP)
    gate_table = jnp.zeros((EXPERTS * blocks * CAP,), jnp.float32).at[slot_index].set(route_gates.reshape(-1).astype(jnp.float32)).reshape(EXPERTS, blocks * CAP)
    padded = jnp.concatenate([normed_flat, jnp.zeros((1, MODEL_WIDTH), jnp.bfloat16)], 0)

    def add_expert(carried, expert):
        row_index = slot_tokens[expert]
        picked = padded[row_index]
        hidden_units = jnp.dot(picked, gate_up[expert], preferred_element_type=jnp.float32)
        active = (jax.nn.silu(hidden_units[:, :FFE]) * hidden_units[:, FFE:]).astype(jnp.bfloat16)
        outputs = jnp.dot(active, down_weight[expert], preferred_element_type=jnp.float32).astype(jnp.bfloat16)
        return (carried.at[row_index].add(gate_table[expert][:, None] * outputs.astype(jnp.float32)), None)
    mixture, unused = lax.scan(add_expert, jnp.zeros((tokens_all + 1, MODEL_WIDTH), jnp.float32), jnp.arange(EXPERTS, dtype=jnp.int32))
    hidden_out = (residual.reshape(tokens_all, MODEL_WIDTH) + mixture[:tokens_all]).astype(jnp.bfloat16).reshape(hidden_in.shape)
    return (hidden_out, cache_out)
```

```python
import functools
import math

import jax
import jax.numpy as jnp
from jax import lax
from jax.experimental import pallas as pl
from jax.experimental.pallas import tpu as pltpu
from jax.sharding import Mesh
from jax.sharding import PartitionSpec as P

D = 1536
HQ = 24
HKV = 8
HD = 64
FFE = 512
TOPK = 8
EPS = 1e-05
NT = 32
TOK = 64
CROWS = 32
SLOT = 16
CH = D // 128
SROWS = SLOT * CH + 16
BF = jnp.bfloat16
F32 = jnp.float32
TEN = ("zhi", "x", "core")
NEG = -1e30
INTERPRET = False


def vmem():
    return pl.BlockSpec(memory_space=pltpu.VMEM)


def params(mib):
    return pltpu.CompilerParams(vmem_limit_bytes=mib << 20)


def dot(a, b):
    return lax.dot_general(a, b, (((1,), (0,)), ((), ())), preferred_element_type=F32)


def iota(shape, dim):
    return lax.broadcasted_iota(jnp.int32, shape, dim)


def pack_kernel(q_ref, f_ref, c_ref, o_ref):
    zeros = jnp.zeros((16, HD), BF)
    for g in range(HKV):
        cols = pl.ds(g * 128, 128)
        for quarter in range(4):
            t = g * 4 + quarter
            rows = q_ref[quarter * 16 : quarter * 16 + 16, g * 192 : g * 192 + 192]
            half = quarter % 2
            o_ref[t, 0:16, :] = rows[:, :128]
            o_ref[t, 16:32, :] = jnp.concatenate([rows[:, 128:], zeros], 1)
            o_ref[t, 32:48, :] = c_ref[half * 16 : half * 16 + 16, cols]
            o_ref[t, 48:80, :] = f_ref[half * 32 : half * 32 + 32, cols]


def pack(queries, fresh, cache):
    return pl.pallas_call(
        pack_kernel,
        out_shape=jax.ShapeDtypeStruct((NT, 80, 128), BF),
        in_specs=[vmem()] * 3,
        out_specs=vmem(),
        interpret=INTERPRET,
        name="pack",
    )(queries, fresh, cache)


def attention_kernel(info_ref, own_ref, oth_ref, o_ref, kv, sc, bias_c, bias_d):
    b = pl.program_id(0)
    length, core, quarter = info_ref[0], info_ref[1], info_ref[2]

    @pl.when(b == 0)
    def _():
        kv[0:512, :] = own_ref[:, 32:48, :].reshape(512, 128)
        kv[512:1024, :] = oth_ref[:, 0:16, :].reshape(512, 128)
        for j in range(4):
            base = 1024 + 512 * j
            kv[base : base + 256, :] = own_ref[8 * j : 8 * j + 8, 48:80, :].reshape(256, 128)
            kv[base + 256 : base + 512, :] = oth_ref[8 * j : 8 * j + 8, 16:48, :].reshape(256, 128)
        col = iota((8, 1024), 1)
        half = jnp.where(col < 512, core, 1 - core)
        inner = col % 512
        place = (inner // 16) * 32 + half * 16 + inner % 16
        bias_c[...] = jnp.where(place < length, 0.0, NEG)
        row = iota((128, 512), 0)
        col = iota((128, 512), 1)
        half = jnp.where(col < 256, core, 1 - core)
        inner = col % 256
        key_at = (inner // 32) * 64 + half * 32 + inner % 32
        query_at = (row // 16) * 64 + quarter * 16 + row % 16
        bias_d[...] = jnp.where(key_at <= query_at, 0.0, NEG)

    first = own_ref[pl.ds(b * 8, 8), 0:16, :].reshape(128, 128).astype(F32) * 0.125
    second = own_ref[pl.ds(b * 8, 8), 16:32, :].reshape(128, 128).astype(F32) * 0.125
    low = iota((128, 128), 1) < HD
    q = jnp.concatenate(
        [
            jnp.where(low, first, 0.0),
            jnp.where(low, pltpu.roll(first, HD, 1), 0.0),
            jnp.where(low, second, 0.0),
        ],
        0,
    ).astype(BF)

    def scores(k):
        keys = kv[pl.ds(pl.multiple_of(k * 512, 512), 512), :]
        return lax.dot_general(q, keys, (((1,), (1,)), ((), ())), preferred_element_type=F32)

    def fold(fn, top, s):
        for j in range(4):
            top = fn(top, s[:, j * 128 : j * 128 + 128])
        return top

    top = jnp.full((384, 128), NEG, F32)
    for k in range(2):
        s = scores(k) + bias_c[0:1, k * 512 : k * 512 + 512]
        sc[k] = s
        top = fold(jnp.maximum, top, s)
    s = scores(2 + b)
    s = s + jnp.concatenate([bias_d[...]] * 3, 0)
    sc[2 + b] = s
    top = fold(jnp.maximum, top, s)

    def middle(k, top):
        s = scores(k)
        sc[k] = s
        return fold(jnp.maximum, top, s)

    top = lax.fori_loop(2, 2 + b, middle, top)
    highest = jnp.max(top, 1, keepdims=True)

    def mix(k, carry):
        total, acc = carry
        p = jnp.exp(sc[k] - highest)
        values = kv[pl.ds(pl.multiple_of(k * 512, 512), 512), :]
        return fold(jnp.add, total, p), acc + dot(p.astype(BF), values)

    zero = jnp.zeros((384, 128), F32)
    total, acc = lax.fori_loop(0, 3 + b, mix, (zero, zero))
    out = acc / jnp.sum(total, 1, keepdims=True)
    a0, a1, a2 = out[0:128], out[128:256], out[256:384]
    pair = jnp.where(low, pltpu.roll(a0, HD, 1), a1).astype(BF)
    last = jnp.where(low, pltpu.roll(a2, HD, 1), 0.0).astype(BF)
    o_ref[pl.ds(b * 8, 8), 0:16, :] = pair.reshape(8, 16, 128)
    o_ref[pl.ds(b * 8, 8), 16:32, :] = last.reshape(8, 16, 128)


def attention(info, own, other):
    return pl.pallas_call(
        attention_kernel,
        out_shape=jax.ShapeDtypeStruct((NT, 32, 128), BF),
        grid=(4,),
        in_specs=[
            pl.BlockSpec(memory_space=pltpu.SMEM),
            vmem(),
            vmem(),
        ],
        out_specs=vmem(),
        scratch_shapes=[
            pltpu.VMEM((3072, 128), BF),
            pltpu.VMEM((6, 384, 512), F32),
            pltpu.VMEM((8, 1024), F32),
            pltpu.VMEM((128, 512), F32),
        ],
        compiler_params=params(32),
        cost_estimate=pl.CostEstimate(
            flops=2 * 2 * 1536 * 2304 * 128, bytes_accessed=3 << 20, transcendentals=1536 * 2304
        ),
        interpret=INTERPRET,
        name="attention",
    )(info, own, other)


def project_kernel(att_ref, w_ref, hid_ref, gain_ref, ids_ref, res_ref, disp_ref):
    g = pl.program_id(0)

    @pl.when(g == 0)
    def _():
        res_ref[...] = jnp.zeros_like(res_ref)

    pair = att_ref[pl.ds(g * 4, 4), 0:16, :].reshape(TOK, 128)
    last = att_ref[pl.ds(g * 4, 4), 16:32, :].reshape(TOK, 128)
    term = dot(pair, w_ref[0:128, :]) + dot(last[:, :HD], w_ref[128:192, :])
    res_ref[...] += term.astype(BF).astype(F32)

    @pl.when(g == HKV - 1)
    def _():
        residual = hid_ref[...].astype(F32) + res_ref[...]
        res_ref[...] = residual
        meansq = jnp.mean(residual * residual, 1, keepdims=True)
        normed = (residual * lax.rsqrt(meansq + EPS) * gain_ref[...]).astype(BF)
        experts = iota((NT, TOK), 0)
        named = jnp.zeros((NT, TOK), F32)
        for k in range(TOPK):
            named = named + jnp.where(ids_ref[k : k + 1, :] == experts, 1.0, 0.0)
        before = jnp.where(iota((TOK, TOK), 0) < iota((TOK, TOK), 1), 1.0, 0.0).astype(BF)
        rank = dot(named.astype(BF), before)
        rank = jnp.where(named > 0.5, rank, -1.0).astype(BF)
        spread = jnp.where(iota((512, NT), 0) // SLOT == iota((512, NT), 1), 1.0, 0.0).astype(BF)
        ranks = dot(spread, rank)
        place = iota((512, TOK), 0) % SLOT
        pick = jnp.where(ranks == place.astype(F32), 1.0, 0.0).astype(BF)
        late = jnp.where(ranks == float(SLOT), 1.0, 0.0)
        extra = jnp.zeros((512, 128), F32)
        for c in range(CH):
            chunk = normed[:, c * 128 : c * 128 + 128]
            disp_ref[:, c * SLOT : (c + 1) * SLOT, :] = (
                dot(pick, chunk).astype(BF).reshape(NT, SLOT, 128)
            )
            extra = extra + dot(jnp.where(place == c, late, 0.0).astype(BF), chunk)
        disp_ref[:, SLOT * CH : SROWS, :] = extra.astype(BF).reshape(NT, 16, 128)


def project(att, weight, hidden, gain, ids_t):
    return pl.pallas_call(
        project_kernel,
        out_shape=(
            jax.ShapeDtypeStruct((TOK, D), F32),
            jax.ShapeDtypeStruct((NT, SROWS, 128), BF),
        ),
        grid=(HKV,),
        in_specs=[
            vmem(),
            pl.BlockSpec((192, D), lambda g: (g, 0)),
            vmem(),
            vmem(),
            vmem(),
        ],
        out_specs=(vmem(), vmem()),
        compiler_params=params(32),
        cost_estimate=pl.CostEstimate(
            flops=2 * TOK * D * D, bytes_accessed=8 << 20, transcendentals=0
        ),
        interpret=INTERPRET,
        name="project",
    )(att, weight, hidden, gain, ids_t)


def gather_extra(block):
    rows = iota((CH * NT, 512), 0)
    cols = iota((CH * NT, 512), 1)
    match = (rows % NT == cols // 16) & (rows // NT == cols % 16)
    stacked = dot(jnp.where(match, 1.0, 0.0).astype(BF), block).astype(BF)
    return [stacked[c * NT : (c + 1) * NT, :] for c in range(CH)]


def spread_extra(rows):
    place = iota((512, NT), 0)
    owner = place // 16 == iota((512, NT), 1)
    out = jnp.zeros((512, 128), F32)
    for c in range(CH):
        match = jnp.where(owner & (place % 16 == c), 1.0, 0.0).astype(BF)
        out = out + dot(match, rows[:, c * 128 : c * 128 + 128])
    return out.astype(BF)


def expert_kernel(in_ref, w_ref, o_ref, x, w1, w2, sems):
    blocks = w_ref.shape[0]
    copies = []
    for d in range(blocks):
        pieces = (
            (w_ref.at[d, 0:64, 0:1024], w1.at[d * 96 : d * 96 + 64, :]),
            (w_ref.at[d, 0:32, 1024:1536], w1.at[d * 96 + 64 : d * 96 + 96, 0:512]),
            (w_ref.at[d, 32:64, 1024:1536], w1.at[d * 96 + 64 : d * 96 + 96, 512:1024]),
            (w_ref.at[d, 64:96, :], w2.at[d * 32 : d * 32 + 32, :]),
        )
        for n, (src, dst) in enumerate(pieces):
            copies.append(pltpu.make_async_copy(src, dst, sems.at[d, n]))
    for copy in copies:
        copy.start()
    for c in range(CH):
        x[0:512, c * 128 : c * 128 + 128] = in_ref[:, c * SLOT : (c + 1) * SLOT, :].reshape(512, 128)
    chunks = gather_extra(in_ref[:, SLOT * CH : SROWS, :].reshape(512, 128))
    for c in range(CH):
        x[512:544, c * 128 : c * 128 + 128] = chunks[c]
    for copy in copies:
        copy.wait()
    hidden = dot(x[...], w1[...])
    gate = hidden[:, :FFE]
    active = (gate / (1.0 + jnp.exp(-gate)) * hidden[:, FFE:]).astype(BF)
    out = dot(active, w2[...]).astype(BF)
    for c in range(CH):
        o_ref[:, c * SLOT : (c + 1) * SLOT, :] = out[0:512, c * 128 : c * 128 + 128].reshape(
            NT, SLOT, 128
        )
    o_ref[:, SLOT * CH : SROWS, :] = spread_extra(out[512:544, :]).reshape(NT, 16, 128)


def expert(slots, weights):
    blocks = weights.shape[0]
    return pl.pallas_call(
        expert_kernel,
        out_shape=jax.ShapeDtypeStruct((NT, SROWS, 128), BF),
        in_specs=[vmem(), pl.BlockSpec(memory_space=pl.ANY)],
        out_specs=vmem(),
        scratch_shapes=[
            pltpu.VMEM((544, D), BF),
            pltpu.VMEM((blocks * 96, 2 * FFE), BF),
            pltpu.VMEM((blocks * 32, D), BF),
            pltpu.SemaphoreType.DMA((blocks, 4)),
        ],
        compiler_params=params(40),
        cost_estimate=pl.CostEstimate(
            flops=2 * 544 * 1536 * 1536, bytes_accessed=9 << 20, transcendentals=544 * 512
        ),
        interpret=INTERPRET,
        name="expert",
    )(slots, weights)


def combine_kernel(in_ref, res_ref, ids_ref, gate_ref, o_ref):
    experts = iota((TOK, NT), 1)
    named = jnp.zeros((TOK, NT), F32)
    gates = jnp.zeros((TOK, NT), F32)
    for k in range(TOPK):
        match = ids_ref[:, k : k + 1] == experts
        named = named + jnp.where(match, 1.0, 0.0)
        gates = gates + jnp.where(match, gate_ref[:, k : k + 1], 0.0)
    before = jnp.where(iota((TOK, TOK), 1) < iota((TOK, TOK), 0), 1.0, 0.0).astype(BF)
    rank = dot(before, named.astype(BF))
    rank = jnp.where(named > 0.5, rank, -1.0)
    spread = jnp.where(iota((NT, 512), 0) == iota((NT, 512), 1) // SLOT, 1.0, 0.0).astype(BF)
    place = (iota((TOK, 512), 1) % SLOT).astype(F32)
    pick = dot(rank.astype(BF), spread) == place
    high = gates.astype(BF)
    low = (gates - high.astype(F32)).astype(BF)
    weights = jnp.concatenate(
        [jnp.where(pick, dot(part, spread), 0.0).astype(BF) for part in (high, low)], 0
    )
    late = rank == float(SLOT)
    late_weights = jnp.concatenate(
        [jnp.where(late, part.astype(F32), 0.0).astype(BF) for part in (high, low)], 0
    )
    chunks = gather_extra(in_ref[:, SLOT * CH : SROWS, :].reshape(512, 128))
    for c in range(CH):
        main = in_ref[:, c * SLOT : (c + 1) * SLOT, :].reshape(512, 128)
        both = dot(weights, main) + dot(late_weights, chunks[c])
        cols = slice(c * 128, c * 128 + 128)
        o_ref[:, cols] = (res_ref[:, cols] + (both[:TOK] + both[TOK:])).astype(BF)


def combine(returned, residual, ids, gates):
    return pl.pallas_call(
        combine_kernel,
        out_shape=jax.ShapeDtypeStruct((TOK, D), BF),
        in_specs=[vmem()] * 4,
        out_specs=vmem(),
        compiler_params=params(32),
        interpret=INTERPRET,
        name="combine",
    )(returned, residual, ids, gates)


def shards(
    hidden_in,
    rotated_queries,
    fresh_key_values,
    cached_key_values,
    cached_len,
    expert_ids,
    route_gates,
    output_weight,
    norm_gain,
    gate_up,
    down_weight,
):
    zlo = lax.axis_index("zlo")
    core = lax.axis_index("core")
    quarter = lax.axis_index(TEN) % 4
    length = cached_len[0]
    ids = expert_ids[0, 0, 0]
    gates = route_gates[0, 0, 0]

    send = pack(rotated_queries[0, 0, 0], fresh_key_values[0, 0, 0], cached_key_values[0])
    full_weight = lax.all_gather(output_weight, TEN, axis=0, tiled=True)
    up = gate_up[0]
    packed = jnp.concatenate(
        [jnp.concatenate([up[:64], jnp.concatenate([up[64:, :512], up[64:, 512:]], 0)], 1), down_weight[0]], 0
    )
    across = lax.ppermute(packed, "zlo", [(0, 1), (1, 0)])
    both = jnp.where(
        zlo == 0, jnp.stack([packed, across], 0), jnp.stack([across, packed], 0)
    )
    weights = lax.all_gather(both, "y", axis=0, tiled=True)

    own = lax.all_to_all(send, TEN, split_axis=0, concat_axis=0, tiled=True)
    other = lax.ppermute(own[:, 32:, :], "core", [(0, 1), (1, 0)])
    info = jnp.stack([length, core.astype(jnp.int32), quarter.astype(jnp.int32)])
    attended = attention(info, own, other)
    att = lax.all_to_all(attended, TEN, split_axis=0, concat_axis=0, tiled=True)
    residual, outbound = project(att, full_weight, hidden_in[0, 0, 0], norm_gain[None], ids.T)
    slots = lax.all_to_all(outbound, TEN, split_axis=0, concat_axis=0, tiled=True)
    computed = expert(slots, weights)
    returned = lax.all_to_all(computed, TEN, split_axis=0, concat_axis=0, tiled=True)
    hidden_out = combine(returned, residual, ids, gates)

    mine = lax.dynamic_slice_in_dim(own[:, 32:, :], quarter * 32, 32, 2)
    theirs = lax.dynamic_slice_in_dim(other, quarter * 32, 32, 2)
    halves = jnp.where(
        core == 0, jnp.stack([mine, theirs], 1), jnp.stack([theirs, mine], 1)
    )
    old_rows = halves[:, :, :16].reshape(NT * CROWS, 32)
    new_rows = halves[:, :, 16:].reshape(NT * TOK, 32)
    total = NT * CROWS + NT * TOK
    base = jnp.concatenate([old_rows, jnp.zeros((NT * TOK, 32), BF)], 0)
    base = jnp.where((jnp.arange(total, dtype=jnp.int32) < length)[:, None], base, jnp.zeros_like(base))
    cache_out = lax.dynamic_update_slice_in_dim(base, new_rows, length, 0)
    return hidden_out.reshape(1, 1, 1, TOK, D), cache_out[None]


def solution(mesh):
    dp, tensor = mesh.devices.shape
    fine = Mesh(mesh.devices.reshape(dp // 2, 2, 4, 4, 2), ("y", "zlo", "zhi", "x", "core"))
    ydp = ("y", "zlo")
    return jax.shard_map(
        shards,
        mesh=fine,
        in_specs=(
            P(ydp, TEN, None, None, None),
            P(ydp, TEN, None, None, None),
            P(ydp, TEN, None, None, None),
            P(ydp, TEN, None),
            P(ydp),
            P(ydp, TEN, None, None, None),
            P(ydp, TEN, None, None, None),
            P(TEN, None),
            P(),
            P(TEN, ydp, None),
            P(TEN, ydp, None),
        ),
        out_specs=(P(ydp, TEN, None, None, None), P(ydp, None, TEN)),
        check_vma=False,
    )
```

```python
import functools
import math

import jax
import jax.numpy as jnp
from jax import lax
from jax.experimental import pallas as pl
from jax.experimental.pallas import tpu as pltpu
from jax.sharding import Mesh
from jax.sharding import PartitionSpec as P

D = 1536
HQ = 24
HKV = 8
HD = 64
FFE = 512
TOPK = 8
EPS = 1e-05
NT = 32
TOK = 64
CROWS = 32
SLOT = 16
CH = D // 128
SROWS = SLOT * CH + 16
BF = jnp.bfloat16
F32 = jnp.float32
TEN = ("zhi", "x", "core")
NEG = -1e30
INTERPRET = False


def vmem():
    return pl.BlockSpec(memory_space=pltpu.VMEM)


def params(mib):
    return pltpu.CompilerParams(vmem_limit_bytes=int(mib * (1 << 20)))


def dot(a, b):
    return lax.dot_general(a, b, (((1,), (0,)), ((), ())), preferred_element_type=F32)


def iota(shape, dim):
    return lax.broadcasted_iota(jnp.int32, shape, dim)


def pack_kernel(q_ref, f_ref, c_ref, o_ref):
    zeros = jnp.zeros((16, HD), BF)
    for g in range(HKV):
        cols = pl.ds(g * 128, 128)
        for quarter in range(4):
            t = g * 4 + quarter
            rows = q_ref[quarter * 16 : quarter * 16 + 16, g * 192 : g * 192 + 192]
            half = quarter % 2
            o_ref[t, 0:16, :] = rows[:, :128]
            o_ref[t, 16:32, :] = jnp.concatenate([rows[:, 128:], zeros], 1)
            o_ref[t, 32:48, :] = c_ref[half * 16 : half * 16 + 16, cols]
            o_ref[t, 48:80, :] = f_ref[half * 32 : half * 32 + 32, cols]


def pack(queries, fresh, cache):
    return pl.pallas_call(
        pack_kernel,
        out_shape=jax.ShapeDtypeStruct((NT, 80, 128), BF),
        in_specs=[vmem()] * 3,
        out_specs=vmem(),
        interpret=INTERPRET,
        name="pack",
    )(queries, fresh, cache)


def attention_kernel(info_ref, own_ref, oth_ref, o_ref, kv, sc, bias_c, bias_d):
    b = pl.program_id(0)
    length, core, quarter = info_ref[0], info_ref[1], info_ref[2]

    @pl.when(b == 0)
    def _():
        kv[0:512, :] = own_ref[:, 32:48, :].reshape(512, 128)
        kv[512:1024, :] = oth_ref[:, 0:16, :].reshape(512, 128)
        for j in range(4):
            base = 1024 + 512 * j
            kv[base : base + 256, :] = own_ref[8 * j : 8 * j + 8, 48:80, :].reshape(256, 128)
            kv[base + 256 : base + 512, :] = oth_ref[8 * j : 8 * j + 8, 16:48, :].reshape(256, 128)
        col = iota((8, 1024), 1)
        half = jnp.where(col < 512, core, 1 - core)
        inner = col % 512
        place = (inner // 16) * 32 + half * 16 + inner % 16
        bias_c[...] = jnp.where(place < length, 0.0, NEG)
        row = iota((128, 512), 0)
        col = iota((128, 512), 1)
        half = jnp.where(col < 256, core, 1 - core)
        inner = col % 256
        key_at = (inner // 32) * 64 + half * 32 + inner % 32
        query_at = (row // 16) * 64 + quarter * 16 + row % 16
        bias_d[...] = jnp.where(key_at <= query_at, 0.0, NEG)

    first = own_ref[pl.ds(b * 8, 8), 0:16, :].reshape(128, 128).astype(F32) * 0.125
    second = own_ref[pl.ds(b * 8, 8), 16:32, :].reshape(128, 128).astype(F32) * 0.125
    low = iota((128, 128), 1) < HD
    q = jnp.concatenate(
        [
            jnp.where(low, first, 0.0),
            jnp.where(low, pltpu.roll(first, HD, 1), 0.0),
            jnp.where(low, second, 0.0),
        ],
        0,
    ).astype(BF)

    def scores(k):
        keys = kv[pl.ds(pl.multiple_of(k * 512, 512), 512), :]
        return lax.dot_general(q, keys, (((1,), (1,)), ((), ())), preferred_element_type=F32)

    def fold(fn, top, s):
        for j in range(4):
            top = fn(top, s[:, j * 128 : j * 128 + 128])
        return top

    top = jnp.full((384, 128), NEG, F32)
    for k in range(2):
        s = scores(k) + bias_c[0:1, k * 512 : k * 512 + 512]
        sc[k] = s
        top = fold(jnp.maximum, top, s)
    s = scores(2 + b)
    s = s + jnp.concatenate([bias_d[...]] * 3, 0)
    sc[2 + b] = s
    top = fold(jnp.maximum, top, s)

    def middle(k, top):
        s = scores(k)
        sc[k] = s
        return fold(jnp.maximum, top, s)

    top = lax.fori_loop(2, 2 + b, middle, top)
    highest = jnp.max(top, 1, keepdims=True)

    def mix(k, carry):
        total, acc = carry
        p = jnp.exp(sc[k] - highest)
        values = kv[pl.ds(pl.multiple_of(k * 512, 512), 512), :]
        return fold(jnp.add, total, p), acc + dot(p.astype(BF), values)

    zero = jnp.zeros((384, 128), F32)
    total, acc = lax.fori_loop(0, 3 + b, mix, (zero, zero))
    out = acc / jnp.sum(total, 1, keepdims=True)
    a0, a1, a2 = out[0:128], out[128:256], out[256:384]
    pair = jnp.where(low, pltpu.roll(a0, HD, 1), a1).astype(BF)
    last = jnp.where(low, pltpu.roll(a2, HD, 1), 0.0).astype(BF)
    o_ref[pl.ds(b * 8, 8), 0:16, :] = pair.reshape(8, 16, 128)
    o_ref[pl.ds(b * 8, 8), 16:32, :] = last.reshape(8, 16, 128)


def attention(info, own, other):
    return pl.pallas_call(
        attention_kernel,
        out_shape=jax.ShapeDtypeStruct((NT, 32, 128), BF),
        grid=(4,),
        in_specs=[
            pl.BlockSpec(memory_space=pltpu.SMEM),
            vmem(),
            vmem(),
        ],
        out_specs=vmem(),
        scratch_shapes=[
            pltpu.VMEM((3072, 128), BF),
            pltpu.VMEM((6, 384, 512), F32),
            pltpu.VMEM((8, 1024), F32),
            pltpu.VMEM((128, 512), F32),
        ],
        compiler_params=params(32),
        cost_estimate=pl.CostEstimate(
            flops=2 * 2 * 1536 * 2304 * 128, bytes_accessed=3 << 20, transcendentals=1536 * 2304
        ),
        interpret=INTERPRET,
        name="attention",
    )(info, own, other)


def merge_kernel(info_ref, own_ref, oth_ref, after_ref, o_ref):
    zlo = info_ref[3]
    o_ref[zlo] = own_ref[...]
    o_ref[1 - zlo] = oth_ref[...]


def merge(info, own, other, after):
    return pl.pallas_call(
        merge_kernel,
        out_shape=jax.ShapeDtypeStruct((2,) + own.shape, BF),
        in_specs=[
            pl.BlockSpec(memory_space=pltpu.SMEM),
            vmem(),
            vmem(),
            pl.BlockSpec(memory_space=pltpu.HBM),
        ],
        out_specs=vmem(),
        cost_estimate=pl.CostEstimate(flops=1 << 33, bytes_accessed=1 << 20, transcendentals=0),
        interpret=INTERPRET,
        name="merge",
    )(info, own, other, after)


def project_kernel(info_ref, att_ref, wo_ref, wx_ref, hid_ref, gain_ref, ids_ref, res_ref, disp_ref, w, sems):
    core = info_ref[1]
    copies = []
    for j in range(NT // 2):
        for n, (src, side) in enumerate(((wo_ref, core), (wx_ref, 1 - core))):
            at = pl.multiple_of((2 * j + side) * 48, 16)
            copies.append(pltpu.make_async_copy(src.at[j], w.at[pl.ds(at, 48), :], sems.at[j, n]))
    for copy in copies:
        copy.start()

    experts = iota((NT, TOK), 0)
    named = jnp.zeros((NT, TOK), F32)
    for k in range(TOPK):
        named = named + jnp.where(ids_ref[k : k + 1, :] == experts, 1.0, 0.0)
    before = jnp.where(iota((TOK, TOK), 0) < iota((TOK, TOK), 1), 1.0, 0.0).astype(BF)
    rank = dot(named.astype(BF), before)
    rank = jnp.where(named > 0.5, rank, -1.0).astype(BF)
    spread = jnp.where(iota((512, NT), 0) // SLOT == iota((512, NT), 1), 1.0, 0.0).astype(BF)
    ranks = dot(spread, rank)
    place = iota((512, TOK), 0) % SLOT
    pick = jnp.where(ranks == place.astype(F32), 1.0, 0.0).astype(BF)
    late = jnp.where(ranks == float(SLOT), 1.0, 0.0)

    total = hid_ref[...].astype(F32)
    for g in range(HKV):
        for copy in copies[4 * g : 4 * g + 4]:
            copy.wait()
        pair = att_ref[g * 4 : g * 4 + 4, 0:16, :].reshape(TOK, 128)
        last = att_ref[g * 4 : g * 4 + 4, 16:32, :].reshape(TOK, 128)
        row = g * 192
        term = dot(pair, w[row : row + 128, :]) + dot(last[:, :HD], w[row + 128 : row + 192, :])
        total = total + term.astype(BF).astype(F32)
    res_ref[...] = total
    meansq = jnp.mean(total * total, 1, keepdims=True)
    normed = (total * lax.rsqrt(meansq + EPS) * gain_ref[...]).astype(BF)
    extra = jnp.zeros((512, 128), F32)
    for c in range(CH):
        chunk = normed[:, c * 128 : c * 128 + 128]
        disp_ref[:, c * SLOT : (c + 1) * SLOT, :] = (
            dot(pick, chunk).astype(BF).reshape(NT, SLOT, 128)
        )
        extra = extra + dot(jnp.where(place == c, late, 0.0).astype(BF), chunk)
    disp_ref[:, SLOT * CH : SROWS, :] = extra.astype(BF).reshape(NT, 16, 128)


def project(info, att, own_weight, other_weight, hidden, gain, ids_t):
    hbm = pl.BlockSpec(memory_space=pltpu.HBM)
    return pl.pallas_call(
        project_kernel,
        out_shape=(
            jax.ShapeDtypeStruct((TOK, D), F32),
            jax.ShapeDtypeStruct((NT, SROWS, 128), BF),
        ),
        in_specs=[pl.BlockSpec(memory_space=pltpu.SMEM), vmem(), hbm, hbm, vmem(), vmem(), vmem()],
        out_specs=(vmem(), vmem()),
        scratch_shapes=[
            pltpu.VMEM((D, D), BF),
            pltpu.SemaphoreType.DMA((NT // 2, 2)),
        ],
        compiler_params=params(61.7),
        cost_estimate=pl.CostEstimate(
            flops=2 * TOK * D * D, bytes_accessed=8 << 20, transcendentals=0
        ),
        interpret=INTERPRET,
        name="project",
    )(info, att, own_weight, other_weight, hidden, gain, ids_t)


def gather_extra(block):
    rows = iota((CH * NT, 512), 0)
    cols = iota((CH * NT, 512), 1)
    match = (rows % NT == cols // 16) & (rows // NT == cols % 16)
    stacked = dot(jnp.where(match, 1.0, 0.0).astype(BF), block).astype(BF)
    return [stacked[c * NT : (c + 1) * NT, :] for c in range(CH)]


def spread_extra(rows):
    place = iota((512, NT), 0)
    owner = place // 16 == iota((512, NT), 1)
    out = jnp.zeros((512, 128), F32)
    for c in range(CH):
        match = jnp.where(owner & (place % 16 == c), 1.0, 0.0).astype(BF)
        out = out + dot(match, rows[:, c * 128 : c * 128 + 128])
    return out.astype(BF)


def expert_kernel(in_ref, w_ref, o_ref, x, w1, w2, sems):
    blocks = w_ref.shape[0]
    copies = []
    for d in range(blocks):
        pieces = (
            (w_ref.at[d, 0:64, 0:1024], w1.at[d * 96 : d * 96 + 64, :]),
            (w_ref.at[d, 0:32, 1024:1536], w1.at[d * 96 + 64 : d * 96 + 96, 0:512]),
            (w_ref.at[d, 32:64, 1024:1536], w1.at[d * 96 + 64 : d * 96 + 96, 512:1024]),
            (w_ref.at[d, 64:96, :], w2.at[d * 32 : d * 32 + 32, :]),
        )
        for n, (src, dst) in enumerate(pieces):
            copies.append(pltpu.make_async_copy(src, dst, sems.at[d, n]))
    firsts = [copy for i, copy in enumerate(copies) if i % 4 < 3]
    lasts = copies[3::4]
    for copy in firsts + lasts:
        copy.start()
    for c in range(CH):
        x[0:512, c * 128 : c * 128 + 128] = in_ref[:, c * SLOT : (c + 1) * SLOT, :].reshape(512, 128)
    chunks = gather_extra(in_ref[:, SLOT * CH : SROWS, :].reshape(512, 128))
    for c in range(CH):
        x[512:544, c * 128 : c * 128 + 128] = chunks[c]
    for copy in firsts:
        copy.wait()
    hidden = dot(x[...], w1[...])
    gate = hidden[:, :FFE]
    active = (gate / (1.0 + jnp.exp(-gate)) * hidden[:, FFE:]).astype(BF)
    for copy in lasts:
        copy.wait()
    out = dot(active, w2[...]).astype(BF)
    for c in range(CH):
        o_ref[:, c * SLOT : (c + 1) * SLOT, :] = out[0:512, c * 128 : c * 128 + 128].reshape(
            NT, SLOT, 128
        )
    o_ref[:, SLOT * CH : SROWS, :] = spread_extra(out[512:544, :]).reshape(NT, 16, 128)


def expert(slots, weights):
    blocks = weights.shape[0]
    return pl.pallas_call(
        expert_kernel,
        out_shape=jax.ShapeDtypeStruct((NT, SROWS, 128), BF),
        in_specs=[vmem(), pl.BlockSpec(memory_space=pltpu.HBM)],
        out_specs=vmem(),
        scratch_shapes=[
            pltpu.VMEM((544, D), BF),
            pltpu.VMEM((blocks * 96, 2 * FFE), BF),
            pltpu.VMEM((blocks * 32, D), BF),
            pltpu.SemaphoreType.DMA((blocks, 4)),
        ],
        compiler_params=params(59.5),
        cost_estimate=pl.CostEstimate(
            flops=2 * 544 * 1536 * 1536, bytes_accessed=9 << 20, transcendentals=544 * 512
        ),
        interpret=INTERPRET,
        name="expert",
    )(slots, weights)


def combine_kernel(in_ref, res_ref, ids_ref, gate_ref, o_ref):
    experts = iota((TOK, NT), 1)
    named = jnp.zeros((TOK, NT), F32)
    gates = jnp.zeros((TOK, NT), F32)
    for k in range(TOPK):
        match = ids_ref[:, k : k + 1] == experts
        named = named + jnp.where(match, 1.0, 0.0)
        gates = gates + jnp.where(match, gate_ref[:, k : k + 1], 0.0)
    before = jnp.where(iota((TOK, TOK), 1) < iota((TOK, TOK), 0), 1.0, 0.0).astype(BF)
    rank = dot(before, named.astype(BF))
    rank = jnp.where(named > 0.5, rank, -1.0)
    spread = jnp.where(iota((NT, 512), 0) == iota((NT, 512), 1) // SLOT, 1.0, 0.0).astype(BF)
    place = (iota((TOK, 512), 1) % SLOT).astype(F32)
    pick = dot(rank.astype(BF), spread) == place
    high = gates.astype(BF)
    low = (gates - high.astype(F32)).astype(BF)
    weights = jnp.concatenate(
        [jnp.where(pick, dot(part, spread), 0.0).astype(BF) for part in (high, low)], 0
    )
    late = rank == float(SLOT)
    late_weights = jnp.concatenate(
        [jnp.where(late, part.astype(F32), 0.0).astype(BF) for part in (high, low)], 0
    )
    chunks = gather_extra(in_ref[:, SLOT * CH : SROWS, :].reshape(512, 128))
    for c in range(CH):
        main = in_ref[:, c * SLOT : (c + 1) * SLOT, :].reshape(512, 128)
        both = dot(weights, main) + dot(late_weights, chunks[c])
        cols = slice(c * 128, c * 128 + 128)
        o_ref[:, cols] = (res_ref[:, cols] + (both[:TOK] + both[TOK:])).astype(BF)


def combine(returned, residual, ids, gates):
    return pl.pallas_call(
        combine_kernel,
        out_shape=jax.ShapeDtypeStruct((TOK, D), BF),
        in_specs=[vmem()] * 4,
        out_specs=vmem(),
        compiler_params=params(32),
        interpret=INTERPRET,
        name="combine",
    )(returned, residual, ids, gates)


def shards(
    hidden_in,
    rotated_queries,
    fresh_key_values,
    cached_key_values,
    cached_len,
    expert_ids,
    route_gates,
    output_weight,
    norm_gain,
    gate_up,
    down_weight,
):
    zlo = lax.axis_index("zlo")
    core = lax.axis_index("core")
    quarter = lax.axis_index(TEN) % 4
    length = cached_len[0]
    ids = expert_ids[0, 0, 0]
    gates = route_gates[0, 0, 0]

    send = pack(rotated_queries[0, 0, 0], fresh_key_values[0, 0, 0], cached_key_values[0])
    own_weight = lax.all_gather(output_weight, ("zhi", "x"), axis=0)
    up, down, _ = lax.optimization_barrier((gate_up[0], down_weight[0], send))
    packed = jnp.concatenate(
        [jnp.concatenate([up[:64], jnp.concatenate([up[64:, :512], up[64:, 512:]], 0)], 1), down], 0
    )

    own = lax.all_to_all(send, TEN, split_axis=0, concat_axis=0, tiled=True)
    other = lax.ppermute(own[:, 32:, :], "core", [(0, 1), (1, 0)])
    packed, _ = lax.optimization_barrier((packed, own))
    across = lax.ppermute(packed, "zlo", [(0, 1), (1, 0)])
    info = jnp.stack([length, core.astype(jnp.int32), quarter.astype(jnp.int32), zlo.astype(jnp.int32)])
    attended = attention(info, own, other)
    both = merge(info, packed, across, attended)
    weights = lax.all_gather(both, "y", axis=0, tiled=True)
    swapping, _ = lax.optimization_barrier((own_weight, both))
    other_weight = lax.ppermute(swapping, "core", [(0, 1), (1, 0)])
    att = lax.all_to_all(attended, TEN, split_axis=0, concat_axis=0, tiled=True)
    residual, outbound = project(
        info, att, own_weight, other_weight, hidden_in[0, 0, 0], norm_gain[None], ids.T)
    slots = lax.all_to_all(outbound, TEN, split_axis=0, concat_axis=0, tiled=True)
    computed = expert(slots, weights)
    returned = lax.all_to_all(computed, TEN, split_axis=0, concat_axis=0, tiled=True)
    hidden_out = combine(returned, residual, ids, gates)

    mine = lax.dynamic_slice_in_dim(own[:, 32:, :], quarter * 32, 32, 2)
    theirs = lax.dynamic_slice_in_dim(other, quarter * 32, 32, 2)
    halves = jnp.where(
        core == 0, jnp.stack([mine, theirs], 1), jnp.stack([theirs, mine], 1)
    )
    old_rows = halves[:, :, :16].reshape(NT * CROWS, 32)
    new_rows = halves[:, :, 16:].reshape(NT * TOK, 32)
    total = NT * CROWS + NT * TOK
    base = jnp.concatenate([old_rows, jnp.zeros((NT * TOK, 32), BF)], 0)
    base = jnp.where((jnp.arange(total, dtype=jnp.int32) < length)[:, None], base, jnp.zeros_like(base))
    cache_out = lax.dynamic_update_slice_in_dim(base, new_rows, length, 0)
    return hidden_out.reshape(1, 1, 1, TOK, D), cache_out[None]


def solution(mesh):
    dp, tensor = mesh.devices.shape
    fine = Mesh(mesh.devices.reshape(dp // 2, 2, 4, 4, 2), ("y", "zlo", "zhi", "x", "core"))
    ydp = ("y", "zlo")
    return jax.shard_map(
        shards,
        mesh=fine,
        in_specs=(
            P(ydp, TEN, None, None, None),
            P(ydp, TEN, None, None, None),
            P(ydp, TEN, None, None, None),
            P(ydp, TEN, None),
            P(ydp),
            P(ydp, TEN, None, None, None),
            P(ydp, TEN, None, None, None),
            P(TEN, None),
            P(),
            P(TEN, ydp, None),
            P(TEN, ydp, None),
        ),
        out_specs=(P(ydp, TEN, None, None, None), P(ydp, None, TEN)),
        check_vma=False,
    )
```

```python
import functools
import math

import jax
import jax.numpy as jnp
from jax import lax
from jax.experimental import pallas as pl
from jax.experimental.pallas import tpu as pltpu
from jax.sharding import Mesh
from jax.sharding import PartitionSpec as P

D = 1536
HQ = 24
HKV = 8
HD = 64
FFE = 512
TOPK = 8
EPS = 1e-05
NT = 32
TOK = 64
CROWS = 32
SLOT = 16
CH = D // 128
SROWS = SLOT * CH + 16
BF = jnp.bfloat16
F32 = jnp.float32
TEN = ("zhi", "x", "core")
NEG = -1e30
INTERPRET = False


def vmem():
    return pl.BlockSpec(memory_space=pltpu.VMEM)


def params(mib):
    return pltpu.CompilerParams(vmem_limit_bytes=int(mib * (1 << 20)))


def dot(a, b):
    return lax.dot_general(a, b, (((1,), (0,)), ((), ())), preferred_element_type=F32)


def iota(shape, dim):
    return lax.broadcasted_iota(jnp.int32, shape, dim)


def pack_kernel(q_ref, f_ref, c_ref, o_ref):
    zeros = jnp.zeros((16, HD), BF)
    for g in range(HKV):
        cols = pl.ds(g * 128, 128)
        for quarter in range(4):
            t = g * 4 + quarter
            rows = q_ref[quarter * 16 : quarter * 16 + 16, g * 192 : g * 192 + 192]
            half = quarter % 2
            o_ref[t, 0:16, :] = rows[:, :128]
            o_ref[t, 16:32, :] = jnp.concatenate([rows[:, 128:], zeros], 1)
            o_ref[t, 32:48, :] = c_ref[half * 16 : half * 16 + 16, cols]
            o_ref[t, 48:80, :] = f_ref[half * 32 : half * 32 + 32, cols]


def pack(queries, fresh, cache):
    return pl.pallas_call(
        pack_kernel,
        out_shape=jax.ShapeDtypeStruct((NT, 80, 128), BF),
        in_specs=[vmem()] * 3,
        out_specs=vmem(),
        interpret=INTERPRET,
        name="pack",
    )(queries, fresh, cache)


def attention_kernel(info_ref, own_ref, oth_ref, o_ref, kv, sc, bias_c, bias_d):
    b = pl.program_id(0)
    length, core, quarter = info_ref[0], info_ref[1], info_ref[2]

    @pl.when(b == 0)
    def _():
        kv[0:512, :] = own_ref[:, 32:48, :].reshape(512, 128)
        kv[512:1024, :] = oth_ref[:, 0:16, :].reshape(512, 128)
        for j in range(4):
            base = 1024 + 512 * j
            kv[base : base + 256, :] = own_ref[8 * j : 8 * j + 8, 48:80, :].reshape(256, 128)
            kv[base + 256 : base + 512, :] = oth_ref[8 * j : 8 * j + 8, 16:48, :].reshape(256, 128)
        col = iota((8, 1024), 1)
        half = jnp.where(col < 512, core, 1 - core)
        inner = col % 512
        place = (inner // 16) * 32 + half * 16 + inner % 16
        bias_c[...] = jnp.where(place < length, 0.0, NEG)
        row = iota((128, 512), 0)
        col = iota((128, 512), 1)
        half = jnp.where(col < 256, core, 1 - core)
        inner = col % 256
        key_at = (inner // 32) * 64 + half * 32 + inner % 32
        query_at = (row // 16) * 64 + quarter * 16 + row % 16
        bias_d[...] = jnp.where(key_at <= query_at, 0.0, NEG)

    first = own_ref[pl.ds(b * 8, 8), 0:16, :].reshape(128, 128).astype(F32) * 0.125
    second = own_ref[pl.ds(b * 8, 8), 16:32, :].reshape(128, 128).astype(F32) * 0.125
    low = iota((128, 128), 1) < HD
    q = jnp.concatenate(
        [
            jnp.where(low, first, 0.0),
            jnp.where(low, pltpu.roll(first, HD, 1), 0.0),
            jnp.where(low, second, 0.0),
        ],
        0,
    ).astype(BF)

    def scores(k):
        keys = kv[pl.ds(pl.multiple_of(k * 512, 512), 512), :]
        return lax.dot_general(q, keys, (((1,), (1,)), ((), ())), preferred_element_type=F32)

    def fold(fn, top, s):
        for j in range(4):
            top = fn(top, s[:, j * 128 : j * 128 + 128])
        return top

    top = jnp.full((384, 128), NEG, F32)
    for k in range(2):
        s = scores(k) + bias_c[0:1, k * 512 : k * 512 + 512]
        sc[k] = s
        top = fold(jnp.maximum, top, s)
    s = scores(2 + b)
    s = s + jnp.concatenate([bias_d[...]] * 3, 0)
    sc[2 + b] = s
    top = fold(jnp.maximum, top, s)

    def middle(k, top):
        s = scores(k)
        sc[k] = s
        return fold(jnp.maximum, top, s)

    top = lax.fori_loop(2, 2 + b, middle, top)
    highest = jnp.max(top, 1, keepdims=True)

    def mix(k, carry):
        total, acc = carry
        p = jnp.exp(sc[k] - highest)
        values = kv[pl.ds(pl.multiple_of(k * 512, 512), 512), :]
        return fold(jnp.add, total, p), acc + dot(p.astype(BF), values)

    zero = jnp.zeros((384, 128), F32)
    total, acc = lax.fori_loop(0, 3 + b, mix, (zero, zero))
    out = acc / jnp.sum(total, 1, keepdims=True)
    a0, a1, a2 = out[0:128], out[128:256], out[256:384]
    pair = jnp.where(low, pltpu.roll(a0, HD, 1), a1).astype(BF)
    last = jnp.where(low, pltpu.roll(a2, HD, 1), 0.0).astype(BF)
    o_ref[pl.ds(b * 8, 8), 0:16, :] = pair.reshape(8, 16, 128)
    o_ref[pl.ds(b * 8, 8), 16:32, :] = last.reshape(8, 16, 128)


def attention(info, own, other):
    return pl.pallas_call(
        attention_kernel,
        out_shape=jax.ShapeDtypeStruct((NT, 32, 128), BF),
        grid=(4,),
        in_specs=[
            pl.BlockSpec(memory_space=pltpu.SMEM),
            vmem(),
            vmem(),
        ],
        out_specs=vmem(),
        scratch_shapes=[
            pltpu.VMEM((3072, 128), BF),
            pltpu.VMEM((6, 384, 512), F32),
            pltpu.VMEM((8, 1024), F32),
            pltpu.VMEM((128, 512), F32),
        ],
        compiler_params=params(32),
        cost_estimate=pl.CostEstimate(
            flops=2 * 2 * 1536 * 2304 * 128, bytes_accessed=3 << 20, transcendentals=1536 * 2304
        ),
        interpret=INTERPRET,
        name="attention",
    )(info, own, other)


def merge_kernel(info_ref, own_ref, oth_ref, after_ref, o_ref):
    zlo = info_ref[3]
    o_ref[zlo] = own_ref[...]
    o_ref[1 - zlo] = oth_ref[...]


def merge(info, own, other, after):
    return pl.pallas_call(
        merge_kernel,
        out_shape=jax.ShapeDtypeStruct((2,) + own.shape, BF),
        in_specs=[
            pl.BlockSpec(memory_space=pltpu.SMEM),
            vmem(),
            vmem(),
            pl.BlockSpec(memory_space=pl.ANY),
        ],
        out_specs=vmem(),
        cost_estimate=pl.CostEstimate(flops=1 << 33, bytes_accessed=1 << 20, transcendentals=0),
        interpret=INTERPRET,
        name="merge",
    )(info, own, other, after)


def prepare_kernel(up_ref, down_ref, w_ref, after_ref, o_ref, wo_ref):
    o_ref[0:64, 0:1024] = up_ref[0:64, :]
    o_ref[0:32, 1024:1536] = up_ref[64:96, 0:512]
    o_ref[32:64, 1024:1536] = up_ref[64:96, 512:1024]
    o_ref[64:96, :] = down_ref[...]
    wo_ref[...] = w_ref[...]


def prepare(up, down, weight, after):
    return pl.pallas_call(
        prepare_kernel,
        out_shape=(jax.ShapeDtypeStruct((96, D), BF), jax.ShapeDtypeStruct(weight.shape, BF)),
        in_specs=[vmem()] * 3 + [pl.BlockSpec(memory_space=pl.ANY)],
        out_specs=(vmem(), vmem()),
        cost_estimate=pl.CostEstimate(flops=1 << 33, bytes_accessed=1 << 20, transcendentals=0),
        interpret=INTERPRET,
        name="prepare",
    )(up, down, weight, after)


def load_weight(src_ref, zhi, w, sems):
    copies = []
    for j in range(NT // 2):
        turn = (zhi + 4 - j // 4) % 4
        copies.append(
            pltpu.make_async_copy(src_ref.at[j % 4, turn], w.at[j * 48 : j * 48 + 48, :], sems.at[j])
        )
        copies[-1].start()
    return copies


def columns(att_ref, side):
    pieces = []
    for g in range(HKV):
        pair = att_ref[g * 4 : g * 4 + 4, 0:16, :].reshape(TOK, 128).astype(F32)
        last = att_ref[g * 4 : g * 4 + 4, 16:32, :].reshape(TOK, 128).astype(F32)
        every = jnp.concatenate([pair, last[:, :HD]], 1)
        for x in range(2):
            at = x * 96
            pieces.append(jnp.where(side == 0, every[:, at : at + 48], every[:, at + 48 : at + 96]))
    return jnp.concatenate(pieces, 1).astype(BF)


def own_part_kernel(info_ref, att_ref, w_ref, o_ref, w, sems):
    copies = load_weight(w_ref, info_ref[4], w, sems)
    cols = columns(att_ref, info_ref[1])
    for copy in copies:
        copy.wait()
    o_ref[...] = dot(cols, w[...])


def own_part(info, att, weight):
    return pl.pallas_call(
        own_part_kernel,
        out_shape=jax.ShapeDtypeStruct((TOK, D), F32),
        in_specs=[
            pl.BlockSpec(memory_space=pltpu.SMEM),
            vmem(),
            pl.BlockSpec(memory_space=pltpu.HBM),
        ],
        out_specs=vmem(),
        scratch_shapes=[pltpu.VMEM((D // 2, D), BF), pltpu.SemaphoreType.DMA((NT // 2,))],
        compiler_params=params(61.7),
        cost_estimate=pl.CostEstimate(flops=1 << 34, bytes_accessed=3 << 20, transcendentals=0),
        interpret=INTERPRET,
        name="own_part",
    )(info, att, weight)


def project_kernel(info_ref, att_ref, part_ref, w_ref, hid_ref, gain_ref, ids_ref, res_ref, disp_ref, w, sems):
    copies = load_weight(w_ref, info_ref[4], w, sems)
    cols = columns(att_ref, 1 - info_ref[1])

    experts = iota((NT, TOK), 0)
    named = jnp.zeros((NT, TOK), F32)
    for k in range(TOPK):
        named = named + jnp.where(ids_ref[k : k + 1, :] == experts, 1.0, 0.0)
    before = jnp.where(iota((TOK, TOK), 0) < iota((TOK, TOK), 1), 1.0, 0.0).astype(BF)
    rank = dot(named.astype(BF), before)
    rank = jnp.where(named > 0.5, rank, -1.0).astype(BF)
    spread = jnp.where(iota((512, NT), 0) // SLOT == iota((512, NT), 1), 1.0, 0.0).astype(BF)
    ranks = dot(spread, rank)
    place = iota((512, TOK), 0) % SLOT
    pick = jnp.where(ranks == place.astype(F32), 1.0, 0.0).astype(BF)
    late = jnp.where(ranks == float(SLOT), 1.0, 0.0)

    base = hid_ref[...].astype(F32) + part_ref[...]
    for copy in copies:
        copy.wait()
    total = base + dot(cols, w[...])
    res_ref[...] = total
    meansq = jnp.mean(total * total, 1, keepdims=True)
    normed = (total * lax.rsqrt(meansq + EPS) * gain_ref[...]).astype(BF)
    extra = jnp.zeros((512, 128), F32)
    for c in range(CH):
        chunk = normed[:, c * 128 : c * 128 + 128]
        disp_ref[:, c * SLOT : (c + 1) * SLOT, :] = (
            dot(pick, chunk).astype(BF).reshape(NT, SLOT, 128)
        )
        extra = extra + dot(jnp.where(place == c, late, 0.0).astype(BF), chunk)
    disp_ref[:, SLOT * CH : SROWS, :] = extra.astype(BF).reshape(NT, 16, 128)


def project(info, att, part, weight, hidden, gain, ids_t):
    return pl.pallas_call(
        project_kernel,
        out_shape=(
            jax.ShapeDtypeStruct((TOK, D), F32),
            jax.ShapeDtypeStruct((NT, SROWS, 128), BF),
        ),
        in_specs=[
            pl.BlockSpec(memory_space=pltpu.SMEM),
            vmem(),
            vmem(),
            pl.BlockSpec(memory_space=pltpu.HBM),
            vmem(),
            vmem(),
            vmem(),
        ],
        out_specs=(vmem(), vmem()),
        scratch_shapes=[pltpu.VMEM((D // 2, D), BF), pltpu.SemaphoreType.DMA((NT // 2,))],
        compiler_params=params(61.7),
        cost_estimate=pl.CostEstimate(
            flops=2 * TOK * D * D, bytes_accessed=8 << 20, transcendentals=0
        ),
        interpret=INTERPRET,
        name="project",
    )(info, att, part, weight, hidden, gain, ids_t)


def gather_extra(block):
    rows = iota((CH * NT, 512), 0)
    cols = iota((CH * NT, 512), 1)
    match = (rows % NT == cols // 16) & (rows // NT == cols % 16)
    stacked = dot(jnp.where(match, 1.0, 0.0).astype(BF), block).astype(BF)
    return [stacked[c * NT : (c + 1) * NT, :] for c in range(CH)]


def spread_extra(rows):
    place = iota((512, NT), 0)
    owner = place // 16 == iota((512, NT), 1)
    out = jnp.zeros((512, 128), F32)
    for c in range(CH):
        match = jnp.where(owner & (place % 16 == c), 1.0, 0.0).astype(BF)
        out = out + dot(match, rows[:, c * 128 : c * 128 + 128])
    return out.astype(BF)


def expert_kernel(in_ref, w_ref, o_ref, x, w1, w2, sems):
    blocks = w_ref.shape[0]
    copies = []
    for d in range(blocks):
        pieces = (
            (w_ref.at[d, 0:64, 0:1024], w1.at[d * 96 : d * 96 + 64, :]),
            (w_ref.at[d, 0:32, 1024:1536], w1.at[d * 96 + 64 : d * 96 + 96, 0:512]),
            (w_ref.at[d, 32:64, 1024:1536], w1.at[d * 96 + 64 : d * 96 + 96, 512:1024]),
            (w_ref.at[d, 64:96, :], w2.at[d * 32 : d * 32 + 32, :]),
        )
        for n, (src, dst) in enumerate(pieces):
            copies.append(pltpu.make_async_copy(src, dst, sems.at[d, n]))
    firsts = [copy for i, copy in enumerate(copies) if i % 4 < 3]
    lasts = copies[3::4]
    for copy in firsts + lasts:
        copy.start()
    for c in range(CH):
        x[0:512, c * 128 : c * 128 + 128] = in_ref[:, c * SLOT : (c + 1) * SLOT, :].reshape(512, 128)
    chunks = gather_extra(in_ref[:, SLOT * CH : SROWS, :].reshape(512, 128))
    for c in range(CH):
        x[512:544, c * 128 : c * 128 + 128] = chunks[c]
    for copy in firsts:
        copy.wait()
    hidden = dot(x[...], w1[...])
    gate = hidden[:, :FFE]
    active = (gate / (1.0 + jnp.exp(-gate)) * hidden[:, FFE:]).astype(BF)
    for copy in lasts:
        copy.wait()
    out = dot(active, w2[...]).astype(BF)
    for c in range(CH):
        o_ref[:, c * SLOT : (c + 1) * SLOT, :] = out[0:512, c * 128 : c * 128 + 128].reshape(
            NT, SLOT, 128
        )
    o_ref[:, SLOT * CH : SROWS, :] = spread_extra(out[512:544, :]).reshape(NT, 16, 128)


def expert(slots, weights):
    blocks = weights.shape[0]
    return pl.pallas_call(
        expert_kernel,
        out_shape=jax.ShapeDtypeStruct((NT, SROWS, 128), BF),
        in_specs=[vmem(), pl.BlockSpec(memory_space=pltpu.HBM)],
        out_specs=vmem(),
        scratch_shapes=[
            pltpu.VMEM((544, D), BF),
            pltpu.VMEM((blocks * 96, 2 * FFE), BF),
            pltpu.VMEM((blocks * 32, D), BF),
            pltpu.SemaphoreType.DMA((blocks, 4)),
        ],
        compiler_params=params(59.5),
        cost_estimate=pl.CostEstimate(
            flops=2 * 544 * 1536 * 1536, bytes_accessed=9 << 20, transcendentals=544 * 512
        ),
        interpret=INTERPRET,
        name="expert",
    )(slots, weights)


def combine_kernel(in_ref, res_ref, ids_ref, gate_ref, o_ref):
    experts = iota((TOK, NT), 1)
    named = jnp.zeros((TOK, NT), F32)
    gates = jnp.zeros((TOK, NT), F32)
    for k in range(TOPK):
        match = ids_ref[:, k : k + 1] == experts
        named = named + jnp.where(match, 1.0, 0.0)
        gates = gates + jnp.where(match, gate_ref[:, k : k + 1], 0.0)
    before = jnp.where(iota((TOK, TOK), 1) < iota((TOK, TOK), 0), 1.0, 0.0).astype(BF)
    rank = dot(before, named.astype(BF))
    rank = jnp.where(named > 0.5, rank, -1.0)
    spread = jnp.where(iota((NT, 512), 0) == iota((NT, 512), 1) // SLOT, 1.0, 0.0).astype(BF)
    place = (iota((TOK, 512), 1) % SLOT).astype(F32)
    pick = dot(rank.astype(BF), spread) == place
    high = gates.astype(BF)
    low = (gates - high.astype(F32)).astype(BF)
    weights = jnp.concatenate(
        [jnp.where(pick, dot(part, spread), 0.0).astype(BF) for part in (high, low)], 0
    )
    late = rank == float(SLOT)
    late_weights = jnp.concatenate(
        [jnp.where(late, part.astype(F32), 0.0).astype(BF) for part in (high, low)], 0
    )
    chunks = gather_extra(in_ref[:, SLOT * CH : SROWS, :].reshape(512, 128))
    for c in range(CH):
        main = in_ref[:, c * SLOT : (c + 1) * SLOT, :].reshape(512, 128)
        both = dot(weights, main) + dot(late_weights, chunks[c])
        cols = slice(c * 128, c * 128 + 128)
        o_ref[:, cols] = (res_ref[:, cols] + (both[:TOK] + both[TOK:])).astype(BF)


def combine(returned, residual, ids, gates):
    return pl.pallas_call(
        combine_kernel,
        out_shape=jax.ShapeDtypeStruct((TOK, D), BF),
        in_specs=[vmem()] * 4,
        out_specs=vmem(),
        compiler_params=params(32),
        interpret=INTERPRET,
        name="combine",
    )(returned, residual, ids, gates)


def shards(
    hidden_in,
    rotated_queries,
    fresh_key_values,
    cached_key_values,
    cached_len,
    expert_ids,
    route_gates,
    output_weight,
    norm_gain,
    gate_up,
    down_weight,
):
    zlo = lax.axis_index("zlo")
    zhi = lax.axis_index("zhi")
    core = lax.axis_index("core")
    quarter = lax.axis_index(TEN) % 4
    length = cached_len[0]
    ids = expert_ids[0, 0, 0]
    gates = route_gates[0, 0, 0]

    send = pack(rotated_queries[0, 0, 0], fresh_key_values[0, 0, 0], cached_key_values[0])
    packed, shard = prepare(gate_up[0], down_weight[0], output_weight, send)
    across = lax.ppermute(packed, "zlo", [(0, 1), (1, 0)])
    turns = [
        lax.ppermute(shard, "zhi", [(z, (z + step) % 4) for z in range(4)]) for step in (1, 3, 2)
    ]
    own = lax.all_to_all(send, TEN, split_axis=0, concat_axis=0, tiled=True)
    (shard, back1, back3, back2, across), _ = lax.optimization_barrier(
        ((shard, *turns, across), own)
    )
    column = jnp.stack([shard, back1, back2, back3], 0)
    own_weight = lax.all_gather(column, "x", axis=0)
    other = lax.ppermute(own[:, 32:, :], "core", [(0, 1), (1, 0)])
    info = jnp.stack([length, core.astype(jnp.int32), quarter.astype(jnp.int32), zlo.astype(jnp.int32), zhi.astype(jnp.int32)])
    attended = attention(info, own, other)
    both = merge(info, packed, across, attended)
    weights = lax.all_gather(both, "y", axis=0, tiled=True)
    att = lax.all_to_all(attended, TEN, split_axis=0, concat_axis=0, tiled=True)
    swapping, _ = lax.optimization_barrier((own_weight, att))
    other_weight = lax.ppermute(swapping, "core", [(0, 1), (1, 0)])
    part = own_part(info, att, own_weight)
    residual, outbound = project(
        info, att, part, other_weight, hidden_in[0, 0, 0], norm_gain[None], ids.T
    )
    slots = lax.all_to_all(outbound, TEN, split_axis=0, concat_axis=0, tiled=True)
    computed = expert(slots, weights)
    returned = lax.all_to_all(computed, TEN, split_axis=0, concat_axis=0, tiled=True)
    hidden_out = combine(returned, residual, ids, gates)

    mine = lax.dynamic_slice_in_dim(own[:, 32:, :], quarter * 32, 32, 2)
    theirs = lax.dynamic_slice_in_dim(other, quarter * 32, 32, 2)
    halves = jnp.where(
        core == 0, jnp.stack([mine, theirs], 1), jnp.stack([theirs, mine], 1)
    )
    old_rows = halves[:, :, :16].reshape(NT * CROWS, 32)
    new_rows = halves[:, :, 16:].reshape(NT * TOK, 32)
    total = NT * CROWS + NT * TOK
    base = jnp.concatenate([old_rows, jnp.zeros((NT * TOK, 32), BF)], 0)
    base = jnp.where((jnp.arange(total, dtype=jnp.int32) < length)[:, None], base, jnp.zeros_like(base))
    cache_out = lax.dynamic_update_slice_in_dim(base, new_rows, length, 0)
    return hidden_out.reshape(1, 1, 1, TOK, D), cache_out[None]


def solution(mesh):
    dp, tensor = mesh.devices.shape
    fine = Mesh(mesh.devices.reshape(dp // 2, 2, 4, 4, 2), ("y", "zlo", "zhi", "x", "core"))
    ydp = ("y", "zlo")
    return jax.shard_map(
        shards,
        mesh=fine,
        in_specs=(
            P(ydp, TEN, None, None, None),
            P(ydp, TEN, None, None, None),
            P(ydp, TEN, None, None, None),
            P(ydp, TEN, None),
            P(ydp),
            P(ydp, TEN, None, None, None),
            P(ydp, TEN, None, None, None),
            P(TEN, None),
            P(),
            P(TEN, ydp, None),
            P(TEN, ydp, None),
        ),
        out_specs=(P(ydp, TEN, None, None, None), P(ydp, None, TEN)),
        check_vma=False,
    )
```

```python
import functools
import math

import jax
import jax.numpy as jnp
from jax import lax
from jax.experimental import pallas as pl
from jax.experimental.pallas import tpu as pltpu
from jax.sharding import Mesh
from jax.sharding import PartitionSpec as P

D = 1536
HQ = 24
HKV = 8
HD = 64
FFE = 512
TOPK = 8
EPS = 1e-05
NT = 32
TOK = 64
CROWS = 32
SLOT = 16
CH = D // 128
SROWS = SLOT * CH + 16
BF = jnp.bfloat16
F32 = jnp.float32
TEN = ("zhi", "x", "core")
NEG = -1e30
INTERPRET = False


def vmem():
    return pl.BlockSpec(memory_space=pltpu.VMEM)


def params(mib):
    return pltpu.CompilerParams(vmem_limit_bytes=int(mib * (1 << 20)))


def dot(a, b):
    return lax.dot_general(a, b, (((1,), (0,)), ((), ())), preferred_element_type=F32)


def iota(shape, dim):
    return lax.broadcasted_iota(jnp.int32, shape, dim)


def pack_kernel(q_ref, f_ref, c_ref, o_ref):
    for t in range(NT):
        g = t // 8 * 2 + t % 2
        x = t // 2 % 4
        cols = pl.ds(g * 128, 128)
        rows = q_ref[x * 16 : x * 16 + 16, g * 192 : g * 192 + 192]
        o_ref[t, 0:16, :] = rows[:, :128]
        o_ref[t, 16:48, :] = c_ref[:, cols]
        o_ref[t, 48:112, :] = f_ref[:, cols]
        last = rows[:, 128:].astype(F32)
        o_ref[t, 112:120, :] = jnp.concatenate([last[0:8], last[8:16]], 1).astype(BF)


def pack(queries, fresh, cache):
    return pl.pallas_call(
        pack_kernel,
        out_shape=jax.ShapeDtypeStruct((NT, 120, 128), BF),
        in_specs=[vmem()] * 3,
        out_specs=vmem(),
        interpret=INTERPRET,
        name="pack",
    )(queries, fresh, cache)


def attention_kernel(info_ref, own_ref, keep_ref, send_ref, kv, sc, bias_c, bias_d):
    b = pl.program_id(0)
    length, core, x = info_ref[0], info_ref[1], info_ref[2]

    @pl.when(b == 0)
    def _():
        kv[0:1024, :] = own_ref[:, 16:48, :].reshape(1024, 128)
        kv[1024:3072, :] = own_ref[:, 48:112, :].reshape(2048, 128)
        bias_c[...] = jnp.where(iota((8, 1024), 1) < length, 0.0, NEG)
        row = iota((128, 512), 0)
        query_at = (row // 16) * 64 + x * 16 + row % 16
        bias_d[...] = jnp.where(iota((128, 512), 1) <= query_at, 0.0, NEG)

    first = own_ref[pl.ds(b * 8, 8), 0:16, :].reshape(128, 128).astype(F32) * 0.125
    last = own_ref[pl.ds(b * 8, 8), 112:120, :].astype(F32).reshape(64, 128) * 0.125
    low = iota((128, 128), 1) < HD
    low2 = iota((64, 128), 1) < HD
    third = jnp.concatenate(
        [
            jnp.where(low2, last, 0.0).reshape(8, 8, 128),
            jnp.where(low2, pltpu.roll(last, HD, 1), 0.0).reshape(8, 8, 128),
        ],
        1,
    ).reshape(128, 128)
    q = jnp.concatenate(
        [jnp.where(low, first, 0.0), jnp.where(low, pltpu.roll(first, HD, 1), 0.0), third], 0
    ).astype(BF)

    def scores(k):
        keys = kv[pl.ds(pl.multiple_of(k * 512, 512), 512), :]
        return lax.dot_general(q, keys, (((1,), (1,)), ((), ())), preferred_element_type=F32)

    def fold(fn, top, s):
        for j in range(4):
            top = fn(top, s[:, j * 128 : j * 128 + 128])
        return top

    top = jnp.full((384, 128), NEG, F32)
    for k in range(2):
        s = scores(k) + bias_c[0:1, k * 512 : k * 512 + 512]
        sc[k] = s
        top = fold(jnp.maximum, top, s)
    s = scores(2 + b)
    s = s + jnp.concatenate([bias_d[...]] * 3, 0)
    sc[2 + b] = s
    top = fold(jnp.maximum, top, s)

    def middle(k, top):
        s = scores(k)
        sc[k] = s
        return fold(jnp.maximum, top, s)

    top = lax.fori_loop(2, 2 + b, middle, top)
    highest = jnp.max(top, 1, keepdims=True)

    def mix(k, carry):
        total, acc = carry
        p = jnp.exp(sc[k] - highest)
        values = kv[pl.ds(pl.multiple_of(k * 512, 512), 512), :]
        return fold(jnp.add, total, p), acc + dot(p.astype(BF), values)

    zero = jnp.zeros((384, 128), F32)
    total, acc = lax.fori_loop(0, 3 + b, mix, (zero, zero))
    out = acc / jnp.sum(total, 1, keepdims=True)
    a0, a1, a2 = out[0:128], out[128:256], out[256:384]
    tiles = (jnp.where(low, pltpu.roll(a0, HD, 1), a1), jnp.where(low, pltpu.roll(a2, HD, 1), 0.0))
    for n, tile in enumerate(tiles):
        halves = tile.reshape(4, 2, 16, 128)
        even, odd = halves[:, 0], halves[:, 1]
        rows = slice(n * 16, n * 16 + 16)
        keep_ref[pl.ds(b * 4, 4), rows, :] = jnp.where(core == 0, even, odd).astype(BF)
        send_ref[pl.ds(b * 4, 4), rows, :] = jnp.where(core == 0, odd, even).astype(BF)


def attention(info, own):
    shape = jax.ShapeDtypeStruct((NT // 2, 32, 128), BF)
    return pl.pallas_call(
        attention_kernel,
        out_shape=(shape, shape),
        grid=(4,),
        in_specs=[pl.BlockSpec(memory_space=pltpu.SMEM), vmem()],
        out_specs=(vmem(), vmem()),
        scratch_shapes=[
            pltpu.VMEM((3072, 128), BF),
            pltpu.VMEM((6, 384, 512), F32),
            pltpu.VMEM((8, 1024), F32),
            pltpu.VMEM((128, 512), F32),
        ],
        compiler_params=params(32),
        cost_estimate=pl.CostEstimate(
            flops=2 * 2 * 1536 * 2304 * 128, bytes_accessed=3 << 20, transcendentals=1536 * 2304
        ),
        interpret=INTERPRET,
        name="attention",
    )(info, own)


def group_sums_kernel(info_ref, own_ref, oth_ref, w_ref, o_ref):
    core = info_ref[1]
    total = jnp.zeros((256, D), F32)
    for src, side in ((own_ref, core), (oth_ref, 1 - core)):
        pair = src[:, 0:16, :].reshape(256, 128)
        last = src[:, 16:32, :].reshape(256, 128)[:, :HD]
        at = pl.multiple_of(side * 192, 64)
        total = total + dot(pair, w_ref[pl.ds(at, 128), :])
        total = total + dot(last, w_ref[pl.ds(pl.multiple_of(at + 128, 64), HD), :])
    o_ref[...] = total.astype(BF).reshape(NT // 2, 16, D)


def group_sums(info, own, other, weight):
    return pl.pallas_call(
        group_sums_kernel,
        out_shape=jax.ShapeDtypeStruct((NT // 2, 16, D), BF),
        in_specs=[pl.BlockSpec(memory_space=pltpu.SMEM)] + [vmem()] * 3,
        out_specs=vmem(),
        compiler_params=params(24),
        cost_estimate=pl.CostEstimate(flops=2 * 256 * 384 * D, bytes_accessed=2 << 20, transcendentals=0),
        interpret=INTERPRET,
        name="group_sums",
    )(info, own, other, weight)


def merge_kernel(info_ref, own_ref, oth_ref, after_ref, o_ref):
    zlo = info_ref[3]
    o_ref[zlo] = own_ref[...]
    o_ref[1 - zlo] = oth_ref[...]


def merge(info, own, other, after):
    return pl.pallas_call(
        merge_kernel,
        out_shape=jax.ShapeDtypeStruct((2,) + own.shape, BF),
        in_specs=[
            pl.BlockSpec(memory_space=pltpu.SMEM),
            vmem(),
            vmem(),
            pl.BlockSpec(memory_space=pl.ANY),
        ],
        out_specs=vmem(),
        cost_estimate=pl.CostEstimate(flops=1 << 33, bytes_accessed=1 << 20, transcendentals=0),
        interpret=INTERPRET,
        name="merge",
    )(info, own, other, after)


def prepare_kernel(up_ref, down_ref, after_ref, o_ref):
    o_ref[0:64, 0:1024] = up_ref[0:64, :]
    o_ref[0:32, 1024:1536] = up_ref[64:96, 0:512]
    o_ref[32:64, 1024:1536] = up_ref[64:96, 512:1024]
    o_ref[64:96, :] = down_ref[...]


def prepare(up, down, after):
    return pl.pallas_call(
        prepare_kernel,
        out_shape=jax.ShapeDtypeStruct((96, D), BF),
        in_specs=[vmem()] * 2 + [pl.BlockSpec(memory_space=pl.ANY)],
        out_specs=vmem(),
        cost_estimate=pl.CostEstimate(flops=1 << 33, bytes_accessed=1 << 20, transcendentals=0),
        interpret=INTERPRET,
        name="prepare",
    )(up, down, after)


def norm_dispatch_kernel(sum_ref, hid_ref, gain_ref, ids_ref, res_ref, disp_ref):
    experts = iota((NT, TOK), 0)
    named = jnp.zeros((NT, TOK), F32)
    for k in range(TOPK):
        named = named + jnp.where(ids_ref[k : k + 1, :] == experts, 1.0, 0.0)
    before = jnp.where(iota((TOK, TOK), 0) < iota((TOK, TOK), 1), 1.0, 0.0).astype(BF)
    rank = dot(named.astype(BF), before)
    rank = jnp.where(named > 0.5, rank, -1.0).astype(BF)
    spread = jnp.where(iota((512, NT), 0) // SLOT == iota((512, NT), 1), 1.0, 0.0).astype(BF)
    ranks = dot(spread, rank)
    place = iota((512, TOK), 0) % SLOT
    pick = jnp.where(ranks == place.astype(F32), 1.0, 0.0).astype(BF)
    late = jnp.where(ranks == float(SLOT), 1.0, 0.0)

    total = hid_ref[...].astype(F32)
    for z in range(4):
        total = total + sum_ref[z * 4 : z * 4 + 4].reshape(TOK, D).astype(F32)
    res_ref[...] = total
    meansq = jnp.mean(total * total, 1, keepdims=True)
    normed = (total * lax.rsqrt(meansq + EPS) * gain_ref[...]).astype(BF)
    extra = jnp.zeros((512, 128), F32)
    for c in range(CH):
        chunk = normed[:, c * 128 : c * 128 + 128]
        disp_ref[:, c * SLOT : (c + 1) * SLOT, :] = (
            dot(pick, chunk).astype(BF).reshape(NT, SLOT, 128)
        )
        extra = extra + dot(jnp.where(place == c, late, 0.0).astype(BF), chunk)
    disp_ref[:, SLOT * CH : SROWS, :] = extra.astype(BF).reshape(NT, 16, 128)


def norm_dispatch(sums, hidden, gain, ids_t):
    return pl.pallas_call(
        norm_dispatch_kernel,
        out_shape=(
            jax.ShapeDtypeStruct((TOK, D), F32),
            jax.ShapeDtypeStruct((NT, SROWS, 128), BF),
        ),
        in_specs=[vmem()] * 4,
        out_specs=(vmem(), vmem()),
        compiler_params=params(32),
        cost_estimate=pl.CostEstimate(flops=1 << 30, bytes_accessed=4 << 20, transcendentals=0),
        interpret=INTERPRET,
        name="norm_dispatch",
    )(sums, hidden, gain, ids_t)


def gather_extra(block):
    rows = iota((CH * NT, 512), 0)
    cols = iota((CH * NT, 512), 1)
    match = (rows % NT == cols // 16) & (rows // NT == cols % 16)
    stacked = dot(jnp.where(match, 1.0, 0.0).astype(BF), block).astype(BF)
    return [stacked[c * NT : (c + 1) * NT, :] for c in range(CH)]


def spread_extra(rows):
    place = iota((512, NT), 0)
    owner = place // 16 == iota((512, NT), 1)
    out = jnp.zeros((512, 128), F32)
    for c in range(CH):
        match = jnp.where(owner & (place % 16 == c), 1.0, 0.0).astype(BF)
        out = out + dot(match, rows[:, c * 128 : c * 128 + 128])
    return out.astype(BF)


def expert_kernel(in_ref, w_ref, o_ref, x, w1, w2, sems):
    blocks = w_ref.shape[0]
    copies = []
    for d in range(blocks):
        pieces = (
            (w_ref.at[d, 0:64, 0:1024], w1.at[d * 96 : d * 96 + 64, :]),
            (w_ref.at[d, 0:32, 1024:1536], w1.at[d * 96 + 64 : d * 96 + 96, 0:512]),
            (w_ref.at[d, 32:64, 1024:1536], w1.at[d * 96 + 64 : d * 96 + 96, 512:1024]),
            (w_ref.at[d, 64:96, :], w2.at[d * 32 : d * 32 + 32, :]),
        )
        for n, (src, dst) in enumerate(pieces):
            copies.append(pltpu.make_async_copy(src, dst, sems.at[d, n]))
    firsts = [copy for i, copy in enumerate(copies) if i % 4 < 3]
    lasts = copies[3::4]
    for copy in firsts + lasts:
        copy.start()
    for c in range(CH):
        x[0:512, c * 128 : c * 128 + 128] = in_ref[:, c * SLOT : (c + 1) * SLOT, :].reshape(512, 128)
    chunks = gather_extra(in_ref[:, SLOT * CH : SROWS, :].reshape(512, 128))
    for c in range(CH):
        x[512:544, c * 128 : c * 128 + 128] = chunks[c]
    for copy in firsts:
        copy.wait()
    hidden = dot(x[...], w1[...])
    gate = hidden[:, :FFE]
    active = (gate / (1.0 + jnp.exp(-gate)) * hidden[:, FFE:]).astype(BF)
    for copy in lasts:
        copy.wait()
    out = dot(active, w2[...]).astype(BF)
    for c in range(CH):
        o_ref[:, c * SLOT : (c + 1) * SLOT, :] = out[0:512, c * 128 : c * 128 + 128].reshape(
            NT, SLOT, 128
        )
    o_ref[:, SLOT * CH : SROWS, :] = spread_extra(out[512:544, :]).reshape(NT, 16, 128)


def expert(slots, weights):
    blocks = weights.shape[0]
    return pl.pallas_call(
        expert_kernel,
        out_shape=jax.ShapeDtypeStruct((NT, SROWS, 128), BF),
        in_specs=[vmem(), pl.BlockSpec(memory_space=pltpu.HBM)],
        out_specs=vmem(),
        scratch_shapes=[
            pltpu.VMEM((544, D), BF),
            pltpu.VMEM((blocks * 96, 2 * FFE), BF),
            pltpu.VMEM((blocks * 32, D), BF),
            pltpu.SemaphoreType.DMA((blocks, 4)),
        ],
        compiler_params=params(58),
        cost_estimate=pl.CostEstimate(
            flops=2 * 544 * 1536 * 1536, bytes_accessed=9 << 20, transcendentals=544 * 512
        ),
        interpret=INTERPRET,
        name="expert",
    )(slots, weights)


def combine_kernel(in_ref, res_ref, ids_ref, gate_ref, o_ref):
    experts = iota((TOK, NT), 1)
    named = jnp.zeros((TOK, NT), F32)
    gates = jnp.zeros((TOK, NT), F32)
    for k in range(TOPK):
        match = ids_ref[:, k : k + 1] == experts
        named = named + jnp.where(match, 1.0, 0.0)
        gates = gates + jnp.where(match, gate_ref[:, k : k + 1], 0.0)
    before = jnp.where(iota((TOK, TOK), 1) < iota((TOK, TOK), 0), 1.0, 0.0).astype(BF)
    rank = dot(before, named.astype(BF))
    rank = jnp.where(named > 0.5, rank, -1.0)
    spread = jnp.where(iota((NT, 512), 0) == iota((NT, 512), 1) // SLOT, 1.0, 0.0).astype(BF)
    place = (iota((TOK, 512), 1) % SLOT).astype(F32)
    pick = dot(rank.astype(BF), spread) == place
    high = gates.astype(BF)
    low = (gates - high.astype(F32)).astype(BF)
    weights = jnp.concatenate(
        [jnp.where(pick, dot(part, spread), 0.0).astype(BF) for part in (high, low)], 0
    )
    late = rank == float(SLOT)
    late_weights = jnp.concatenate(
        [jnp.where(late, part.astype(F32), 0.0).astype(BF) for part in (high, low)], 0
    )
    chunks = gather_extra(in_ref[:, SLOT * CH : SROWS, :].reshape(512, 128))
    for c in range(CH):
        main = in_ref[:, c * SLOT : (c + 1) * SLOT, :].reshape(512, 128)
        both = dot(weights, main) + dot(late_weights, chunks[c])
        cols = slice(c * 128, c * 128 + 128)
        o_ref[:, cols] = (res_ref[:, cols] + (both[:TOK] + both[TOK:])).astype(BF)


def combine(returned, residual, ids, gates):
    return pl.pallas_call(
        combine_kernel,
        out_shape=jax.ShapeDtypeStruct((TOK, D), BF),
        in_specs=[vmem()] * 4,
        out_specs=vmem(),
        compiler_params=params(32),
        interpret=INTERPRET,
        name="combine",
    )(returned, residual, ids, gates)


def shards(
    hidden_in,
    rotated_queries,
    fresh_key_values,
    cached_key_values,
    cached_len,
    expert_ids,
    route_gates,
    output_weight,
    norm_gain,
    gate_up,
    down_weight,
):
    zlo = lax.axis_index("zlo").astype(jnp.int32)
    x = lax.axis_index("x").astype(jnp.int32)
    core = lax.axis_index("core").astype(jnp.int32)
    length = cached_len[0]
    info = jnp.stack([length, core, x, zlo])
    ids = expert_ids[0, 0, 0]
    gates = route_gates[0, 0, 0]

    plane_weight = lax.all_gather(output_weight, ("x", "core"), axis=0, tiled=True)
    send = pack(rotated_queries[0, 0, 0], fresh_key_values[0, 0, 0], cached_key_values[0])
    packed = prepare(gate_up[0], down_weight[0], send)
    across = lax.ppermute(packed, "zlo", [(0, 1), (1, 0)])
    own = lax.all_to_all(send, TEN, split_axis=0, concat_axis=0, tiled=True)
    own, across = lax.optimization_barrier((own, across))
    kept, sent = attention(info, own)
    swapped = lax.ppermute(sent, "core", [(0, 1), (1, 0)])
    terms = group_sums(info, kept, swapped, plane_weight)
    both = merge(info, packed, across, terms)
    weights = lax.all_gather(both, "y", axis=0, tiled=True)
    sums = lax.all_to_all(terms, ("zhi", "x"), split_axis=0, concat_axis=0, tiled=True)
    residual, outbound = norm_dispatch(sums, hidden_in[0, 0, 0], norm_gain[None], ids.T)
    slots = lax.all_to_all(outbound, TEN, split_axis=0, concat_axis=0, tiled=True)
    computed = expert(slots, weights)
    returned = lax.all_to_all(computed, TEN, split_axis=0, concat_axis=0, tiled=True)
    hidden_out = combine(returned, residual, ids, gates)

    pairs = own[:, 16:112, :]
    low_x = x % 2
    mine = lax.dynamic_slice_in_dim(pairs, (low_x * 2 + core) * 32, 32, 2)
    for_other = lax.dynamic_slice_in_dim(pairs, (low_x * 2 + 1 - core) * 32, 32, 2)
    theirs = lax.ppermute(for_other, "core", [(0, 1), (1, 0)])
    chosen = jnp.where(core == x // 2, mine, theirs)
    old_rows = chosen[:, :CROWS].reshape(NT * CROWS, 32)
    new_rows = chosen[:, CROWS:].reshape(NT * TOK, 32)
    total = NT * CROWS + NT * TOK
    base = jnp.concatenate([old_rows, jnp.zeros((NT * TOK, 32), BF)], 0)
    base = jnp.where((jnp.arange(total, dtype=jnp.int32) < length)[:, None], base, jnp.zeros_like(base))
    cache_out = lax.dynamic_update_slice_in_dim(base, new_rows, length, 0)
    return hidden_out.reshape(1, 1, 1, TOK, D), cache_out[None]


def solution(mesh):
    dp, tensor = mesh.devices.shape
    fine = Mesh(mesh.devices.reshape(dp // 2, 2, 4, 4, 2), ("y", "zlo", "zhi", "x", "core"))
    ydp = ("y", "zlo")
    return jax.shard_map(
        shards,
        mesh=fine,
        in_specs=(
            P(ydp, TEN, None, None, None),
            P(ydp, TEN, None, None, None),
            P(ydp, TEN, None, None, None),
            P(ydp, TEN, None),
            P(ydp),
            P(ydp, TEN, None, None, None),
            P(ydp, TEN, None, None, None),
            P(TEN, None),
            P(),
            P(TEN, ydp, None),
            P(TEN, ydp, None),
        ),
        out_specs=(P(ydp, TEN, None, None, None), P(ydp, None, TEN)),
        check_vma=False,
    )
```

```python
import functools
import math

import jax
import jax.numpy as jnp
from jax import lax
from jax.experimental import pallas as pl
from jax.experimental.pallas import tpu as pltpu
from jax.sharding import Mesh
from jax.sharding import PartitionSpec as P

D = 1536
HQ = 24
HKV = 8
HD = 64
FFE = 512
TOPK = 8
EPS = 1e-05
NT = 32
TOK = 64
CROWS = 32
SLOT = 16
CH = D // 128
SROWS = SLOT * CH + 16
BF = jnp.bfloat16
F32 = jnp.float32
TEN = ("zhi", "x", "core")
NEG = -1e30
INTERPRET = False


def vmem():
    return pl.BlockSpec(memory_space=pltpu.VMEM)


def params(mib):
    return pltpu.CompilerParams(vmem_limit_bytes=int(mib * (1 << 20)))


def dot(a, b):
    return lax.dot_general(a, b, (((1,), (0,)), ((), ())), preferred_element_type=F32)


def iota(shape, dim):
    return lax.broadcasted_iota(jnp.int32, shape, dim)


def pack_kernel(q_ref, f_ref, c_ref, o_ref):
    for g in range(HKV):
        cols = pl.ds(g * 128, 128)
        rows = q_ref[:, g * 192 : g * 192 + 192]
        o_ref[g, 0:64, :] = rows[:, :128]
        o_ref[g, 64:96, :] = jnp.concatenate([rows[0:32, 128:], rows[32:64, 128:]], 1)
        o_ref[g, 96:128, :] = c_ref[:, cols]
        o_ref[g, 128:192, :] = f_ref[:, cols]


def pack(queries, fresh, cache):
    return pl.pallas_call(
        pack_kernel,
        out_shape=jax.ShapeDtypeStruct((HKV, 192, 128), BF),
        in_specs=[vmem()] * 3,
        out_specs=vmem(),
        interpret=INTERPRET,
        name="pack",
    )(queries, fresh, cache)


def attention_kernel(info_ref, own_ref, pair_ref, keep_ref, send_ref, kv, sc, bias_c, bias_d):
    b = pl.program_id(0)
    length, core, x = info_ref[0], info_ref[1], info_ref[2]

    @pl.when(b == 0)
    def _():
        for t in range(NT):
            src = pair_ref.at[t // 2 % 4, t // 8 * 2 + t % 2]
            kv[t * 32 : t * 32 + 32, :] = src[0:32, :]
            kv[1024 + t * 64 : 1088 + t * 64, :] = src[32:96, :]
        bias_c[...] = jnp.where(iota((8, 1024), 1) < length, 0.0, NEG)
        query_at = x * 128 + iota((128, 512), 0)
        bias_d[...] = jnp.where(iota((128, 512), 1) <= query_at, 0.0, NEG)

    first = own_ref[pl.ds(b * 2, 2), 0:64, :].reshape(128, 128).astype(F32) * 0.125
    last = own_ref[pl.ds(b * 2, 2), 64:96, :].reshape(64, 128).astype(F32) * 0.125
    low = iota((128, 128), 1) < HD
    turned = pltpu.roll(last, HD, 1)
    third = jnp.concatenate([last[0:32], turned[0:32], last[32:64], turned[32:64]], 0)
    q = jnp.concatenate(
        [
            jnp.where(low, first, 0.0),
            jnp.where(low, pltpu.roll(first, HD, 1), 0.0),
            jnp.where(low, third, 0.0),
        ],
        0,
    ).astype(BF)

    def scores(k):
        keys = kv[pl.ds(pl.multiple_of(k * 512, 512), 512), :]
        return lax.dot_general(q, keys, (((1,), (1,)), ((), ())), preferred_element_type=F32)

    def fold(fn, top, s):
        for j in range(4):
            top = fn(top, s[:, j * 128 : j * 128 + 128])
        return top

    top = jnp.full((384, 128), NEG, F32)
    for k in range(2):
        s = scores(k) + bias_c[0:1, k * 512 : k * 512 + 512]
        sc[k] = s
        top = fold(jnp.maximum, top, s)
    s = scores(2 + b)
    s = s + jnp.concatenate([bias_d[...]] * 3, 0)
    sc[2 + b] = s
    top = fold(jnp.maximum, top, s)

    def middle(k, top):
        s = scores(k)
        sc[k] = s
        return fold(jnp.maximum, top, s)

    top = lax.fori_loop(2, 2 + b, middle, top)
    highest = jnp.max(top, 1, keepdims=True)

    def mix(k, carry):
        total, acc = carry
        p = jnp.exp(sc[k] - highest)
        values = kv[pl.ds(pl.multiple_of(k * 512, 512), 512), :]
        return fold(jnp.add, total, p), acc + dot(p.astype(BF), values)

    zero = jnp.zeros((384, 128), F32)
    total, acc = lax.fori_loop(0, 3 + b, mix, (zero, zero))
    out = acc / jnp.sum(total, 1, keepdims=True)
    a0, a1, a2 = out[0:128], out[128:256], out[256:384]
    tiles = (jnp.where(low, pltpu.roll(a0, HD, 1), a1), jnp.where(low, pltpu.roll(a2, HD, 1), 0.0))
    for n, tile in enumerate(tiles):
        even, odd = tile[0:64], tile[64:128]
        rows = slice(n * 64, n * 64 + 64)
        keep_ref[b, rows, :] = jnp.where(core == 0, even, odd).astype(BF)
        send_ref[b, rows, :] = jnp.where(core == 0, odd, even).astype(BF)


def attention(info, own, pairs):
    shape = jax.ShapeDtypeStruct((4, 128, 128), BF)
    return pl.pallas_call(
        attention_kernel,
        out_shape=(shape, shape),
        grid=(4,),
        in_specs=[pl.BlockSpec(memory_space=pltpu.SMEM), vmem(), vmem()],
        out_specs=(vmem(), vmem()),
        scratch_shapes=[
            pltpu.VMEM((3072, 128), BF),
            pltpu.VMEM((6, 384, 512), F32),
            pltpu.VMEM((8, 1024), F32),
            pltpu.VMEM((128, 512), F32),
        ],
        compiler_params=params(32),
        cost_estimate=pl.CostEstimate(
            flops=2 * 2 * 1536 * 2304 * 128, bytes_accessed=3 << 20, transcendentals=1536 * 2304
        ),
        interpret=INTERPRET,
        name="attention",
    )(info, own, pairs)


def group_sums_kernel(info_ref, own_ref, oth_ref, w_ref, o_ref):
    core = info_ref[1]
    total = jnp.zeros((256, D), F32)
    for src, side in ((own_ref, core), (oth_ref, 1 - core)):
        pair = src[:, 0:64, :].reshape(256, 128)
        last = src[:, 64:128, :].reshape(256, 128)[:, :HD]
        at = pl.multiple_of(side * 192, 64)
        total = total + dot(pair, w_ref[pl.ds(at, 128), :])
        total = total + dot(last, w_ref[pl.ds(pl.multiple_of(at + 128, 64), HD), :])
    o_ref[...] = total.astype(BF).reshape(4, TOK, D)


def group_sums(info, own, other, weight):
    return pl.pallas_call(
        group_sums_kernel,
        out_shape=jax.ShapeDtypeStruct((4, TOK, D), BF),
        in_specs=[pl.BlockSpec(memory_space=pltpu.SMEM)] + [vmem()] * 3,
        out_specs=vmem(),
        compiler_params=params(62.5),
        cost_estimate=pl.CostEstimate(flops=2 * 256 * 384 * D, bytes_accessed=2 << 20, transcendentals=0),
        interpret=INTERPRET,
        name="group_sums",
    )(info, own, other, weight)


def prepare_kernel(up_ref, down_ref, after_ref, o_ref):
    o_ref[0:64, 0:1024] = up_ref[0:64, :]
    o_ref[0:32, 1024:1536] = up_ref[64:96, 0:512]
    o_ref[32:64, 1024:1536] = up_ref[64:96, 512:1024]
    o_ref[64:96, :] = down_ref[...]


def prepare(up, down, after):
    return pl.pallas_call(
        prepare_kernel,
        out_shape=jax.ShapeDtypeStruct((96, D), BF),
        in_specs=[vmem()] * 2 + [pl.BlockSpec(memory_space=pl.ANY)],
        out_specs=vmem(),
        cost_estimate=pl.CostEstimate(flops=1 << 33, bytes_accessed=1 << 20, transcendentals=0),
        interpret=INTERPRET,
        name="prepare",
    )(up, down, after)


def norm_dispatch_kernel(sum_ref, hid_ref, gain_ref, ids_ref, res_ref, disp_ref):
    experts = iota((NT, TOK), 0)
    named = jnp.zeros((NT, TOK), F32)
    for k in range(TOPK):
        named = named + jnp.where(ids_ref[k : k + 1, :] == experts, 1.0, 0.0)
    before = jnp.where(iota((TOK, TOK), 0) < iota((TOK, TOK), 1), 1.0, 0.0).astype(BF)
    rank = dot(named.astype(BF), before)
    rank = jnp.where(named > 0.5, rank, -1.0).astype(BF)
    spread = jnp.where(iota((512, NT), 0) // SLOT == iota((512, NT), 1), 1.0, 0.0).astype(BF)
    ranks = dot(spread, rank)
    place = iota((512, TOK), 0) % SLOT
    pick = jnp.where(ranks == place.astype(F32), 1.0, 0.0).astype(BF)
    late = jnp.where(ranks == float(SLOT), 1.0, 0.0)

    total = hid_ref[...].astype(F32)
    for z in range(4):
        total = total + sum_ref[z].astype(F32)
    res_ref[...] = total
    meansq = jnp.mean(total * total, 1, keepdims=True)
    normed = (total * lax.rsqrt(meansq + EPS) * gain_ref[...]).astype(BF)
    extra = jnp.zeros((512, 128), F32)
    for c in range(CH):
        chunk = normed[:, c * 128 : c * 128 + 128]
        disp_ref[:, c * SLOT : (c + 1) * SLOT, :] = (
            dot(pick, chunk).astype(BF).reshape(NT, SLOT, 128)
        )
        extra = extra + dot(jnp.where(place == c, late, 0.0).astype(BF), chunk)
    disp_ref[:, SLOT * CH : SROWS, :] = extra.astype(BF).reshape(NT, 16, 128)


def norm_dispatch(sums, hidden, gain, ids_t):
    return pl.pallas_call(
        norm_dispatch_kernel,
        out_shape=(
            jax.ShapeDtypeStruct((TOK, D), F32),
            jax.ShapeDtypeStruct((NT, SROWS, 128), BF),
        ),
        in_specs=[vmem()] * 4,
        out_specs=(vmem(), vmem()),
        compiler_params=params(32),
        cost_estimate=pl.CostEstimate(flops=1 << 30, bytes_accessed=4 << 20, transcendentals=0),
        interpret=INTERPRET,
        name="norm_dispatch",
    )(sums, hidden, gain, ids_t)


def gather_extra(block):
    rows = iota((CH * NT, 512), 0)
    cols = iota((CH * NT, 512), 1)
    match = (rows % NT == cols // 16) & (rows // NT == cols % 16)
    stacked = dot(jnp.where(match, 1.0, 0.0).astype(BF), block).astype(BF)
    return [stacked[c * NT : (c + 1) * NT, :] for c in range(CH)]


def spread_extra(rows):
    place = iota((512, NT), 0)
    owner = place // 16 == iota((512, NT), 1)
    out = jnp.zeros((512, 128), F32)
    for c in range(CH):
        match = jnp.where(owner & (place % 16 == c), 1.0, 0.0).astype(BF)
        out = out + dot(match, rows[:, c * 128 : c * 128 + 128])
    return out.astype(BF)


def expert_kernel(info_ref, in_ref, wo_ref, wx_ref, o_ref, x, w1, w2, sems):
    zlo = info_ref[3]
    copies = []
    for d in range(2 * wo_ref.shape[0]):
        w_ref, block = (wo_ref, zlo) if d % 2 == 0 else (wx_ref, 1 - zlo)
        block = block + d // 2 * 2
        top = pl.multiple_of(block * 96, 32)
        pieces = (
            (w_ref.at[d // 2, 0:64, 0:1024], w1.at[pl.ds(top, 64), :]),
            (w_ref.at[d // 2, 0:32, 1024:1536], w1.at[pl.ds(top + 64, 32), 0:512]),
            (w_ref.at[d // 2, 32:64, 1024:1536], w1.at[pl.ds(top + 64, 32), 512:1024]),
            (w_ref.at[d // 2, 64:96, :], w2.at[pl.ds(pl.multiple_of(block * 32, 32), 32), :]),
        )
        for n, (src, dst) in enumerate(pieces):
            copies.append(pltpu.make_async_copy(src, dst, sems.at[d, n]))
    firsts = [copy for i, copy in enumerate(copies) if i % 4 < 3]
    lasts = copies[3::4]
    for copy in firsts + lasts:
        copy.start()
    for c in range(CH):
        x[0:512, c * 128 : c * 128 + 128] = in_ref[:, c * SLOT : (c + 1) * SLOT, :].reshape(512, 128)
    chunks = gather_extra(in_ref[:, SLOT * CH : SROWS, :].reshape(512, 128))
    for c in range(CH):
        x[512:544, c * 128 : c * 128 + 128] = chunks[c]
    for copy in firsts:
        copy.wait()
    hidden = dot(x[...], w1[...])
    gate = hidden[:, :FFE]
    active = (gate / (1.0 + jnp.exp(-gate)) * hidden[:, FFE:]).astype(BF)
    for copy in lasts:
        copy.wait()
    out = dot(active, w2[...]).astype(BF)
    for c in range(CH):
        o_ref[:, c * SLOT : (c + 1) * SLOT, :] = out[0:512, c * 128 : c * 128 + 128].reshape(
            NT, SLOT, 128
        )
    o_ref[:, SLOT * CH : SROWS, :] = spread_extra(out[512:544, :]).reshape(NT, 16, 128)


def expert(info, slots, own_weights, other_weights):
    blocks = 2 * own_weights.shape[0]
    return pl.pallas_call(
        expert_kernel,
        out_shape=jax.ShapeDtypeStruct((NT, SROWS, 128), BF),
        in_specs=[pl.BlockSpec(memory_space=pltpu.SMEM), vmem()]
        + [pl.BlockSpec(memory_space=pltpu.HBM)] * 2,
        out_specs=vmem(),
        scratch_shapes=[
            pltpu.VMEM((544, D), BF),
            pltpu.VMEM((blocks * 96, 2 * FFE), BF),
            pltpu.VMEM((blocks * 32, D), BF),
            pltpu.SemaphoreType.DMA((blocks, 4)),
        ],
        compiler_params=params(58),
        cost_estimate=pl.CostEstimate(
            flops=2 * 544 * 1536 * 1536, bytes_accessed=9 << 20, transcendentals=544 * 512
        ),
        interpret=INTERPRET,
        name="expert",
    )(info, slots, own_weights, other_weights)


def combine_kernel(in_ref, res_ref, ids_ref, gate_ref, o_ref):
    experts = iota((TOK, NT), 1)
    named = jnp.zeros((TOK, NT), F32)
    gates = jnp.zeros((TOK, NT), F32)
    for k in range(TOPK):
        match = ids_ref[:, k : k + 1] == experts
        named = named + jnp.where(match, 1.0, 0.0)
        gates = gates + jnp.where(match, gate_ref[:, k : k + 1], 0.0)
    before = jnp.where(iota((TOK, TOK), 1) < iota((TOK, TOK), 0), 1.0, 0.0).astype(BF)
    rank = dot(before, named.astype(BF))
    rank = jnp.where(named > 0.5, rank, -1.0)
    spread = jnp.where(iota((NT, 512), 0) == iota((NT, 512), 1) // SLOT, 1.0, 0.0).astype(BF)
    place = (iota((TOK, 512), 1) % SLOT).astype(F32)
    pick = dot(rank.astype(BF), spread) == place
    high = gates.astype(BF)
    low = (gates - high.astype(F32)).astype(BF)
    weights = jnp.concatenate(
        [jnp.where(pick, dot(part, spread), 0.0).astype(BF) for part in (high, low)], 0
    )
    late = rank == float(SLOT)
    late_weights = jnp.concatenate(
        [jnp.where(late, part.astype(F32), 0.0).astype(BF) for part in (high, low)], 0
    )
    chunks = gather_extra(in_ref[:, SLOT * CH : SROWS, :].reshape(512, 128))
    for c in range(CH):
        main = in_ref[:, c * SLOT : (c + 1) * SLOT, :].reshape(512, 128)
        both = dot(weights, main) + dot(late_weights, chunks[c])
        cols = slice(c * 128, c * 128 + 128)
        o_ref[:, cols] = (res_ref[:, cols] + (both[:TOK] + both[TOK:])).astype(BF)


def combine(returned, residual, ids, gates):
    return pl.pallas_call(
        combine_kernel,
        out_shape=jax.ShapeDtypeStruct((TOK, D), BF),
        in_specs=[vmem()] * 4,
        out_specs=vmem(),
        compiler_params=params(32),
        interpret=INTERPRET,
        name="combine",
    )(returned, residual, ids, gates)


def shards(
    hidden_in,
    rotated_queries,
    fresh_key_values,
    cached_key_values,
    cached_len,
    expert_ids,
    route_gates,
    output_weight,
    norm_gain,
    gate_up,
    down_weight,
):
    zlo = lax.axis_index("zlo").astype(jnp.int32)
    x = lax.axis_index("x").astype(jnp.int32)
    core = lax.axis_index("core").astype(jnp.int32)
    length = cached_len[0]
    info = jnp.stack([length, core, x, zlo])
    ids = expert_ids[0, 0, 0]
    gates = route_gates[0, 0, 0]

    plane_weight = lax.all_gather(output_weight, ("x", "core"), axis=0, tiled=True)
    send = pack(rotated_queries[0, 0, 0], fresh_key_values[0, 0, 0], cached_key_values[0])
    own = lax.all_to_all(send, ("zhi", "core"), split_axis=0, concat_axis=0, tiled=True)
    packed = prepare(gate_up[0], down_weight[0], own)
    own_weights = lax.all_gather(packed, "y", axis=0)
    across = lax.ppermute(packed, "zlo", [(0, 1), (1, 0)])
    spread = jnp.broadcast_to(own[None, :, 96:], (4, HKV, 96, 128))
    pairs = lax.all_to_all(spread, "x", split_axis=0, concat_axis=0, tiled=True)
    kept, sent = attention(info, own, pairs)
    across, sent = lax.optimization_barrier((across, sent))
    other_weights = lax.all_gather(across, "y", axis=0)
    swapped = lax.ppermute(sent, "core", [(0, 1), (1, 0)])
    terms = group_sums(info, kept, swapped, plane_weight)
    sums = lax.all_to_all(terms, "zhi", split_axis=0, concat_axis=0, tiled=True)
    residual, outbound = norm_dispatch(sums, hidden_in[0, 0, 0], norm_gain[None], ids.T)
    slots = lax.all_to_all(outbound, TEN, split_axis=0, concat_axis=0, tiled=True)
    computed = expert(info, slots, own_weights, other_weights)
    returned = lax.all_to_all(computed, TEN, split_axis=0, concat_axis=0, tiled=True)
    hidden_out = combine(returned, residual, ids, gates)

    low_x = x % 2
    mine = lax.dynamic_slice_in_dim(pairs, (low_x * 2 + core) * 32, 32, 3)
    for_other = lax.dynamic_slice_in_dim(pairs, (low_x * 2 + 1 - core) * 32, 32, 3)
    theirs = lax.ppermute(for_other, "core", [(0, 1), (1, 0)])
    chosen = jnp.where(core == x // 2, mine, theirs).reshape(4, 4, 2, 96, 32)
    chosen = jnp.transpose(chosen, (1, 0, 2, 3, 4)).reshape(NT, 96, 32)
    old_rows = chosen[:, :CROWS].reshape(NT * CROWS, 32)
    new_rows = chosen[:, CROWS:].reshape(NT * TOK, 32)
    total = NT * CROWS + NT * TOK
    base = jnp.concatenate([old_rows, jnp.zeros((NT * TOK, 32), BF)], 0)
    base = jnp.where((jnp.arange(total, dtype=jnp.int32) < length)[:, None], base, jnp.zeros_like(base))
    cache_out = lax.dynamic_update_slice_in_dim(base, new_rows, length, 0)
    return hidden_out.reshape(1, 1, 1, TOK, D), cache_out[None]


def solution(mesh):
    dp, tensor = mesh.devices.shape
    fine = Mesh(mesh.devices.reshape(dp // 2, 2, 4, 4, 2), ("y", "zlo", "zhi", "x", "core"))
    ydp = ("y", "zlo")
    return jax.shard_map(
        shards,
        mesh=fine,
        in_specs=(
            P(ydp, TEN, None, None, None),
            P(ydp, TEN, None, None, None),
            P(ydp, TEN, None, None, None),
            P(ydp, TEN, None),
            P(ydp),
            P(ydp, TEN, None, None, None),
            P(ydp, TEN, None, None, None),
            P(TEN, None),
            P(),
            P(TEN, ydp, None),
            P(TEN, ydp, None),
        ),
        out_specs=(P(ydp, TEN, None, None, None), P(ydp, None, TEN)),
        check_vma=False,
    )
```

```python
import functools
import math

import jax
import jax.numpy as jnp
from jax import lax
from jax.experimental import pallas as pl
from jax.experimental.pallas import tpu as pltpu
from jax.sharding import Mesh
from jax.sharding import PartitionSpec as P

D = 1536
HQ = 24
HKV = 8
HD = 64
FFE = 512
TOPK = 8
EPS = 1e-05
NT = 32
TOK = 64
CROWS = 32
SLOT = 16
CH = D // 128
SROWS = SLOT * CH + 16
BF = jnp.bfloat16
F32 = jnp.float32
TEN = ("zhi", "x", "core")
NEG = -1e30
INTERPRET = False


def vmem():
    return pl.BlockSpec(memory_space=pltpu.VMEM)


def params(mib):
    return pltpu.CompilerParams(vmem_limit_bytes=int(mib * (1 << 20)))


def dot(a, b):
    return lax.dot_general(a, b, (((1,), (0,)), ((), ())), preferred_element_type=F32)


def iota(shape, dim):
    return lax.broadcasted_iota(jnp.int32, shape, dim)


def pack_kernel(q_ref, f_ref, c_ref, o_ref):
    for g in range(HKV):
        cols = pl.ds(g * 128, 128)
        rows = q_ref[:, g * 192 : g * 192 + 192]
        o_ref[g, 0:64, :] = rows[:, :128]
        o_ref[g, 64:96, :] = jnp.concatenate([rows[0:32, 128:], rows[32:64, 128:]], 1)
        o_ref[g, 96:128, :] = c_ref[:, cols]
        o_ref[g, 128:192, :] = f_ref[:, cols]


def pack(queries, fresh, cache):
    return pl.pallas_call(
        pack_kernel,
        out_shape=jax.ShapeDtypeStruct((HKV, 192, 128), BF),
        in_specs=[vmem()] * 3,
        out_specs=vmem(),
        interpret=INTERPRET,
        name="pack",
    )(queries, fresh, cache)


def attention_kernel(info_ref, own_ref, pair_ref, keep_ref, send_ref, kv, sc, bias_c, bias_d):
    b = pl.program_id(0)
    length, core, x = info_ref[0], info_ref[1], info_ref[2]

    @pl.when(b == 0)
    def _():
        for t in range(NT):
            src = pair_ref.at[t // 2 % 4, t // 8 * 2 + t % 2]
            kv[t * 32 : t * 32 + 32, :] = src[0:32, :]
            kv[1024 + t * 64 : 1088 + t * 64, :] = src[32:96, :]
        bias_c[...] = jnp.where(iota((8, 1024), 1) < length, 0.0, NEG)
        query_at = x * 128 + iota((128, 512), 0)
        bias_d[...] = jnp.where(iota((128, 512), 1) <= query_at, 0.0, NEG)

    first = own_ref[pl.ds(b * 2, 2), 0:64, :].reshape(128, 128).astype(F32) * 0.125
    last = own_ref[pl.ds(b * 2, 2), 64:96, :].reshape(64, 128).astype(F32) * 0.125
    low = iota((128, 128), 1) < HD
    turned = pltpu.roll(last, HD, 1)
    third = jnp.concatenate([last[0:32], turned[0:32], last[32:64], turned[32:64]], 0)
    q = jnp.concatenate(
        [
            jnp.where(low, first, 0.0),
            jnp.where(low, pltpu.roll(first, HD, 1), 0.0),
            jnp.where(low, third, 0.0),
        ],
        0,
    ).astype(BF)

    def scores(k):
        keys = kv[pl.ds(pl.multiple_of(k * 512, 512), 512), :]
        return lax.dot_general(q, keys, (((1,), (1,)), ((), ())), preferred_element_type=F32)

    def fold(fn, top, s):
        for j in range(4):
            top = fn(top, s[:, j * 128 : j * 128 + 128])
        return top

    top = jnp.full((384, 128), NEG, F32)
    for k in range(2):
        s = scores(k) + bias_c[0:1, k * 512 : k * 512 + 512]
        sc[k] = s
        top = fold(jnp.maximum, top, s)
    s = scores(2 + b)
    s = s + jnp.concatenate([bias_d[...]] * 3, 0)
    sc[2 + b] = s
    top = fold(jnp.maximum, top, s)

    def middle(k, top):
        s = scores(k)
        sc[k] = s
        return fold(jnp.maximum, top, s)

    top = lax.fori_loop(2, 2 + b, middle, top)
    highest = jnp.max(top, 1, keepdims=True)

    def mix(k, carry):
        total, acc = carry
        p = jnp.exp(sc[k] - highest)
        values = kv[pl.ds(pl.multiple_of(k * 512, 512), 512), :]
        return fold(jnp.add, total, p), acc + dot(p.astype(BF), values)

    zero = jnp.zeros((384, 128), F32)
    total, acc = lax.fori_loop(0, 3 + b, mix, (zero, zero))
    out = acc / jnp.sum(total, 1, keepdims=True)
    a0, a1, a2 = out[0:128], out[128:256], out[256:384]
    tiles = (jnp.where(low, pltpu.roll(a0, HD, 1), a1), jnp.where(low, pltpu.roll(a2, HD, 1), 0.0))
    for n, tile in enumerate(tiles):
        even, odd = tile[0:64], tile[64:128]
        rows = slice(n * 64, n * 64 + 64)
        keep_ref[b, rows, :] = jnp.where(core == 0, even, odd).astype(BF)
        send_ref[b, rows, :] = jnp.where(core == 0, odd, even).astype(BF)


def attention(info, own, pairs):
    shape = jax.ShapeDtypeStruct((4, 128, 128), BF)
    return pl.pallas_call(
        attention_kernel,
        out_shape=(shape, shape),
        grid=(4,),
        in_specs=[pl.BlockSpec(memory_space=pltpu.SMEM), vmem(), vmem()],
        out_specs=(vmem(), vmem()),
        scratch_shapes=[
            pltpu.VMEM((3072, 128), BF),
            pltpu.VMEM((6, 384, 512), F32),
            pltpu.VMEM((8, 1024), F32),
            pltpu.VMEM((128, 512), F32),
        ],
        compiler_params=params(32),
        cost_estimate=pl.CostEstimate(
            flops=2 * 2 * 1536 * 2304 * 128, bytes_accessed=3 << 20, transcendentals=1536 * 2304
        ),
        interpret=INTERPRET,
        name="attention",
    )(info, own, pairs)


def group_sums_kernel(info_ref, own_ref, oth_ref, wo_ref, wx_ref, o_ref, w, o, sems, out_sems):
    core, x = info_ref[1], info_ref[2]
    copies = []
    for at in range(4):
        turn = (x + 4 - at) % 4
        for n, (src, side) in enumerate(((wo_ref, core), (wx_ref, 1 - core))):
            row = pl.multiple_of((2 * at + side) * 48, 16)
            copies.append(pltpu.make_async_copy(src.at[turn], w.at[pl.ds(row, 48), :], sems.at[at, n]))
            copies[-1].start()
    sides = ((own_ref, core), (oth_ref, 1 - core))
    pairs = [src[:, 0:64, :].reshape(256, 128) for src, _ in sides]
    lasts = [src[:, 64:128, :].reshape(256, 128)[:, :HD] for src, _ in sides]
    for copy in copies:
        copy.wait()
    sent = []
    for n in range(3):
        cols = pl.ds(n * 512, 512)
        total = jnp.zeros((256, 512), F32)
        for pair, last, (_, side) in zip(pairs, lasts, sides):
            at = pl.multiple_of(side * 192, 64)
            total = total + dot(pair, w[pl.ds(at, 128), cols])
            total = total + dot(last, w[pl.ds(pl.multiple_of(at + 128, 64), HD), cols])
        o[:, :, cols] = total.astype(BF).reshape(4, TOK, 512)
        sent.append(pltpu.make_async_copy(o.at[:, :, cols], o_ref.at[:, :, cols], out_sems.at[n]))
        sent[-1].start()
    for copy in sent:
        copy.wait()


def group_sums(info, own, other, own_weight, other_weight):
    anywhere = pl.BlockSpec(memory_space=pl.ANY)
    return pl.pallas_call(
        group_sums_kernel,
        out_shape=jax.ShapeDtypeStruct((4, TOK, D), BF),
        in_specs=[pl.BlockSpec(memory_space=pltpu.SMEM), vmem(), vmem(), anywhere, anywhere],
        out_specs=pl.BlockSpec(memory_space=pltpu.HBM),
        scratch_shapes=[
            pltpu.VMEM((384, D), BF),
            pltpu.VMEM((4, TOK, D), BF),
            pltpu.SemaphoreType.DMA((4, 2)),
            pltpu.SemaphoreType.DMA((3,)),
        ],
        compiler_params=params(20),
        cost_estimate=pl.CostEstimate(flops=2 * 256 * 384 * D, bytes_accessed=2 << 20, transcendentals=0),
        interpret=INTERPRET,
        name="group_sums",
    )(info, own, other, own_weight, other_weight)


def prepare_kernel(up_ref, down_ref, shard_ref, after_ref, o_ref, so_ref):
    o_ref[0:64, 0:1024] = up_ref[0:64, :]
    o_ref[0:32, 1024:1536] = up_ref[64:96, 0:512]
    o_ref[32:64, 1024:1536] = up_ref[64:96, 512:1024]
    o_ref[64:96, :] = down_ref[...]
    so_ref[...] = shard_ref[...]


def prepare(up, down, shard, after):
    return pl.pallas_call(
        prepare_kernel,
        out_shape=(jax.ShapeDtypeStruct((96, D), BF), jax.ShapeDtypeStruct(shard.shape, BF)),
        in_specs=[vmem()] * 3 + [pl.BlockSpec(memory_space=pl.ANY)],
        out_specs=(vmem(), vmem()),
        cost_estimate=pl.CostEstimate(flops=1 << 33, bytes_accessed=1 << 20, transcendentals=0),
        interpret=INTERPRET,
        name="prepare",
    )(up, down, shard, after)


def norm_dispatch_kernel(sum_ref, hid_ref, gain_ref, ids_ref, res_ref, disp_ref):
    experts = iota((NT, TOK), 0)
    named = jnp.zeros((NT, TOK), F32)
    for k in range(TOPK):
        named = named + jnp.where(ids_ref[k : k + 1, :] == experts, 1.0, 0.0)
    before = jnp.where(iota((TOK, TOK), 0) < iota((TOK, TOK), 1), 1.0, 0.0).astype(BF)
    rank = dot(named.astype(BF), before)
    rank = jnp.where(named > 0.5, rank, -1.0).astype(BF)
    spread = jnp.where(iota((512, NT), 0) // SLOT == iota((512, NT), 1), 1.0, 0.0).astype(BF)
    ranks = dot(spread, rank)
    place = iota((512, TOK), 0) % SLOT
    pick = jnp.where(ranks == place.astype(F32), 1.0, 0.0).astype(BF)
    late = jnp.where(ranks == float(SLOT), 1.0, 0.0)

    total = hid_ref[...].astype(F32)
    for z in range(4):
        total = total + sum_ref[z].astype(F32)
    res_ref[...] = total
    meansq = jnp.mean(total * total, 1, keepdims=True)
    normed = (total * lax.rsqrt(meansq + EPS) * gain_ref[...]).astype(BF)
    extra = jnp.zeros((512, 128), F32)
    for c in range(CH):
        chunk = normed[:, c * 128 : c * 128 + 128]
        disp_ref[:, c * SLOT : (c + 1) * SLOT, :] = (
            dot(pick, chunk).astype(BF).reshape(NT, SLOT, 128)
        )
        extra = extra + dot(jnp.where(place == c, late, 0.0).astype(BF), chunk)
    disp_ref[:, SLOT * CH : SROWS, :] = extra.astype(BF).reshape(NT, 16, 128)


def norm_dispatch(sums, hidden, gain, ids_t):
    return pl.pallas_call(
        norm_dispatch_kernel,
        out_shape=(
            jax.ShapeDtypeStruct((TOK, D), F32),
            jax.ShapeDtypeStruct((NT, SROWS, 128), BF),
        ),
        in_specs=[vmem()] * 4,
        out_specs=(vmem(), vmem()),
        compiler_params=params(32),
        cost_estimate=pl.CostEstimate(flops=1 << 30, bytes_accessed=4 << 20, transcendentals=0),
        interpret=INTERPRET,
        name="norm_dispatch",
    )(sums, hidden, gain, ids_t)


def gather_extra(block):
    rows = iota((CH * NT, 512), 0)
    cols = iota((CH * NT, 512), 1)
    match = (rows % NT == cols // 16) & (rows // NT == cols % 16)
    stacked = dot(jnp.where(match, 1.0, 0.0).astype(BF), block).astype(BF)
    return [stacked[c * NT : (c + 1) * NT, :] for c in range(CH)]


def expert_kernel(info_ref, in_ref, wo_ref, wx_ref, o_ref, x, w1, w2, o, sems, out_sems):
    zlo = info_ref[3]
    copies = []
    for d in range(2 * wo_ref.shape[0]):
        w_ref, block = (wo_ref, zlo) if d % 2 == 0 else (wx_ref, 1 - zlo)
        block = block + d // 2 * 2
        top = pl.multiple_of(block * 96, 32)
        pieces = (
            (w_ref.at[d // 2, 0:64, 0:1024], w1.at[pl.ds(top, 64), :]),
            (w_ref.at[d // 2, 0:32, 1024:1536], w1.at[pl.ds(top + 64, 32), 0:512]),
            (w_ref.at[d // 2, 32:64, 1024:1536], w1.at[pl.ds(top + 64, 32), 512:1024]),
            (w_ref.at[d // 2, 64:96, :], w2.at[pl.ds(pl.multiple_of(block * 32, 32), 32), :]),
        )
        for n, (src, dst) in enumerate(pieces):
            copies.append(pltpu.make_async_copy(src, dst, sems.at[d, n]))
    firsts = [copy for i, copy in enumerate(copies) if i % 4 < 3]
    lasts = copies[3::4]
    for copy in firsts + lasts:
        copy.start()
    depth = w1.shape[0] // 4
    for c in range(CH):
        x[0:512, c * 128 : c * 128 + 128] = in_ref[:, c * SLOT : (c + 1) * SLOT, :].reshape(512, 128)
    chunks = gather_extra(in_ref[:, SLOT * CH : SROWS, :].reshape(512, 128))
    for c in range(CH):
        x[512:544, c * 128 : c * 128 + 128] = chunks[c]
    hidden = jnp.zeros((544, 2 * FFE), F32)
    for n in range(4):
        for copy in firsts[n * len(firsts) // 4 : (n + 1) * len(firsts) // 4]:
            copy.wait()
        at = n * depth
        hidden = hidden + dot(x[:, at : at + depth], w1[at : at + depth, :])
    gate = hidden[:, :FFE]
    active = (gate / (1.0 + jnp.exp(-gate)) * hidden[:, FFE:]).astype(BF)
    for copy in lasts:
        copy.wait()
    place = iota((512, NT), 0)
    owner = place // 16 == iota((512, NT), 1)
    extra = jnp.zeros((512, 128), F32)
    sent = []
    for c in range(0, CH, 2):
        out = dot(active, w2[:, c * 128 : c * 128 + 256]).astype(BF)
        for n in range(2):
            cols = slice(n * 128, n * 128 + 128)
            o[:, (c + n) * SLOT : (c + n + 1) * SLOT, :] = out[0:512, cols].reshape(NT, SLOT, 128)
            match = jnp.where(owner & (place % 16 == c + n), 1.0, 0.0).astype(BF)
            extra = extra + dot(match, out[512:544, cols])
        rows = pl.ds(c * SLOT, 2 * SLOT)
        sent.append(pltpu.make_async_copy(o.at[:, rows, :], o_ref.at[:, rows, :], out_sems.at[c // 2]))
        sent[-1].start()
    o[:, SLOT * CH : SROWS, :] = extra.astype(BF).reshape(NT, 16, 128)
    rows = pl.ds(CH * SLOT, 16)
    sent.append(pltpu.make_async_copy(o.at[:, rows, :], o_ref.at[:, rows, :], out_sems.at[CH // 2]))
    sent[-1].start()
    for copy in sent:
        copy.wait()


def expert(info, slots, own_weights, other_weights):
    blocks = 2 * own_weights.shape[0]
    return pl.pallas_call(
        expert_kernel,
        out_shape=jax.ShapeDtypeStruct((NT, SROWS, 128), BF),
        in_specs=[pl.BlockSpec(memory_space=pltpu.SMEM), vmem()]
        + [pl.BlockSpec(memory_space=pltpu.HBM)] * 2,
        out_specs=pl.BlockSpec(memory_space=pltpu.HBM),
        scratch_shapes=[
            pltpu.VMEM((544, D), BF),
            pltpu.VMEM((blocks * 96, 2 * FFE), BF),
            pltpu.VMEM((blocks * 32, D), BF),
            pltpu.VMEM((NT, SROWS, 128), BF),
            pltpu.SemaphoreType.DMA((blocks, 4)),
            pltpu.SemaphoreType.DMA((CH // 2 + 1,)),
        ],
        compiler_params=params(58),
        cost_estimate=pl.CostEstimate(
            flops=2 * 544 * 1536 * 1536, bytes_accessed=9 << 20, transcendentals=544 * 512
        ),
        interpret=INTERPRET,
        name="expert",
    )(info, slots, own_weights, other_weights)


def combine_kernel(in_ref, res_ref, ids_ref, gate_ref, o_ref):
    experts = iota((TOK, NT), 1)
    named = jnp.zeros((TOK, NT), F32)
    gates = jnp.zeros((TOK, NT), F32)
    for k in range(TOPK):
        match = ids_ref[:, k : k + 1] == experts
        named = named + jnp.where(match, 1.0, 0.0)
        gates = gates + jnp.where(match, gate_ref[:, k : k + 1], 0.0)
    before = jnp.where(iota((TOK, TOK), 1) < iota((TOK, TOK), 0), 1.0, 0.0).astype(BF)
    rank = dot(before, named.astype(BF))
    rank = jnp.where(named > 0.5, rank, -1.0)
    spread = jnp.where(iota((NT, 512), 0) == iota((NT, 512), 1) // SLOT, 1.0, 0.0).astype(BF)
    place = (iota((TOK, 512), 1) % SLOT).astype(F32)
    pick = dot(rank.astype(BF), spread) == place
    high = gates.astype(BF)
    low = (gates - high.astype(F32)).astype(BF)
    weights = jnp.concatenate(
        [jnp.where(pick, dot(part, spread), 0.0).astype(BF) for part in (high, low)], 0
    )
    late = rank == float(SLOT)
    late_weights = jnp.concatenate(
        [jnp.where(late, part.astype(F32), 0.0).astype(BF) for part in (high, low)], 0
    )
    chunks = gather_extra(in_ref[:, SLOT * CH : SROWS, :].reshape(512, 128))
    for c in range(CH):
        main = in_ref[:, c * SLOT : (c + 1) * SLOT, :].reshape(512, 128)
        both = dot(weights, main) + dot(late_weights, chunks[c])
        cols = slice(c * 128, c * 128 + 128)
        o_ref[:, cols] = (res_ref[:, cols] + (both[:TOK] + both[TOK:])).astype(BF)


def combine(returned, residual, ids, gates):
    return pl.pallas_call(
        combine_kernel,
        out_shape=jax.ShapeDtypeStruct((TOK, D), BF),
        in_specs=[vmem()] * 4,
        out_specs=vmem(),
        compiler_params=params(32),
        interpret=INTERPRET,
        name="combine",
    )(returned, residual, ids, gates)


def shards(
    hidden_in,
    rotated_queries,
    fresh_key_values,
    cached_key_values,
    cached_len,
    expert_ids,
    route_gates,
    output_weight,
    norm_gain,
    gate_up,
    down_weight,
):
    zlo = lax.axis_index("zlo").astype(jnp.int32)
    x = lax.axis_index("x").astype(jnp.int32)
    core = lax.axis_index("core").astype(jnp.int32)
    length = cached_len[0]
    info = jnp.stack([length, core, x, zlo])
    ids = expert_ids[0, 0, 0]
    gates = route_gates[0, 0, 0]

    send = pack(rotated_queries[0, 0, 0], fresh_key_values[0, 0, 0], cached_key_values[0])
    packed, shard = prepare(gate_up[0], down_weight[0], output_weight, send)
    own_weights = lax.all_gather(packed, "y", axis=0)
    turns = [
        lax.ppermute(shard, "x", [(n, (n + step) % 4) for n in range(4)]) for step in (1, 2, 3)
    ]
    own = lax.all_to_all(send, ("zhi", "core"), split_axis=0, concat_axis=0, tiled=True)
    turns, packed, own = lax.optimization_barrier((turns, packed, own))
    across = lax.ppermute(packed, "zlo", [(0, 1), (1, 0)])
    own_rows = jnp.stack([shard, *turns], 0)
    other_rows = lax.ppermute(own_rows, "core", [(0, 1), (1, 0)])
    spread = jnp.broadcast_to(own[None, :, 96:], (4, HKV, 96, 128))
    pairs = lax.all_to_all(spread, "x", split_axis=0, concat_axis=0, tiled=True)
    kept, sent = attention(info, own, pairs)
    across, other_rows, sent = lax.optimization_barrier((across, other_rows, sent))
    other_weights = lax.all_gather(across, "y", axis=0)
    swapped = lax.ppermute(sent, "core", [(0, 1), (1, 0)])
    terms = group_sums(info, kept, swapped, own_rows, other_rows)
    sums = lax.all_to_all(terms, "zhi", split_axis=0, concat_axis=0, tiled=True)
    residual, outbound = norm_dispatch(sums, hidden_in[0, 0, 0], norm_gain[None], ids.T)
    slots = lax.all_to_all(outbound, TEN, split_axis=0, concat_axis=0, tiled=True)
    computed = expert(info, slots, own_weights, other_weights)
    returned = lax.all_to_all(computed, TEN, split_axis=0, concat_axis=0, tiled=True)
    hidden_out = combine(returned, residual, ids, gates)

    low_x = x % 2
    mine = lax.dynamic_slice_in_dim(pairs, (low_x * 2 + core) * 32, 32, 3)
    for_other = lax.dynamic_slice_in_dim(pairs, (low_x * 2 + 1 - core) * 32, 32, 3)
    theirs = lax.ppermute(for_other, "core", [(0, 1), (1, 0)])
    chosen = jnp.where(core == x // 2, mine, theirs).reshape(4, 4, 2, 96, 32)
    chosen = jnp.transpose(chosen, (1, 0, 2, 3, 4)).reshape(NT, 96, 32)
    old_rows = chosen[:, :CROWS].reshape(NT * CROWS, 32)
    new_rows = chosen[:, CROWS:].reshape(NT * TOK, 32)
    total = NT * CROWS + NT * TOK
    base = jnp.concatenate([old_rows, jnp.zeros((NT * TOK, 32), BF)], 0)
    base = jnp.where((jnp.arange(total, dtype=jnp.int32) < length)[:, None], base, jnp.zeros_like(base))
    cache_out = lax.dynamic_update_slice_in_dim(base, new_rows, length, 0)
    return hidden_out.reshape(1, 1, 1, TOK, D), cache_out[None]


def solution(mesh):
    dp, tensor = mesh.devices.shape
    fine = Mesh(mesh.devices.reshape(dp // 2, 2, 4, 4, 2), ("y", "zlo", "zhi", "x", "core"))
    ydp = ("y", "zlo")
    return jax.shard_map(
        shards,
        mesh=fine,
        in_specs=(
            P(ydp, TEN, None, None, None),
            P(ydp, TEN, None, None, None),
            P(ydp, TEN, None, None, None),
            P(ydp, TEN, None),
            P(ydp),
            P(ydp, TEN, None, None, None),
            P(ydp, TEN, None, None, None),
            P(TEN, None),
            P(),
            P(TEN, ydp, None),
            P(TEN, ydp, None),
        ),
        out_specs=(P(ydp, TEN, None, None, None), P(ydp, None, TEN)),
        check_vma=False,
    )
```

```python
import functools
import math

import jax
import jax.numpy as jnp
from jax import lax
from jax.experimental import pallas as pl
from jax.experimental.pallas import tpu as pltpu
from jax.sharding import Mesh
from jax.sharding import PartitionSpec as P

D = 1536
HQ = 24
HKV = 8
HD = 64
FFE = 512
TOPK = 8
EPS = 1e-05
NT = 32
TOK = 64
CROWS = 32
SLOT = 16
CH = D // 128
SROWS = SLOT * CH + 16
BF = jnp.bfloat16
F32 = jnp.float32
TEN = ("zhi", "x", "core")
NEG = -1e30
INTERPRET = False


def vmem():
    return pl.BlockSpec(memory_space=pltpu.VMEM)


def params(mib):
    return pltpu.CompilerParams(vmem_limit_bytes=int(mib * (1 << 20)))


def dot(a, b):
    return lax.dot_general(a, b, (((1,), (0,)), ((), ())), preferred_element_type=F32)


def iota(shape, dim):
    return lax.broadcasted_iota(jnp.int32, shape, dim)


def pack_kernel(q_ref, f_ref, c_ref, o_ref):
    for g in range(HKV):
        cols = pl.ds(g * 128, 128)
        rows = q_ref[:, g * 192 : g * 192 + 192]
        o_ref[g, 0:64, :] = rows[:, :128]
        o_ref[g, 64:96, :] = jnp.concatenate([rows[0:32, 128:], rows[32:64, 128:]], 1)
        o_ref[g, 96:128, :] = c_ref[:, cols]
        o_ref[g, 128:192, :] = f_ref[:, cols]


def pack(queries, fresh, cache):
    return pl.pallas_call(
        pack_kernel,
        out_shape=jax.ShapeDtypeStruct((HKV, 192, 128), BF),
        in_specs=[vmem()] * 3,
        out_specs=vmem(),
        interpret=INTERPRET,
        name="pack",
    )(queries, fresh, cache)


def attention_kernel(info_ref, own_ref, pair_ref, keep_ref, send_ref, kv, vals, keys, sc, probs, bias_c, bias_d):
    b = pl.program_id(0)
    length, core, x = info_ref[0], info_ref[1], info_ref[2]

    @pl.when(b == 0)
    def _():
        for t in range(NT):
            src = pair_ref.at[t // 2 % 4, t // 8 * 2 + t % 2]
            kv[t * 32 : t * 32 + 32, :] = src[0:32, :]
            kv[1024 + t * 64 : 1088 + t * 64, :] = src[32:96, :]
        for t in range(6):
            some = kv[t * 512 : t * 512 + 512, :].astype(F32)
            vals[t * 512 : t * 512 + 512, :] = jnp.where(iota((512, 128), 1) < HD, 1.0, some).astype(BF)
            keys[:, t * 512 : t * 512 + 512] = some.T.astype(BF)
        bias_c[...] = jnp.where(iota((8, 1024), 1) < length, 0.0, NEG)
        query_at = x * 128 + iota((128, 512), 0)
        bias_d[...] = jnp.where(iota((128, 512), 1) <= query_at, 0.0, NEG)

    low = iota((128, 128), 1) < HD

    def block(b):
        first = own_ref[b * 2 : b * 2 + 2, 0:64, :].reshape(128, 128).astype(F32) * 0.125
        last = own_ref[b * 2 : b * 2 + 2, 64:96, :].reshape(64, 128).astype(F32) * 0.125
        turned = pltpu.roll(last, HD, 1)
        third = jnp.concatenate([last[0:32], turned[0:32], last[32:64], turned[32:64]], 0)
        heads = (first, pltpu.roll(first, HD, 1), third)
        q = jnp.concatenate([jnp.where(low, head, 0.0) for head in heads], 0).astype(BF)
        count = 3 + b
        top = jnp.full((384, 128), NEG, F32)
        for k in range(count):
            at = k * 512
            s = dot(q, keys[:, at : at + 512])
            if k < 2:
                s = s + bias_c[0:1, at : at + 512]
            elif k == count - 1:
                s = s + jnp.concatenate([bias_d[...]] * 3, 0)
            sc[k] = s
            for j in range(4):
                top = jnp.maximum(top, s[:, j * 128 : j * 128 + 128])
        highest = jnp.max(top, 1, keepdims=True)
        accs = []
        for h in range(3):
            rows = slice(h * 128, h * 128 + 128)
            for k in range(count):
                part = jnp.exp(sc[k, rows, :] - highest[rows])
                probs[rows, k * 512 : k * 512 + 512] = part.astype(BF)
            accs.append(dot(probs[rows, : count * 512], vals[: count * 512, :]))
        acc = jnp.concatenate(accs, 0)
        out = acc / pltpu.roll(acc, HD, 1)
        a0, a1, a2 = out[0:128], out[128:256], out[256:384]
        tiles = (
            jnp.where(low, pltpu.roll(a0, HD, 1), a1),
            jnp.where(low, pltpu.roll(a2, HD, 1), 0.0),
        )
        for n, tile in enumerate(tiles):
            even, odd = tile[0:64], tile[64:128]
            rows = slice(n * 64, n * 64 + 64)
            keep_ref[b, rows, :] = jnp.where(core == 0, even, odd).astype(BF)
            send_ref[b, rows, :] = jnp.where(core == 0, odd, even).astype(BF)

    for n in range(4):
        pl.when(b == n)(functools.partial(block, n))


def attention(info, own, pairs):
    shape = jax.ShapeDtypeStruct((4, 128, 128), BF)
    return pl.pallas_call(
        attention_kernel,
        out_shape=(shape, shape),
        grid=(4,),
        in_specs=[pl.BlockSpec(memory_space=pltpu.SMEM), vmem(), vmem()],
        out_specs=(vmem(), vmem()),
        scratch_shapes=[
            pltpu.VMEM((3072, 128), BF),
            pltpu.VMEM((3072, 128), BF),
            pltpu.VMEM((128, 3072), BF),
            pltpu.VMEM((6, 384, 512), F32),
            pltpu.VMEM((384, 3072), BF),
            pltpu.VMEM((8, 1024), F32),
            pltpu.VMEM((128, 512), F32),
        ],
        compiler_params=params(32),
        cost_estimate=pl.CostEstimate(
            flops=2 * 2 * 1536 * 2304 * 128, bytes_accessed=3 << 20, transcendentals=1536 * 2304
        ),
        interpret=INTERPRET,
        name="attention",
    )(info, own, pairs)


def group_sums_kernel(info_ref, own_ref, oth_ref, wo_ref, wx_ref, o_ref, w, o, sems, out_sems):
    core, x = info_ref[1], info_ref[2]
    copies = []
    for at in range(4):
        turn = (x + 4 - at) % 4
        for n, (src, side) in enumerate(((wo_ref, core), (wx_ref, 1 - core))):
            row = pl.multiple_of((2 * at + side) * 48, 16)
            copies.append(pltpu.make_async_copy(src.at[turn], w.at[pl.ds(row, 48), :], sems.at[at, n]))
            copies[-1].start()
    sides = ((own_ref, core), (oth_ref, 1 - core))
    pairs = [src[:, 0:64, :].reshape(256, 128) for src, _ in sides]
    lasts = [src[:, 64:128, :].reshape(256, 128)[:, :HD] for src, _ in sides]
    for copy in copies:
        copy.wait()
    sent = []
    for n in range(3):
        cols = pl.ds(n * 512, 512)
        total = jnp.zeros((256, 512), F32)
        for pair, last, (_, side) in zip(pairs, lasts, sides):
            at = pl.multiple_of(side * 192, 64)
            total = total + dot(pair, w[pl.ds(at, 128), cols])
            total = total + dot(last, w[pl.ds(pl.multiple_of(at + 128, 64), HD), cols])
        o[:, :, cols] = total.astype(BF).reshape(4, TOK, 512)
        sent.append(pltpu.make_async_copy(o.at[:, :, cols], o_ref.at[:, :, cols], out_sems.at[n]))
        sent[-1].start()
    for copy in sent:
        copy.wait()


def group_sums(info, own, other, own_weight, other_weight):
    anywhere = pl.BlockSpec(memory_space=pl.ANY)
    return pl.pallas_call(
        group_sums_kernel,
        out_shape=jax.ShapeDtypeStruct((4, TOK, D), BF),
        in_specs=[pl.BlockSpec(memory_space=pltpu.SMEM), vmem(), vmem(), anywhere, anywhere],
        out_specs=pl.BlockSpec(memory_space=pltpu.HBM),
        scratch_shapes=[
            pltpu.VMEM((384, D), BF),
            pltpu.VMEM((4, TOK, D), BF),
            pltpu.SemaphoreType.DMA((4, 2)),
            pltpu.SemaphoreType.DMA((3,)),
        ],
        compiler_params=params(20),
        cost_estimate=pl.CostEstimate(flops=2 * 256 * 384 * D, bytes_accessed=2 << 20, transcendentals=0),
        interpret=INTERPRET,
        name="group_sums",
    )(info, own, other, own_weight, other_weight)


def prepare_kernel(up_ref, down_ref, shard_ref, after_ref, o_ref, so_ref):
    o_ref[0:64, 0:1024] = up_ref[0:64, :]
    o_ref[0:32, 1024:1536] = up_ref[64:96, 0:512]
    o_ref[32:64, 1024:1536] = up_ref[64:96, 512:1024]
    o_ref[64:96, :] = down_ref[...]
    so_ref[...] = shard_ref[...]


def prepare(up, down, shard, after):
    return pl.pallas_call(
        prepare_kernel,
        out_shape=(jax.ShapeDtypeStruct((96, D), BF), jax.ShapeDtypeStruct(shard.shape, BF)),
        in_specs=[vmem()] * 3 + [pl.BlockSpec(memory_space=pl.ANY)],
        out_specs=(vmem(), vmem()),
        cost_estimate=pl.CostEstimate(flops=1 << 33, bytes_accessed=1 << 20, transcendentals=0),
        interpret=INTERPRET,
        name="prepare",
    )(up, down, shard, after)


def norm_dispatch_kernel(sum_ref, hid_ref, gain_ref, ids_ref, res_ref, disp_ref):
    experts = iota((NT, TOK), 0)
    named = jnp.zeros((NT, TOK), F32)
    for k in range(TOPK):
        named = named + jnp.where(ids_ref[k : k + 1, :] == experts, 1.0, 0.0)
    before = jnp.where(iota((TOK, TOK), 0) < iota((TOK, TOK), 1), 1.0, 0.0).astype(BF)
    rank = dot(named.astype(BF), before)
    rank = jnp.where(named > 0.5, rank, -1.0).astype(BF)
    spread = jnp.where(iota((512, NT), 0) // SLOT == iota((512, NT), 1), 1.0, 0.0).astype(BF)
    ranks = dot(spread, rank)
    place = iota((512, TOK), 0) % SLOT
    pick = jnp.where(ranks == place.astype(F32), 1.0, 0.0).astype(BF)
    late = jnp.where(ranks == float(SLOT), 1.0, 0.0)

    total = hid_ref[...].astype(F32)
    for z in range(4):
        total = total + sum_ref[z].astype(F32)
    res_ref[...] = total
    meansq = jnp.mean(total * total, 1, keepdims=True)
    normed = (total * lax.rsqrt(meansq + EPS) * gain_ref[...]).astype(BF)
    extra = jnp.zeros((512, 128), F32)
    for c in range(CH):
        chunk = normed[:, c * 128 : c * 128 + 128]
        disp_ref[:, c * SLOT : (c + 1) * SLOT, :] = (
            dot(pick, chunk).astype(BF).reshape(NT, SLOT, 128)
        )
        extra = extra + dot(jnp.where(place == c, late, 0.0).astype(BF), chunk)
    disp_ref[:, SLOT * CH : SROWS, :] = extra.astype(BF).reshape(NT, 16, 128)


def norm_dispatch(sums, hidden, gain, ids_t):
    return pl.pallas_call(
        norm_dispatch_kernel,
        out_shape=(
            jax.ShapeDtypeStruct((TOK, D), F32),
            jax.ShapeDtypeStruct((NT, SROWS, 128), BF),
        ),
        in_specs=[vmem()] * 4,
        out_specs=(vmem(), vmem()),
        compiler_params=params(32),
        cost_estimate=pl.CostEstimate(flops=1 << 30, bytes_accessed=4 << 20, transcendentals=0),
        interpret=INTERPRET,
        name="norm_dispatch",
    )(sums, hidden, gain, ids_t)


def gather_extra(block):
    rows = iota((CH * NT, 512), 0)
    cols = iota((CH * NT, 512), 1)
    match = (rows % NT == cols // 16) & (rows // NT == cols % 16)
    stacked = dot(jnp.where(match, 1.0, 0.0).astype(BF), block).astype(BF)
    return [stacked[c * NT : (c + 1) * NT, :] for c in range(CH)]


def unpack_kernel(info_ref, wo_ref, wx_ref, w1_ref, w2_ref):
    zlo = info_ref[3]
    for d in range(2 * wo_ref.shape[0]):
        src, block = (wo_ref, zlo) if d % 2 == 0 else (wx_ref, 1 - zlo)
        block = block + d // 2 * 2
        top = pl.multiple_of(block * 96, 32)
        w1_ref[pl.ds(top, 64), :] = src[d // 2, 0:64, 0:1024]
        w1_ref[pl.ds(top + 64, 32), 0:512] = src[d // 2, 0:32, 1024:1536]
        w1_ref[pl.ds(top + 64, 32), 512:1024] = src[d // 2, 32:64, 1024:1536]
        w2_ref[pl.ds(pl.multiple_of(block * 32, 32), 32), :] = src[d // 2, 64:96, :]


def unpack(info, own_weights, other_weights):
    blocks = 2 * own_weights.shape[0]
    return pl.pallas_call(
        unpack_kernel,
        out_shape=(
            jax.ShapeDtypeStruct((blocks * 96, 2 * FFE), BF),
            jax.ShapeDtypeStruct((blocks * 32, D), BF),
        ),
        in_specs=[pl.BlockSpec(memory_space=pltpu.SMEM), vmem(), vmem()],
        out_specs=(vmem(), vmem()),
        compiler_params=params(20),
        interpret=INTERPRET,
        name="unpack",
    )(info, own_weights, other_weights)


def expert_kernel(in_ref, up_ref, down_ref, o_ref, x, w1, w2, o, sems, out_sems):
    loads = [
        pltpu.make_async_copy(src.at[rows, :], dst.at[rows, :], sems.at[n])
        for n, (src, dst, rows) in enumerate(
            ((up_ref, w1, pl.ds(0, 768)), (up_ref, w1, pl.ds(768, 768)), (down_ref, w2, pl.ds(0, FFE)))
        )
    ]
    for copy in loads:
        copy.start()
    for c in range(CH):
        x[0:512, c * 128 : c * 128 + 128] = in_ref[:, c * SLOT : (c + 1) * SLOT, :].reshape(512, 128)
    chunks = gather_extra(in_ref[:, SLOT * CH : SROWS, :].reshape(512, 128))
    for c in range(CH):
        x[512:544, c * 128 : c * 128 + 128] = chunks[c]
    loads[0].wait()
    hidden = dot(x[:, 0:768], w1[0:768, :])
    loads[1].wait()
    hidden = hidden + dot(x[:, 768:1536], w1[768:1536, :])
    gate = hidden[:, :FFE]
    active = (gate / (1.0 + jnp.exp(-gate)) * hidden[:, FFE:]).astype(BF)
    loads[2].wait()
    place = iota((512, NT), 0)
    owner = place // 16 == iota((512, NT), 1)
    extra = jnp.zeros((512, 128), F32)
    sent = []
    for c in range(0, CH, 2):
        out = dot(active, w2[:, c * 128 : c * 128 + 256]).astype(BF)
        for n in range(2):
            cols = slice(n * 128, n * 128 + 128)
            o[:, (c + n) * SLOT : (c + n + 1) * SLOT, :] = out[0:512, cols].reshape(NT, SLOT, 128)
            match = jnp.where(owner & (place % 16 == c + n), 1.0, 0.0).astype(BF)
            extra = extra + dot(match, out[512:544, cols])
        rows = pl.ds(c * SLOT, 2 * SLOT)
        sent.append(pltpu.make_async_copy(o.at[:, rows, :], o_ref.at[:, rows, :], out_sems.at[c // 2]))
        sent[-1].start()
    o[:, SLOT * CH : SROWS, :] = extra.astype(BF).reshape(NT, 16, 128)
    rows = pl.ds(CH * SLOT, 16)
    sent.append(pltpu.make_async_copy(o.at[:, rows, :], o_ref.at[:, rows, :], out_sems.at[CH // 2]))
    sent[-1].start()
    for copy in sent:
        copy.wait()


def expert(slots, up, down):
    return pl.pallas_call(
        expert_kernel,
        out_shape=jax.ShapeDtypeStruct((NT, SROWS, 128), BF),
        in_specs=[vmem()] + [pl.BlockSpec(memory_space=pltpu.HBM)] * 2,
        out_specs=pl.BlockSpec(memory_space=pltpu.HBM),
        scratch_shapes=[
            pltpu.VMEM((544, D), BF),
            pltpu.VMEM(up.shape, BF),
            pltpu.VMEM(down.shape, BF),
            pltpu.VMEM((NT, SROWS, 128), BF),
            pltpu.SemaphoreType.DMA((3,)),
            pltpu.SemaphoreType.DMA((CH // 2 + 1,)),
        ],
        compiler_params=params(58),
        cost_estimate=pl.CostEstimate(
            flops=2 * 544 * 1536 * 1536, bytes_accessed=9 << 20, transcendentals=544 * 512
        ),
        interpret=INTERPRET,
        name="expert",
    )(slots, up, down)


def combine_kernel(in_ref, res_ref, ids_ref, gate_ref, o_ref):
    experts = iota((TOK, NT), 1)
    named = jnp.zeros((TOK, NT), F32)
    gates = jnp.zeros((TOK, NT), F32)
    for k in range(TOPK):
        match = ids_ref[:, k : k + 1] == experts
        named = named + jnp.where(match, 1.0, 0.0)
        gates = gates + jnp.where(match, gate_ref[:, k : k + 1], 0.0)
    before = jnp.where(iota((TOK, TOK), 1) < iota((TOK, TOK), 0), 1.0, 0.0).astype(BF)
    rank = dot(before, named.astype(BF))
    rank = jnp.where(named > 0.5, rank, -1.0)
    spread = jnp.where(iota((NT, 512), 0) == iota((NT, 512), 1) // SLOT, 1.0, 0.0).astype(BF)
    place = (iota((TOK, 512), 1) % SLOT).astype(F32)
    pick = dot(rank.astype(BF), spread) == place
    high = gates.astype(BF)
    low = (gates - high.astype(F32)).astype(BF)
    weights = jnp.concatenate(
        [jnp.where(pick, dot(part, spread), 0.0).astype(BF) for part in (high, low)], 0
    )
    late = rank == float(SLOT)
    late_weights = jnp.concatenate(
        [jnp.where(late, part.astype(F32), 0.0).astype(BF) for part in (high, low)], 0
    )
    chunks = gather_extra(in_ref[:, SLOT * CH : SROWS, :].reshape(512, 128))
    for c in range(CH):
        main = in_ref[:, c * SLOT : (c + 1) * SLOT, :].reshape(512, 128)
        both = dot(weights, main) + dot(late_weights, chunks[c])
        cols = slice(c * 128, c * 128 + 128)
        o_ref[:, cols] = (res_ref[:, cols] + (both[:TOK] + both[TOK:])).astype(BF)


def combine(returned, residual, ids, gates):
    return pl.pallas_call(
        combine_kernel,
        out_shape=jax.ShapeDtypeStruct((TOK, D), BF),
        in_specs=[vmem()] * 4,
        out_specs=vmem(),
        compiler_params=params(32),
        interpret=INTERPRET,
        name="combine",
    )(returned, residual, ids, gates)


def shards(
    hidden_in,
    rotated_queries,
    fresh_key_values,
    cached_key_values,
    cached_len,
    expert_ids,
    route_gates,
    output_weight,
    norm_gain,
    gate_up,
    down_weight,
):
    zlo = lax.axis_index("zlo").astype(jnp.int32)
    x = lax.axis_index("x").astype(jnp.int32)
    core = lax.axis_index("core").astype(jnp.int32)
    length = cached_len[0]
    info = jnp.stack([length, core, x, zlo])
    ids = expert_ids[0, 0, 0]
    gates = route_gates[0, 0, 0]

    send = pack(rotated_queries[0, 0, 0], fresh_key_values[0, 0, 0], cached_key_values[0])
    packed, shard = prepare(gate_up[0], down_weight[0], output_weight, send)
    turns = [
        lax.ppermute(shard, "x", [(n, (n + step) % 4) for n in range(4)]) for step in (1, 2, 3)
    ]
    own = lax.all_to_all(send, ("zhi", "core"), split_axis=0, concat_axis=0, tiled=True)
    turns, packed, own = lax.optimization_barrier((turns, packed, own))
    own_weights = lax.all_gather(packed, "y", axis=0)
    across = lax.ppermute(packed, "zlo", [(0, 1), (1, 0)])
    own_rows = jnp.stack([shard, *turns], 0)
    other_rows = lax.ppermute(own_rows, "core", [(0, 1), (1, 0)])
    spread = jnp.broadcast_to(own[None, :, 96:], (4, HKV, 96, 128))
    pairs = lax.all_to_all(spread, "x", split_axis=0, concat_axis=0, tiled=True)
    kept, sent = attention(info, own, pairs)
    across, other_rows, sent = lax.optimization_barrier((across, other_rows, sent))
    other_weights = lax.all_gather(across, "y", axis=0)
    swapped = lax.ppermute(sent, "core", [(0, 1), (1, 0)])
    terms = group_sums(info, kept, swapped, own_rows, other_rows)
    sums = lax.all_to_all(terms, "zhi", split_axis=0, concat_axis=0, tiled=True)
    residual, outbound = norm_dispatch(sums, hidden_in[0, 0, 0], norm_gain[None], ids.T)
    slots = lax.all_to_all(outbound, TEN, split_axis=0, concat_axis=0, tiled=True)
    computed = expert(slots, *unpack(info, own_weights, other_weights))
    returned = lax.all_to_all(computed, TEN, split_axis=0, concat_axis=0, tiled=True)
    hidden_out = combine(returned, residual, ids, gates)

    low_x = x % 2
    mine = lax.dynamic_slice_in_dim(pairs, (low_x * 2 + core) * 32, 32, 3)
    for_other = lax.dynamic_slice_in_dim(pairs, (low_x * 2 + 1 - core) * 32, 32, 3)
    theirs = lax.ppermute(for_other, "core", [(0, 1), (1, 0)])
    chosen = jnp.where(core == x // 2, mine, theirs).reshape(4, 4, 2, 96, 32)
    chosen = jnp.transpose(chosen, (1, 0, 2, 3, 4)).reshape(NT, 96, 32)
    old_rows = chosen[:, :CROWS].reshape(NT * CROWS, 32)
    new_rows = chosen[:, CROWS:].reshape(NT * TOK, 32)
    total = NT * CROWS + NT * TOK
    base = jnp.concatenate([old_rows, jnp.zeros((NT * TOK, 32), BF)], 0)
    base = jnp.where((jnp.arange(total, dtype=jnp.int32) < length)[:, None], base, jnp.zeros_like(base))
    cache_out = lax.dynamic_update_slice_in_dim(base, new_rows, length, 0)
    return hidden_out.reshape(1, 1, 1, TOK, D), cache_out[None]


def solution(mesh):
    dp, tensor = mesh.devices.shape
    fine = Mesh(mesh.devices.reshape(dp // 2, 2, 4, 4, 2), ("y", "zlo", "zhi", "x", "core"))
    ydp = ("y", "zlo")
    return jax.shard_map(
        shards,
        mesh=fine,
        in_specs=(
            P(ydp, TEN, None, None, None),
            P(ydp, TEN, None, None, None),
            P(ydp, TEN, None, None, None),
            P(ydp, TEN, None),
            P(ydp),
            P(ydp, TEN, None, None, None),
            P(ydp, TEN, None, None, None),
            P(TEN, None),
            P(),
            P(TEN, ydp, None),
            P(TEN, ydp, None),
        ),
        out_specs=(P(ydp, TEN, None, None, None), P(ydp, None, TEN)),
        check_vma=False,
    )
```

```python
import functools
import math

import jax
import jax.numpy as jnp
from jax import lax
from jax.experimental import pallas as pl
from jax.experimental.pallas import tpu as pltpu
from jax.sharding import Mesh
from jax.sharding import PartitionSpec as P

D = 1536
HQ = 24
HKV = 8
HD = 64
FFE = 512
TOPK = 8
EPS = 1e-05
NT = 32
TOK = 64
CROWS = 32
SLOT = 16
CH = D // 128
SROWS = SLOT * CH + 16
BF = jnp.bfloat16
F32 = jnp.float32
TEN = ("zhi", "x", "core")
NEG = -1e30
INTERPRET = False


def vmem():
    return pl.BlockSpec(memory_space=pltpu.VMEM)


def params(mib):
    return pltpu.CompilerParams(vmem_limit_bytes=int(mib * (1 << 20)))


def dot(a, b):
    return lax.dot_general(a, b, (((1,), (0,)), ((), ())), preferred_element_type=F32)


def iota(shape, dim):
    return lax.broadcasted_iota(jnp.int32, shape, dim)


def pack_kernel(q_ref, f_ref, c_ref, o_ref):
    for g in range(HKV):
        cols = pl.ds(g * 128, 128)
        rows = q_ref[:, g * 192 : g * 192 + 192]
        o_ref[g, 0:64, :] = rows[:, :128]
        o_ref[g, 64:96, :] = jnp.concatenate([rows[0:32, 128:], rows[32:64, 128:]], 1)
        o_ref[g, 96:128, :] = c_ref[:, cols]
        o_ref[g, 128:192, :] = f_ref[:, cols]


def pack(queries, fresh, cache):
    return pl.pallas_call(
        pack_kernel,
        out_shape=jax.ShapeDtypeStruct((HKV, 192, 128), BF),
        in_specs=[vmem()] * 3,
        out_specs=vmem(),
        interpret=INTERPRET,
        name="pack",
    )(queries, fresh, cache)


def attention_kernel(info_ref, own_ref, pair_ref, keep_ref, send_ref, kv, vals, keys, sc, probs, bias_c, bias_d):
    b = pl.program_id(0)
    length, core, x = info_ref[0], info_ref[1], info_ref[2]

    @pl.when(b == 0)
    def _():
        for t in range(NT):
            src = pair_ref.at[t // 2 % 4, t // 8 * 2 + t % 2]
            kv[t * 32 : t * 32 + 32, :] = src[0:32, :]
            kv[1024 + t * 64 : 1088 + t * 64, :] = src[32:96, :]
        for t in range(6):
            some = kv[t * 512 : t * 512 + 512, :].astype(F32)
            vals[t * 512 : t * 512 + 512, :] = jnp.where(iota((512, 128), 1) < HD, 1.0, some).astype(BF)
            keys[:, t * 512 : t * 512 + 512] = some.T.astype(BF)
        bias_c[...] = jnp.where(iota((8, 1024), 1) < length, 0.0, NEG)
        query_at = x * 128 + iota((128, 512), 0)
        bias_d[...] = jnp.where(iota((128, 512), 1) <= query_at, 0.0, NEG)

    low = iota((128, 128), 1) < HD

    def block(b):
        first = own_ref[b * 2 : b * 2 + 2, 0:64, :].reshape(128, 128).astype(F32) * 0.125
        last = own_ref[b * 2 : b * 2 + 2, 64:96, :].reshape(64, 128).astype(F32) * 0.125
        turned = pltpu.roll(last, HD, 1)
        third = jnp.concatenate([last[0:32], turned[0:32], last[32:64], turned[32:64]], 0)
        heads = (first, pltpu.roll(first, HD, 1), third)
        q = jnp.concatenate([jnp.where(low, head, 0.0) for head in heads], 0).astype(BF)
        count = 3 + b
        top = jnp.full((384, 128), NEG, F32)
        for k in range(count):
            at = k * 512
            s = dot(q, keys[:, at : at + 512])
            if k < 2:
                s = s + bias_c[0:1, at : at + 512]
            elif k == count - 1:
                s = s + jnp.concatenate([bias_d[...]] * 3, 0)
            sc[k] = s
            for j in range(4):
                top = jnp.maximum(top, s[:, j * 128 : j * 128 + 128])
        highest = jnp.max(top, 1, keepdims=True)
        accs = []
        for h in range(3):
            rows = slice(h * 128, h * 128 + 128)
            for k in range(count):
                part = jnp.exp(sc[k, rows, :] - highest[rows])
                probs[rows, k * 512 : k * 512 + 512] = part.astype(BF)
            accs.append(dot(probs[rows, : count * 512], vals[: count * 512, :]))
        acc = jnp.concatenate(accs, 0)
        out = acc / pltpu.roll(acc, HD, 1)
        a0, a1, a2 = out[0:128], out[128:256], out[256:384]
        tiles = (
            jnp.where(low, pltpu.roll(a0, HD, 1), a1),
            jnp.where(low, pltpu.roll(a2, HD, 1), 0.0),
        )
        for n, tile in enumerate(tiles):
            even, odd = tile[0:64], tile[64:128]
            rows = slice(n * 64, n * 64 + 64)
            keep_ref[b, rows, :] = jnp.where(core == 0, even, odd).astype(BF)
            send_ref[b, rows, :] = jnp.where(core == 0, odd, even).astype(BF)

    for n in range(4):
        pl.when(b == n)(functools.partial(block, n))


def attention(info, own, pairs):
    shape = jax.ShapeDtypeStruct((4, 128, 128), BF)
    return pl.pallas_call(
        attention_kernel,
        out_shape=(shape, shape),
        grid=(4,),
        in_specs=[pl.BlockSpec(memory_space=pltpu.SMEM), vmem(), vmem()],
        out_specs=(vmem(), vmem()),
        scratch_shapes=[
            pltpu.VMEM((3072, 128), BF),
            pltpu.VMEM((3072, 128), BF),
            pltpu.VMEM((128, 3072), BF),
            pltpu.VMEM((6, 384, 512), F32),
            pltpu.VMEM((384, 3072), BF),
            pltpu.VMEM((8, 1024), F32),
            pltpu.VMEM((128, 512), F32),
        ],
        compiler_params=params(32),
        cost_estimate=pl.CostEstimate(
            flops=2 * 2 * 1536 * 2304 * 128, bytes_accessed=3 << 20, transcendentals=1536 * 2304
        ),
        interpret=INTERPRET,
        name="attention",
    )(info, own, pairs)


def group_sums_kernel(info_ref, own_ref, oth_ref, w, o_ref, o, out_sems):
    core = info_ref[1]
    sides = ((own_ref, core), (oth_ref, 1 - core))
    pairs = [src[:, 0:64, :].reshape(256, 128) for src, _ in sides]
    lasts = [src[:, 64:128, :].reshape(256, 128)[:, :HD] for src, _ in sides]
    sent = []
    for n in range(3):
        cols = pl.ds(n * 512, 512)
        total = jnp.zeros((256, 512), F32)
        for pair, last, (_, side) in zip(pairs, lasts, sides):
            at = pl.multiple_of(side * 192, 64)
            total = total + dot(pair, w[pl.ds(at, 128), cols])
            total = total + dot(last, w[pl.ds(pl.multiple_of(at + 128, 64), HD), cols])
        o[:, :, cols] = total.astype(BF).reshape(4, TOK, 512)
        sent.append(pltpu.make_async_copy(o.at[:, :, cols], o_ref.at[:, :, cols], out_sems.at[n]))
        sent[-1].start()
    for copy in sent:
        copy.wait()


def group_sums(info, own, other, weight):
    return pl.pallas_call(
        group_sums_kernel,
        out_shape=jax.ShapeDtypeStruct((4, TOK, D), BF),
        in_specs=[pl.BlockSpec(memory_space=pltpu.SMEM)] + [vmem()] * 3,
        out_specs=pl.BlockSpec(memory_space=pltpu.HBM),
        scratch_shapes=[
            pltpu.VMEM((4, TOK, D), BF),
            pltpu.SemaphoreType.DMA((3,)),
        ],
        compiler_params=params(20),
        cost_estimate=pl.CostEstimate(flops=2 * 256 * 384 * D, bytes_accessed=2 << 20, transcendentals=0),
        interpret=INTERPRET,
        name="group_sums",
    )(info, own, other, weight)


def prepare_kernel(up_ref, down_ref, after_ref, o_ref):
    o_ref[0:64, 0:1024] = up_ref[0:64, :]
    o_ref[0:32, 1024:1536] = up_ref[64:96, 0:512]
    o_ref[32:64, 1024:1536] = up_ref[64:96, 512:1024]
    o_ref[64:96, :] = down_ref[...]


def prepare(up, down, after):
    return pl.pallas_call(
        prepare_kernel,
        out_shape=jax.ShapeDtypeStruct((96, D), BF),
        in_specs=[vmem()] * 2 + [pl.BlockSpec(memory_space=pl.ANY)],
        out_specs=vmem(),
        cost_estimate=pl.CostEstimate(flops=1 << 33, bytes_accessed=1 << 20, transcendentals=0),
        interpret=INTERPRET,
        name="prepare",
    )(up, down, after)


def norm_dispatch_kernel(sum_ref, hid_ref, gain_ref, ids_ref, res_ref, disp_ref):
    experts = iota((NT, TOK), 0)
    named = jnp.zeros((NT, TOK), F32)
    for k in range(TOPK):
        named = named + jnp.where(ids_ref[k : k + 1, :] == experts, 1.0, 0.0)
    before = jnp.where(iota((TOK, TOK), 0) < iota((TOK, TOK), 1), 1.0, 0.0).astype(BF)
    rank = dot(named.astype(BF), before)
    rank = jnp.where(named > 0.5, rank, -1.0).astype(BF)
    spread = jnp.where(iota((512, NT), 0) // SLOT == iota((512, NT), 1), 1.0, 0.0).astype(BF)
    ranks = dot(spread, rank)
    place = iota((512, TOK), 0) % SLOT
    pick = jnp.where(ranks == place.astype(F32), 1.0, 0.0).astype(BF)
    late = jnp.where(ranks == float(SLOT), 1.0, 0.0)

    total = hid_ref[...].astype(F32)
    for z in range(4):
        total = total + sum_ref[z].astype(F32)
    res_ref[...] = total
    meansq = jnp.mean(total * total, 1, keepdims=True)
    normed = (total * lax.rsqrt(meansq + EPS) * gain_ref[...]).astype(BF)
    extra = jnp.zeros((512, 128), F32)
    for c in range(CH):
        chunk = normed[:, c * 128 : c * 128 + 128]
        disp_ref[:, c * SLOT : (c + 1) * SLOT, :] = (
            dot(pick, chunk).astype(BF).reshape(NT, SLOT, 128)
        )
        extra = extra + dot(jnp.where(place == c, late, 0.0).astype(BF), chunk)
    disp_ref[:, SLOT * CH : SROWS, :] = extra.astype(BF).reshape(NT, 16, 128)


def norm_dispatch(sums, hidden, gain, ids_t):
    return pl.pallas_call(
        norm_dispatch_kernel,
        out_shape=(
            jax.ShapeDtypeStruct((TOK, D), F32),
            jax.ShapeDtypeStruct((NT, SROWS, 128), BF),
        ),
        in_specs=[vmem()] * 4,
        out_specs=(vmem(), vmem()),
        compiler_params=params(32),
        cost_estimate=pl.CostEstimate(flops=1 << 30, bytes_accessed=4 << 20, transcendentals=0),
        interpret=INTERPRET,
        name="norm_dispatch",
    )(sums, hidden, gain, ids_t)


def gather_extra(block):
    rows = iota((CH * NT, 512), 0)
    cols = iota((CH * NT, 512), 1)
    match = (rows % NT == cols // 16) & (rows // NT == cols % 16)
    stacked = dot(jnp.where(match, 1.0, 0.0).astype(BF), block).astype(BF)
    return [stacked[c * NT : (c + 1) * NT, :] for c in range(CH)]


def unpack_kernel(info_ref, wo_ref, wx_ref, w1_ref, w2_ref):
    zlo = info_ref[3]
    for d in range(2 * wo_ref.shape[0]):
        src, block = (wo_ref, zlo) if d % 2 == 0 else (wx_ref, 1 - zlo)
        block = block + d // 2 * 2
        top = pl.multiple_of(block * 96, 32)
        w1_ref[pl.ds(top, 64), :] = src[d // 2, 0:64, 0:1024]
        w1_ref[pl.ds(top + 64, 32), 0:512] = src[d // 2, 0:32, 1024:1536]
        w1_ref[pl.ds(top + 64, 32), 512:1024] = src[d // 2, 32:64, 1024:1536]
        w2_ref[pl.ds(pl.multiple_of(block * 32, 32), 32), :] = src[d // 2, 64:96, :]


def unpack(info, own_weights, other_weights):
    blocks = 2 * own_weights.shape[0]
    return pl.pallas_call(
        unpack_kernel,
        out_shape=(
            jax.ShapeDtypeStruct((blocks * 96, 2 * FFE), BF),
            jax.ShapeDtypeStruct((blocks * 32, D), BF),
        ),
        in_specs=[pl.BlockSpec(memory_space=pltpu.SMEM), vmem(), vmem()],
        out_specs=(vmem(), vmem()),
        compiler_params=params(20),
        interpret=INTERPRET,
        name="unpack",
    )(info, own_weights, other_weights)


def expert_kernel(in_ref, up_ref, down_ref, o_ref, x, w1, w2, o, sems, out_sems):
    loads = [
        pltpu.make_async_copy(src.at[rows, :], dst.at[rows, :], sems.at[n])
        for n, (src, dst, rows) in enumerate(
            ((up_ref, w1, pl.ds(0, 768)), (up_ref, w1, pl.ds(768, 768)), (down_ref, w2, pl.ds(0, FFE)))
        )
    ]
    for copy in loads:
        copy.start()
    for c in range(CH):
        x[0:512, c * 128 : c * 128 + 128] = in_ref[:, c * SLOT : (c + 1) * SLOT, :].reshape(512, 128)
    chunks = gather_extra(in_ref[:, SLOT * CH : SROWS, :].reshape(512, 128))
    for c in range(CH):
        x[512:544, c * 128 : c * 128 + 128] = chunks[c]
    loads[0].wait()
    hidden = dot(x[:, 0:768], w1[0:768, :])
    loads[1].wait()
    hidden = hidden + dot(x[:, 768:1536], w1[768:1536, :])
    gate = hidden[:, :FFE]
    active = (gate / (1.0 + jnp.exp(-gate)) * hidden[:, FFE:]).astype(BF)
    loads[2].wait()
    place = iota((512, NT), 0)
    owner = place // 16 == iota((512, NT), 1)
    extra = jnp.zeros((512, 128), F32)
    sent = []
    for c in range(0, CH, 2):
        out = dot(active, w2[:, c * 128 : c * 128 + 256]).astype(BF)
        for n in range(2):
            cols = slice(n * 128, n * 128 + 128)
            o[:, (c + n) * SLOT : (c + n + 1) * SLOT, :] = out[0:512, cols].reshape(NT, SLOT, 128)
            match = jnp.where(owner & (place % 16 == c + n), 1.0, 0.0).astype(BF)
            extra = extra + dot(match, out[512:544, cols])
        rows = pl.ds(c * SLOT, 2 * SLOT)
        sent.append(pltpu.make_async_copy(o.at[:, rows, :], o_ref.at[:, rows, :], out_sems.at[c // 2]))
        sent[-1].start()
    o[:, SLOT * CH : SROWS, :] = extra.astype(BF).reshape(NT, 16, 128)
    rows = pl.ds(CH * SLOT, 16)
    sent.append(pltpu.make_async_copy(o.at[:, rows, :], o_ref.at[:, rows, :], out_sems.at[CH // 2]))
    sent[-1].start()
    for copy in sent:
        copy.wait()


def expert(slots, up, down):
    return pl.pallas_call(
        expert_kernel,
        out_shape=jax.ShapeDtypeStruct((NT, SROWS, 128), BF),
        in_specs=[vmem()] + [pl.BlockSpec(memory_space=pltpu.HBM)] * 2,
        out_specs=pl.BlockSpec(memory_space=pltpu.HBM),
        scratch_shapes=[
            pltpu.VMEM((544, D), BF),
            pltpu.VMEM(up.shape, BF),
            pltpu.VMEM(down.shape, BF),
            pltpu.VMEM((NT, SROWS, 128), BF),
            pltpu.SemaphoreType.DMA((3,)),
            pltpu.SemaphoreType.DMA((CH // 2 + 1,)),
        ],
        compiler_params=params(58),
        cost_estimate=pl.CostEstimate(
            flops=2 * 544 * 1536 * 1536, bytes_accessed=9 << 20, transcendentals=544 * 512
        ),
        interpret=INTERPRET,
        name="expert",
    )(slots, up, down)


def combine_kernel(in_ref, res_ref, ids_ref, gate_ref, o_ref):
    experts = iota((TOK, NT), 1)
    named = jnp.zeros((TOK, NT), F32)
    gates = jnp.zeros((TOK, NT), F32)
    for k in range(TOPK):
        match = ids_ref[:, k : k + 1] == experts
        named = named + jnp.where(match, 1.0, 0.0)
        gates = gates + jnp.where(match, gate_ref[:, k : k + 1], 0.0)
    before = jnp.where(iota((TOK, TOK), 1) < iota((TOK, TOK), 0), 1.0, 0.0).astype(BF)
    rank = dot(before, named.astype(BF))
    rank = jnp.where(named > 0.5, rank, -1.0)
    spread = jnp.where(iota((NT, 512), 0) == iota((NT, 512), 1) // SLOT, 1.0, 0.0).astype(BF)
    place = (iota((TOK, 512), 1) % SLOT).astype(F32)
    pick = dot(rank.astype(BF), spread) == place
    high = gates.astype(BF)
    low = (gates - high.astype(F32)).astype(BF)
    weights = jnp.concatenate(
        [jnp.where(pick, dot(part, spread), 0.0).astype(BF) for part in (high, low)], 0
    )
    late = rank == float(SLOT)
    late_weights = jnp.concatenate(
        [jnp.where(late, part.astype(F32), 0.0).astype(BF) for part in (high, low)], 0
    )
    chunks = gather_extra(in_ref[:, SLOT * CH : SROWS, :].reshape(512, 128))
    for c in range(CH):
        main = in_ref[:, c * SLOT : (c + 1) * SLOT, :].reshape(512, 128)
        both = dot(weights, main) + dot(late_weights, chunks[c])
        cols = slice(c * 128, c * 128 + 128)
        o_ref[:, cols] = (res_ref[:, cols] + (both[:TOK] + both[TOK:])).astype(BF)


def combine(returned, residual, ids, gates):
    return pl.pallas_call(
        combine_kernel,
        out_shape=jax.ShapeDtypeStruct((TOK, D), BF),
        in_specs=[vmem()] * 4,
        out_specs=vmem(),
        compiler_params=params(32),
        interpret=INTERPRET,
        name="combine",
    )(returned, residual, ids, gates)


def shards(
    hidden_in,
    rotated_queries,
    fresh_key_values,
    cached_key_values,
    cached_len,
    expert_ids,
    route_gates,
    output_weight,
    norm_gain,
    gate_up,
    down_weight,
):
    zlo = lax.axis_index("zlo").astype(jnp.int32)
    x = lax.axis_index("x").astype(jnp.int32)
    core = lax.axis_index("core").astype(jnp.int32)
    length = cached_len[0]
    info = jnp.stack([length, core, x, zlo])
    ids = expert_ids[0, 0, 0]
    gates = route_gates[0, 0, 0]

    send = pack(rotated_queries[0, 0, 0], fresh_key_values[0, 0, 0], cached_key_values[0])
    plane_weight = lax.all_gather(output_weight, ("x", "core"), axis=0, tiled=True)
    packed = prepare(gate_up[0], down_weight[0], send)
    own = lax.all_to_all(send, ("zhi", "core"), split_axis=0, concat_axis=0, tiled=True)
    packed, own = lax.optimization_barrier((packed, own))
    own_weights = lax.all_gather(packed, "y", axis=0)
    across = lax.ppermute(packed, "zlo", [(0, 1), (1, 0)])
    spread = jnp.broadcast_to(own[None, :, 96:], (4, HKV, 96, 128))
    pairs = lax.all_to_all(spread, "x", split_axis=0, concat_axis=0, tiled=True)
    pairs, plane_weight = lax.optimization_barrier((pairs, plane_weight))
    kept, sent = attention(info, own, pairs)
    across, sent = lax.optimization_barrier((across, sent))
    other_weights = lax.all_gather(across, "y", axis=0)
    swapped = lax.ppermute(sent, "core", [(0, 1), (1, 0)])
    terms = group_sums(info, kept, swapped, plane_weight)
    sums = lax.all_to_all(terms, "zhi", split_axis=0, concat_axis=0, tiled=True)
    residual, outbound = norm_dispatch(sums, hidden_in[0, 0, 0], norm_gain[None], ids.T)
    slots = lax.all_to_all(outbound, TEN, split_axis=0, concat_axis=0, tiled=True)
    computed = expert(slots, *unpack(info, own_weights, other_weights))
    returned = lax.all_to_all(computed, TEN, split_axis=0, concat_axis=0, tiled=True)
    hidden_out = combine(returned, residual, ids, gates)

    low_x = x % 2
    mine = lax.dynamic_slice_in_dim(pairs, (low_x * 2 + core) * 32, 32, 3)
    for_other = lax.dynamic_slice_in_dim(pairs, (low_x * 2 + 1 - core) * 32, 32, 3)
    theirs = lax.ppermute(for_other, "core", [(0, 1), (1, 0)])
    chosen = jnp.where(core == x // 2, mine, theirs).reshape(4, 4, 2, 96, 32)
    chosen = jnp.transpose(chosen, (1, 0, 2, 3, 4)).reshape(NT, 96, 32)
    old_rows = chosen[:, :CROWS].reshape(NT * CROWS, 32)
    new_rows = chosen[:, CROWS:].reshape(NT * TOK, 32)
    total = NT * CROWS + NT * TOK
    base = jnp.concatenate([old_rows, jnp.zeros((NT * TOK, 32), BF)], 0)
    base = jnp.where((jnp.arange(total, dtype=jnp.int32) < length)[:, None], base, jnp.zeros_like(base))
    cache_out = lax.dynamic_update_slice_in_dim(base, new_rows, length, 0)
    return hidden_out.reshape(1, 1, 1, TOK, D), cache_out[None]


def solution(mesh):
    dp, tensor = mesh.devices.shape
    fine = Mesh(mesh.devices.reshape(dp // 2, 2, 4, 4, 2), ("y", "zlo", "zhi", "x", "core"))
    ydp = ("y", "zlo")
    return jax.shard_map(
        shards,
        mesh=fine,
        in_specs=(
            P(ydp, TEN, None, None, None),
            P(ydp, TEN, None, None, None),
            P(ydp, TEN, None, None, None),
            P(ydp, TEN, None),
            P(ydp),
            P(ydp, TEN, None, None, None),
            P(ydp, TEN, None, None, None),
            P(TEN, None),
            P(),
            P(TEN, ydp, None),
            P(TEN, ydp, None),
        ),
        out_specs=(P(ydp, TEN, None, None, None), P(ydp, None, TEN)),
        check_vma=False,
    )
```

```python
import functools
import math

import jax
import jax.numpy as jnp
from jax import lax
from jax.experimental import pallas as pl
from jax.experimental.pallas import tpu as pltpu
from jax.sharding import Mesh
from jax.sharding import PartitionSpec as P

D = 1536
HQ = 24
HKV = 8
HD = 64
FFE = 512
TOPK = 8
EPS = 1e-05
NT = 32
TOK = 64
CROWS = 32
SLOT = 16
CH = D // 128
SROWS = SLOT * CH + 16
BF = jnp.bfloat16
F32 = jnp.float32
TEN = ("zhi", "x", "core")
NEG = -1e30
INTERPRET = False


def vmem():
    return pl.BlockSpec(memory_space=pltpu.VMEM)


def params(mib):
    return pltpu.CompilerParams(vmem_limit_bytes=int(mib * (1 << 20)))


def dot(a, b):
    return lax.dot_general(a, b, (((1,), (0,)), ((), ())), preferred_element_type=F32)


def iota(shape, dim):
    return lax.broadcasted_iota(jnp.int32, shape, dim)


def pack_kernel(q_ref, f_ref, c_ref, o_ref):
    for g in range(HKV):
        cols = pl.ds(g * 128, 128)
        rows = q_ref[:, g * 192 : g * 192 + 192]
        o_ref[g, 0:64, :] = rows[:, :128]
        o_ref[g, 64:96, :] = jnp.concatenate([rows[0:32, 128:], rows[32:64, 128:]], 1)
        o_ref[g, 96:128, :] = c_ref[:, cols]
        o_ref[g, 128:192, :] = f_ref[:, cols]


def pack(queries, fresh, cache):
    return pl.pallas_call(
        pack_kernel,
        out_shape=jax.ShapeDtypeStruct((HKV, 192, 128), BF),
        in_specs=[vmem()] * 3,
        out_specs=vmem(),
        interpret=INTERPRET,
        name="pack",
    )(queries, fresh, cache)


def attention_kernel(info_ref, own_ref, pair_ref, keep_ref, send_ref, kv, vals, keys, sc, probs, bias_c, bias_d):
    b = pl.program_id(0)
    length, core, x = info_ref[0], info_ref[1], info_ref[2]

    @pl.when(b == 0)
    def _():
        for t in range(NT):
            src = pair_ref.at[t // 2 % 4, t // 8 * 2 + t % 2]
            kv[t * 32 : t * 32 + 32, :] = src[0:32, :]
            kv[1024 + t * 64 : 1088 + t * 64, :] = src[32:96, :]
        for t in range(6):
            some = kv[t * 512 : t * 512 + 512, :].astype(F32)
            vals[t * 512 : t * 512 + 512, :] = jnp.where(iota((512, 128), 1) < HD, 1.0, some).astype(BF)
            keys[:, t * 512 : t * 512 + 512] = some.T.astype(BF)
        bias_c[...] = jnp.where(iota((8, 1024), 1) < length, 0.0, NEG)
        query_at = x * 128 + iota((128, 512), 0)
        bias_d[...] = jnp.where(iota((128, 512), 1) <= query_at, 0.0, NEG)

    low = iota((128, 128), 1) < HD

    def block(b):
        first = own_ref[b * 2 : b * 2 + 2, 0:64, :].reshape(128, 128).astype(F32) * 0.125
        last = own_ref[b * 2 : b * 2 + 2, 64:96, :].reshape(64, 128).astype(F32) * 0.125
        turned = pltpu.roll(last, HD, 1)
        third = jnp.concatenate([last[0:32], turned[0:32], last[32:64], turned[32:64]], 0)
        heads = (first, pltpu.roll(first, HD, 1), third)
        q = jnp.concatenate([jnp.where(low, head, 0.0) for head in heads], 0).astype(BF)
        count = 3 + b
        top = jnp.full((384, 128), NEG, F32)
        for k in range(count):
            at = k * 512
            s = dot(q, keys[:, at : at + 512])
            if k < 2:
                s = s + bias_c[0:1, at : at + 512]
            elif k == count - 1:
                s = s + jnp.concatenate([bias_d[...]] * 3, 0)
            sc[k] = s
            for j in range(4):
                top = jnp.maximum(top, s[:, j * 128 : j * 128 + 128])
        highest = jnp.max(top, 1, keepdims=True)
        accs = []
        for h in range(3):
            rows = slice(h * 128, h * 128 + 128)
            for k in range(count):
                part = jnp.exp(sc[k, rows, :] - highest[rows])
                probs[rows, k * 512 : k * 512 + 512] = part.astype(BF)
            accs.append(dot(probs[rows, : count * 512], vals[: count * 512, :]))
        acc = jnp.concatenate(accs, 0)
        out = acc / pltpu.roll(acc, HD, 1)
        a0, a1, a2 = out[0:128], out[128:256], out[256:384]
        tiles = (
            jnp.where(low, pltpu.roll(a0, HD, 1), a1),
            jnp.where(low, pltpu.roll(a2, HD, 1), 0.0),
        )
        for n, tile in enumerate(tiles):
            even, odd = tile[0:64], tile[64:128]
            rows = slice(n * 64, n * 64 + 64)
            keep_ref[b, rows, :] = jnp.where(core == 0, even, odd).astype(BF)
            send_ref[b, rows, :] = jnp.where(core == 0, odd, even).astype(BF)

    for n in range(4):
        pl.when(b == n)(functools.partial(block, n))


def attention(info, own, pairs):
    shape = jax.ShapeDtypeStruct((4, 128, 128), BF)
    return pl.pallas_call(
        attention_kernel,
        out_shape=(shape, shape),
        grid=(4,),
        in_specs=[pl.BlockSpec(memory_space=pltpu.SMEM), vmem(), vmem()],
        out_specs=(vmem(), vmem()),
        scratch_shapes=[
            pltpu.VMEM((3072, 128), BF),
            pltpu.VMEM((3072, 128), BF),
            pltpu.VMEM((128, 3072), BF),
            pltpu.VMEM((6, 384, 512), F32),
            pltpu.VMEM((384, 3072), BF),
            pltpu.VMEM((8, 1024), F32),
            pltpu.VMEM((128, 512), F32),
        ],
        compiler_params=params(32),
        cost_estimate=pl.CostEstimate(
            flops=2 * 2 * 1536 * 2304 * 128, bytes_accessed=3 << 20, transcendentals=1536 * 2304
        ),
        interpret=INTERPRET,
        name="attention",
    )(info, own, pairs)


def group_sums_kernel(info_ref, own_ref, oth_ref, w, o_ref, o, out_sems):
    core = info_ref[1]
    sides = ((own_ref, core), (oth_ref, 1 - core))
    pairs = [src[:, 0:64, :].reshape(256, 128) for src, _ in sides]
    lasts = [src[:, 64:128, :].reshape(256, 128)[:, :HD] for src, _ in sides]
    sent = []
    for n in range(3):
        cols = pl.ds(n * 512, 512)
        total = jnp.zeros((256, 512), F32)
        for pair, last, (_, side) in zip(pairs, lasts, sides):
            at = pl.multiple_of(side * 192, 64)
            total = total + dot(pair, w[pl.ds(at, 128), cols])
            total = total + dot(last, w[pl.ds(pl.multiple_of(at + 128, 64), HD), cols])
        o[:, :, cols] = total.astype(BF).reshape(4, TOK, 512)
        sent.append(pltpu.make_async_copy(o.at[:, :, cols], o_ref.at[:, :, cols], out_sems.at[n]))
        sent[-1].start()
    for copy in sent:
        copy.wait()


def group_sums(info, own, other, weight):
    return pl.pallas_call(
        group_sums_kernel,
        out_shape=jax.ShapeDtypeStruct((4, TOK, D), BF),
        in_specs=[pl.BlockSpec(memory_space=pltpu.SMEM)] + [vmem()] * 3,
        out_specs=pl.BlockSpec(memory_space=pltpu.HBM),
        scratch_shapes=[
            pltpu.VMEM((4, TOK, D), BF),
            pltpu.SemaphoreType.DMA((3,)),
        ],
        compiler_params=params(20),
        cost_estimate=pl.CostEstimate(flops=2 * 256 * 384 * D, bytes_accessed=2 << 20, transcendentals=0),
        interpret=INTERPRET,
        name="group_sums",
    )(info, own, other, weight)


def prepare_kernel(up_ref, down_ref, after_ref, o_ref):
    o_ref[0:64, 0:1024] = up_ref[0:64, :]
    o_ref[0:32, 1024:1536] = up_ref[64:96, 0:512]
    o_ref[32:64, 1024:1536] = up_ref[64:96, 512:1024]
    o_ref[64:96, :] = down_ref[...]


def prepare(up, down, after):
    return pl.pallas_call(
        prepare_kernel,
        out_shape=jax.ShapeDtypeStruct((96, D), BF),
        in_specs=[vmem()] * 2 + [pl.BlockSpec(memory_space=pl.ANY)],
        out_specs=vmem(),
        cost_estimate=pl.CostEstimate(flops=1 << 33, bytes_accessed=1 << 20, transcendentals=0),
        interpret=INTERPRET,
        name="prepare",
    )(up, down, after)


def norm_dispatch_kernel(sum_ref, hid_ref, gain_ref, ids_ref, res_ref, disp_ref):
    experts = iota((NT, TOK), 0)
    named = jnp.zeros((NT, TOK), F32)
    for k in range(TOPK):
        named = named + jnp.where(ids_ref[k : k + 1, :] == experts, 1.0, 0.0)
    before = jnp.where(iota((TOK, TOK), 0) < iota((TOK, TOK), 1), 1.0, 0.0).astype(BF)
    rank = dot(named.astype(BF), before)
    rank = jnp.where(named > 0.5, rank, -1.0).astype(BF)
    spread = jnp.where(iota((512, NT), 0) // SLOT == iota((512, NT), 1), 1.0, 0.0).astype(BF)
    ranks = dot(spread, rank)
    place = iota((512, TOK), 0) % SLOT
    pick = jnp.where(ranks == place.astype(F32), 1.0, 0.0).astype(BF)
    late = jnp.where(ranks == float(SLOT), 1.0, 0.0)

    total = hid_ref[...].astype(F32)
    for z in range(4):
        total = total + sum_ref[z].astype(F32)
    res_ref[...] = total
    meansq = jnp.mean(total * total, 1, keepdims=True)
    normed = (total * lax.rsqrt(meansq + EPS) * gain_ref[...]).astype(BF)
    extra = jnp.zeros((512, 128), F32)
    for c in range(CH):
        chunk = normed[:, c * 128 : c * 128 + 128]
        disp_ref[:, c * SLOT : (c + 1) * SLOT, :] = (
            dot(pick, chunk).astype(BF).reshape(NT, SLOT, 128)
        )
        extra = extra + dot(jnp.where(place == c, late, 0.0).astype(BF), chunk)
    disp_ref[:, SLOT * CH : SROWS, :] = extra.astype(BF).reshape(NT, 16, 128)


def norm_dispatch(sums, hidden, gain, ids_t):
    return pl.pallas_call(
        norm_dispatch_kernel,
        out_shape=(
            jax.ShapeDtypeStruct((TOK, D), F32),
            jax.ShapeDtypeStruct((NT, SROWS, 128), BF),
        ),
        in_specs=[vmem()] * 4,
        out_specs=(vmem(), vmem()),
        compiler_params=params(32),
        cost_estimate=pl.CostEstimate(flops=1 << 30, bytes_accessed=4 << 20, transcendentals=0),
        interpret=INTERPRET,
        name="norm_dispatch",
    )(sums, hidden, gain, ids_t)


def gather_extra(block):
    rows = iota((CH * NT, 512), 0)
    cols = iota((CH * NT, 512), 1)
    match = (rows % NT == cols // 16) & (rows // NT == cols % 16)
    stacked = dot(jnp.where(match, 1.0, 0.0).astype(BF), block).astype(BF)
    return [stacked[c * NT : (c + 1) * NT, :] for c in range(CH)]


def merge_kernel(info_ref, own_ref, oth_ref, o_ref):
    zlo = info_ref[3]
    o_ref[zlo] = own_ref[...]
    o_ref[1 - zlo] = oth_ref[...]


def merge(info, own, other):
    return pl.pallas_call(
        merge_kernel,
        out_shape=jax.ShapeDtypeStruct((2,) + own.shape, BF),
        in_specs=[
            pl.BlockSpec(memory_space=pltpu.SMEM),
            vmem(),
            vmem(),
        ],
        out_specs=vmem(),
        cost_estimate=pl.CostEstimate(flops=1 << 33, bytes_accessed=1 << 20, transcendentals=0),
        interpret=INTERPRET,
        name="merge",
    )(info, own, other)


def unpack_kernel(src, w1_ref, w2_ref):
    for d in range(src.shape[0]):
        top = d * 96
        w1_ref[top : top + 64, :] = src[d, 0:64, 0:1024]
        w1_ref[top + 64 : top + 96, 0:512] = src[d, 0:32, 1024:1536]
        w1_ref[top + 64 : top + 96, 512:1024] = src[d, 32:64, 1024:1536]
        w2_ref[d * 32 : d * 32 + 32, :] = src[d, 64:96, :]


def unpack(weights):
    blocks = weights.shape[0]
    return pl.pallas_call(
        unpack_kernel,
        out_shape=(
            jax.ShapeDtypeStruct((blocks * 96, 2 * FFE), BF),
            jax.ShapeDtypeStruct((blocks * 32, D), BF),
        ),
        in_specs=[vmem()],
        out_specs=(vmem(), vmem()),
        compiler_params=params(20),
        interpret=INTERPRET,
        name="unpack",
    )(weights)


def expert_kernel(in_ref, up_ref, down_ref, o_ref, x, w1, w2, o, sems, out_sems):
    loads = [
        pltpu.make_async_copy(src.at[rows, :], dst.at[rows, :], sems.at[n])
        for n, (src, dst, rows) in enumerate(
            ((up_ref, w1, pl.ds(0, 768)), (up_ref, w1, pl.ds(768, 768)), (down_ref, w2, pl.ds(0, FFE)))
        )
    ]
    for copy in loads:
        copy.start()
    for c in range(CH):
        x[0:512, c * 128 : c * 128 + 128] = in_ref[:, c * SLOT : (c + 1) * SLOT, :].reshape(512, 128)
    chunks = gather_extra(in_ref[:, SLOT * CH : SROWS, :].reshape(512, 128))
    for c in range(CH):
        x[512:544, c * 128 : c * 128 + 128] = chunks[c]
    loads[0].wait()
    hidden = dot(x[:, 0:768], w1[0:768, :])
    loads[1].wait()
    hidden = hidden + dot(x[:, 768:1536], w1[768:1536, :])
    gate = hidden[:, :FFE]
    active = (gate / (1.0 + jnp.exp(-gate)) * hidden[:, FFE:]).astype(BF)
    loads[2].wait()
    place = iota((512, NT), 0)
    owner = place // 16 == iota((512, NT), 1)
    extra = jnp.zeros((512, 128), F32)
    sent = []
    for c in range(0, CH, 2):
        out = dot(active, w2[:, c * 128 : c * 128 + 256]).astype(BF)
        for n in range(2):
            cols = slice(n * 128, n * 128 + 128)
            o[:, (c + n) * SLOT : (c + n + 1) * SLOT, :] = out[0:512, cols].reshape(NT, SLOT, 128)
            match = jnp.where(owner & (place % 16 == c + n), 1.0, 0.0).astype(BF)
            extra = extra + dot(match, out[512:544, cols])
        rows = pl.ds(c * SLOT, 2 * SLOT)
        sent.append(pltpu.make_async_copy(o.at[:, rows, :], o_ref.at[:, rows, :], out_sems.at[c // 2]))
        sent[-1].start()
    o[:, SLOT * CH : SROWS, :] = extra.astype(BF).reshape(NT, 16, 128)
    rows = pl.ds(CH * SLOT, 16)
    sent.append(pltpu.make_async_copy(o.at[:, rows, :], o_ref.at[:, rows, :], out_sems.at[CH // 2]))
    sent[-1].start()
    for copy in sent:
        copy.wait()


def expert(slots, up, down):
    return pl.pallas_call(
        expert_kernel,
        out_shape=jax.ShapeDtypeStruct((NT, SROWS, 128), BF),
        in_specs=[vmem()] + [pl.BlockSpec(memory_space=pltpu.HBM)] * 2,
        out_specs=pl.BlockSpec(memory_space=pltpu.HBM),
        scratch_shapes=[
            pltpu.VMEM((544, D), BF),
            pltpu.VMEM(up.shape, BF),
            pltpu.VMEM(down.shape, BF),
            pltpu.VMEM((NT, SROWS, 128), BF),
            pltpu.SemaphoreType.DMA((3,)),
            pltpu.SemaphoreType.DMA((CH // 2 + 1,)),
        ],
        compiler_params=params(58),
        cost_estimate=pl.CostEstimate(
            flops=2 * 544 * 1536 * 1536, bytes_accessed=9 << 20, transcendentals=544 * 512
        ),
        interpret=INTERPRET,
        name="expert",
    )(slots, up, down)


def combine_kernel(in_ref, res_ref, ids_ref, gate_ref, o_ref):
    experts = iota((TOK, NT), 1)
    named = jnp.zeros((TOK, NT), F32)
    gates = jnp.zeros((TOK, NT), F32)
    for k in range(TOPK):
        match = ids_ref[:, k : k + 1] == experts
        named = named + jnp.where(match, 1.0, 0.0)
        gates = gates + jnp.where(match, gate_ref[:, k : k + 1], 0.0)
    before = jnp.where(iota((TOK, TOK), 1) < iota((TOK, TOK), 0), 1.0, 0.0).astype(BF)
    rank = dot(before, named.astype(BF))
    rank = jnp.where(named > 0.5, rank, -1.0)
    spread = jnp.where(iota((NT, 512), 0) == iota((NT, 512), 1) // SLOT, 1.0, 0.0).astype(BF)
    place = (iota((TOK, 512), 1) % SLOT).astype(F32)
    pick = dot(rank.astype(BF), spread) == place
    high = gates.astype(BF)
    low = (gates - high.astype(F32)).astype(BF)
    weights = jnp.concatenate(
        [jnp.where(pick, dot(part, spread), 0.0).astype(BF) for part in (high, low)], 0
    )
    late = rank == float(SLOT)
    late_weights = jnp.concatenate(
        [jnp.where(late, part.astype(F32), 0.0).astype(BF) for part in (high, low)], 0
    )
    chunks = gather_extra(in_ref[:, SLOT * CH : SROWS, :].reshape(512, 128))
    for c in range(CH):
        main = in_ref[:, c * SLOT : (c + 1) * SLOT, :].reshape(512, 128)
        both = dot(weights, main) + dot(late_weights, chunks[c])
        cols = slice(c * 128, c * 128 + 128)
        o_ref[:, cols] = (res_ref[:, cols] + (both[:TOK] + both[TOK:])).astype(BF)


def combine(returned, residual, ids, gates):
    return pl.pallas_call(
        combine_kernel,
        out_shape=jax.ShapeDtypeStruct((TOK, D), BF),
        in_specs=[vmem()] * 4,
        out_specs=vmem(),
        compiler_params=params(32),
        interpret=INTERPRET,
        name="combine",
    )(returned, residual, ids, gates)


def shards(
    hidden_in,
    rotated_queries,
    fresh_key_values,
    cached_key_values,
    cached_len,
    expert_ids,
    route_gates,
    output_weight,
    norm_gain,
    gate_up,
    down_weight,
):
    zlo = lax.axis_index("zlo").astype(jnp.int32)
    x = lax.axis_index("x").astype(jnp.int32)
    core = lax.axis_index("core").astype(jnp.int32)
    length = cached_len[0]
    info = jnp.stack([length, core, x, zlo])
    ids = expert_ids[0, 0, 0]
    gates = route_gates[0, 0, 0]

    send = pack(rotated_queries[0, 0, 0], fresh_key_values[0, 0, 0], cached_key_values[0])
    plane_weight = lax.all_gather(output_weight, ("x", "core"), axis=0, tiled=True)
    packed = prepare(gate_up[0], down_weight[0], send)
    own = lax.all_to_all(send, ("zhi", "core"), split_axis=0, concat_axis=0, tiled=True)
    across = lax.ppermute(packed, "zlo", [(0, 1), (1, 0)])
    packed, across, own = lax.optimization_barrier((packed, across, own))
    both = merge(info, packed, across)
    spread = jnp.broadcast_to(own[None, :, 96:], (4, HKV, 96, 128))
    pairs = lax.all_to_all(spread, "x", split_axis=0, concat_axis=0, tiled=True)
    pairs, plane_weight, both = lax.optimization_barrier((pairs, plane_weight, both))
    weights = lax.all_gather(both, "y", axis=0, tiled=True)
    kept, sent = attention(info, own, pairs)
    swapped = lax.ppermute(sent, "core", [(0, 1), (1, 0)])
    terms = group_sums(info, kept, swapped, plane_weight)
    sums = lax.all_to_all(terms, "zhi", split_axis=0, concat_axis=0, tiled=True)
    residual, outbound = norm_dispatch(sums, hidden_in[0, 0, 0], norm_gain[None], ids.T)
    slots = lax.all_to_all(outbound, TEN, split_axis=0, concat_axis=0, tiled=True)
    computed = expert(slots, *unpack(weights))
    returned = lax.all_to_all(computed, TEN, split_axis=0, concat_axis=0, tiled=True)
    hidden_out = combine(returned, residual, ids, gates)

    low_x = x % 2
    mine = lax.dynamic_slice_in_dim(pairs, (low_x * 2 + core) * 32, 32, 3)
    for_other = lax.dynamic_slice_in_dim(pairs, (low_x * 2 + 1 - core) * 32, 32, 3)
    theirs = lax.ppermute(for_other, "core", [(0, 1), (1, 0)])
    chosen = jnp.where(core == x // 2, mine, theirs).reshape(4, 4, 2, 96, 32)
    chosen = jnp.transpose(chosen, (1, 0, 2, 3, 4)).reshape(NT, 96, 32)
    old_rows = chosen[:, :CROWS].reshape(NT * CROWS, 32)
    new_rows = chosen[:, CROWS:].reshape(NT * TOK, 32)
    total = NT * CROWS + NT * TOK
    base = jnp.concatenate([old_rows, jnp.zeros((NT * TOK, 32), BF)], 0)
    base = jnp.where((jnp.arange(total, dtype=jnp.int32) < length)[:, None], base, jnp.zeros_like(base))
    cache_out = lax.dynamic_update_slice_in_dim(base, new_rows, length, 0)
    return hidden_out.reshape(1, 1, 1, TOK, D), cache_out[None]


def solution(mesh):
    dp, tensor = mesh.devices.shape
    fine = Mesh(mesh.devices.reshape(dp // 2, 2, 4, 4, 2), ("y", "zlo", "zhi", "x", "core"))
    ydp = ("y", "zlo")
    return jax.shard_map(
        shards,
        mesh=fine,
        in_specs=(
            P(ydp, TEN, None, None, None),
            P(ydp, TEN, None, None, None),
            P(ydp, TEN, None, None, None),
            P(ydp, TEN, None),
            P(ydp),
            P(ydp, TEN, None, None, None),
            P(ydp, TEN, None, None, None),
            P(TEN, None),
            P(),
            P(TEN, ydp, None),
            P(TEN, ydp, None),
        ),
        out_specs=(P(ydp, TEN, None, None, None), P(ydp, None, TEN)),
        check_vma=False,
    )
```

```python
import functools
import math

import jax
import jax.numpy as jnp
from jax import lax
from jax.experimental import pallas as pl
from jax.experimental.pallas import tpu as pltpu
from jax.sharding import Mesh
from jax.sharding import PartitionSpec as P

D = 1536
HQ = 24
HKV = 8
HD = 64
FFE = 512
TOPK = 8
EPS = 1e-05
NT = 32
TOK = 64
CROWS = 32
SLOT = 16
CH = D // 128
SROWS = SLOT * CH + 16
BF = jnp.bfloat16
F32 = jnp.float32
TEN = ("zhi", "x", "core")
NEG = -1e30
INTERPRET = False


def vmem():
    return pl.BlockSpec(memory_space=pltpu.VMEM)


def params(mib):
    return pltpu.CompilerParams(vmem_limit_bytes=int(mib * (1 << 20)))


def dot(a, b):
    return lax.dot_general(a, b, (((1,), (0,)), ((), ())), preferred_element_type=F32)


def iota(shape, dim):
    return lax.broadcasted_iota(jnp.int32, shape, dim)


def pack_kernel(q_ref, f_ref, c_ref, o_ref):
    for g in range(HKV):
        cols = pl.ds(g * 128, 128)
        rows = q_ref[:, g * 192 : g * 192 + 192]
        o_ref[g, 0:64, :] = rows[:, :128]
        o_ref[g, 64:96, :] = jnp.concatenate([rows[0:32, 128:], rows[32:64, 128:]], 1)
        o_ref[g, 96:128, :] = c_ref[:, cols]
        o_ref[g, 128:192, :] = f_ref[:, cols]


def pack(queries, fresh, cache):
    return pl.pallas_call(
        pack_kernel,
        out_shape=jax.ShapeDtypeStruct((HKV, 192, 128), BF),
        in_specs=[vmem()] * 3,
        out_specs=vmem(),
        interpret=INTERPRET,
        name="pack",
    )(queries, fresh, cache)


def attention_kernel(info_ref, own_ref, pair_ref, keep_ref, send_ref, kv, vals, keys, sc, probs, bias_c, bias_d):
    b = pl.program_id(0)
    length, core, x = info_ref[0], info_ref[1], info_ref[2]

    @pl.when(b == 0)
    def _():
        for t in range(NT):
            src = pair_ref.at[t // 2 % 4, t // 8 * 2 + t % 2]
            kv[t * 32 : t * 32 + 32, :] = src[0:32, :]
            kv[1024 + t * 64 : 1088 + t * 64, :] = src[32:96, :]
        for t in range(6):
            some = kv[t * 512 : t * 512 + 512, :].astype(F32)
            vals[t * 512 : t * 512 + 512, :] = jnp.where(iota((512, 128), 1) < HD, 1.0, some).astype(BF)
            keys[:, t * 512 : t * 512 + 512] = some.T.astype(BF)
        bias_c[...] = jnp.where(iota((8, 1024), 1) < length, 0.0, NEG)
        query_at = x * 128 + iota((128, 512), 0)
        bias_d[...] = jnp.where(iota((128, 512), 1) <= query_at, 0.0, NEG)

    low = iota((128, 128), 1) < HD

    def block(b):
        first = own_ref[b * 2 : b * 2 + 2, 0:64, :].reshape(128, 128).astype(F32) * 0.125
        last = own_ref[b * 2 : b * 2 + 2, 64:96, :].reshape(64, 128).astype(F32) * 0.125
        turned = pltpu.roll(last, HD, 1)
        third = jnp.concatenate([last[0:32], turned[0:32], last[32:64], turned[32:64]], 0)
        heads = (first, pltpu.roll(first, HD, 1), third)
        q = jnp.concatenate([jnp.where(low, head, 0.0) for head in heads], 0).astype(BF)
        count = 3 + b
        top = jnp.full((384, 128), NEG, F32)
        for k in range(count):
            at = k * 512
            s = dot(q, keys[:, at : at + 512])
            if k < 2:
                s = s + bias_c[0:1, at : at + 512]
            elif k == count - 1:
                s = s + jnp.concatenate([bias_d[...]] * 3, 0)
            sc[k] = s
            for j in range(4):
                top = jnp.maximum(top, s[:, j * 128 : j * 128 + 128])
        highest = jnp.max(top, 1, keepdims=True)
        accs = []
        for h in range(3):
            rows = slice(h * 128, h * 128 + 128)
            for k in range(count):
                part = jnp.exp(sc[k, rows, :] - highest[rows])
                probs[rows, k * 512 : k * 512 + 512] = part.astype(BF)
            accs.append(dot(probs[rows, : count * 512], vals[: count * 512, :]))
        acc = jnp.concatenate(accs, 0)
        out = acc / pltpu.roll(acc, HD, 1)
        a0, a1, a2 = out[0:128], out[128:256], out[256:384]
        tiles = (
            jnp.where(low, pltpu.roll(a0, HD, 1), a1),
            jnp.where(low, pltpu.roll(a2, HD, 1), 0.0),
        )
        for n, tile in enumerate(tiles):
            even, odd = tile[0:64], tile[64:128]
            rows = slice(n * 64, n * 64 + 64)
            keep_ref[b, rows, :] = jnp.where(core == 0, even, odd).astype(BF)
            send_ref[b, rows, :] = jnp.where(core == 0, odd, even).astype(BF)

    for n in range(4):
        pl.when(b == n)(functools.partial(block, n))


def attention(info, own, pairs):
    shape = jax.ShapeDtypeStruct((4, 128, 128), BF)
    return pl.pallas_call(
        attention_kernel,
        out_shape=(shape, shape),
        grid=(4,),
        in_specs=[pl.BlockSpec(memory_space=pltpu.SMEM), vmem(), vmem()],
        out_specs=(vmem(), vmem()),
        scratch_shapes=[
            pltpu.VMEM((3072, 128), BF),
            pltpu.VMEM((3072, 128), BF),
            pltpu.VMEM((128, 3072), BF),
            pltpu.VMEM((6, 384, 512), F32),
            pltpu.VMEM((384, 3072), BF),
            pltpu.VMEM((8, 1024), F32),
            pltpu.VMEM((128, 512), F32),
        ],
        compiler_params=params(32),
        cost_estimate=pl.CostEstimate(
            flops=2 * 2 * 1536 * 2304 * 128, bytes_accessed=3 << 20, transcendentals=1536 * 2304
        ),
        interpret=INTERPRET,
        name="attention",
    )(info, own, pairs)


def group_sums_kernel(info_ref, own_ref, oth_ref, w, o_ref, o, out_sems):
    core = info_ref[1]
    sides = ((own_ref, core), (oth_ref, 1 - core))
    pairs = [src[:, 0:64, :].reshape(256, 128) for src, _ in sides]
    lasts = [src[:, 64:128, :].reshape(256, 128)[:, :HD] for src, _ in sides]
    sent = []
    for n in range(3):
        cols = pl.ds(n * 512, 512)
        total = jnp.zeros((256, 512), F32)
        for pair, last, (_, side) in zip(pairs, lasts, sides):
            at = pl.multiple_of(side * 192, 64)
            total = total + dot(pair, w[pl.ds(at, 128), cols])
            total = total + dot(last, w[pl.ds(pl.multiple_of(at + 128, 64), HD), cols])
        o[:, :, cols] = total.astype(BF).reshape(4, TOK, 512)
        sent.append(pltpu.make_async_copy(o.at[:, :, cols], o_ref.at[:, :, cols], out_sems.at[n]))
        sent[-1].start()
    for copy in sent:
        copy.wait()


def group_sums(info, own, other, weight):
    return pl.pallas_call(
        group_sums_kernel,
        out_shape=jax.ShapeDtypeStruct((4, TOK, D), BF),
        in_specs=[pl.BlockSpec(memory_space=pltpu.SMEM)] + [vmem()] * 3,
        out_specs=pl.BlockSpec(memory_space=pltpu.HBM),
        scratch_shapes=[
            pltpu.VMEM((4, TOK, D), BF),
            pltpu.SemaphoreType.DMA((3,)),
        ],
        compiler_params=params(20),
        cost_estimate=pl.CostEstimate(flops=2 * 256 * 384 * D, bytes_accessed=2 << 20, transcendentals=0),
        interpret=INTERPRET,
        name="group_sums",
    )(info, own, other, weight)


def prepare_kernel(up_ref, down_ref, after_ref, o_ref):
    o_ref[0:64, 0:1024] = up_ref[0:64, :]
    o_ref[0:32, 1024:1536] = up_ref[64:96, 0:512]
    o_ref[32:64, 1024:1536] = up_ref[64:96, 512:1024]
    o_ref[64:96, :] = down_ref[...]


def prepare(up, down, after):
    return pl.pallas_call(
        prepare_kernel,
        out_shape=jax.ShapeDtypeStruct((96, D), BF),
        in_specs=[vmem()] * 2 + [pl.BlockSpec(memory_space=pl.ANY)],
        out_specs=vmem(),
        cost_estimate=pl.CostEstimate(flops=1 << 33, bytes_accessed=1 << 20, transcendentals=0),
        interpret=INTERPRET,
        name="prepare",
    )(up, down, after)


def norm_dispatch_kernel(sum_ref, hid_ref, gain_ref, ids_ref, res_ref, disp_ref):
    experts = iota((NT, TOK), 0)
    named = jnp.zeros((NT, TOK), F32)
    for k in range(TOPK):
        named = named + jnp.where(ids_ref[k : k + 1, :] == experts, 1.0, 0.0)
    before = jnp.where(iota((TOK, TOK), 0) < iota((TOK, TOK), 1), 1.0, 0.0).astype(BF)
    rank = dot(named.astype(BF), before)
    rank = jnp.where(named > 0.5, rank, -1.0).astype(BF)
    spread = jnp.where(iota((512, NT), 0) // SLOT == iota((512, NT), 1), 1.0, 0.0).astype(BF)
    ranks = dot(spread, rank)
    place = iota((512, TOK), 0) % SLOT
    pick = jnp.where(ranks == place.astype(F32), 1.0, 0.0).astype(BF)
    late = jnp.where(ranks == float(SLOT), 1.0, 0.0)

    total = hid_ref[...].astype(F32)
    for z in range(4):
        total = total + sum_ref[z].astype(F32)
    res_ref[...] = total
    meansq = jnp.mean(total * total, 1, keepdims=True)
    normed = (total * lax.rsqrt(meansq + EPS) * gain_ref[...]).astype(BF)
    extra = jnp.zeros((512, 128), F32)
    for c in range(CH):
        chunk = normed[:, c * 128 : c * 128 + 128]
        disp_ref[:, c * SLOT : (c + 1) * SLOT, :] = (
            dot(pick, chunk).astype(BF).reshape(NT, SLOT, 128)
        )
        extra = extra + dot(jnp.where(place == c, late, 0.0).astype(BF), chunk)
    disp_ref[:, SLOT * CH : SROWS, :] = extra.astype(BF).reshape(NT, 16, 128)


def norm_dispatch(sums, hidden, gain, ids_t):
    return pl.pallas_call(
        norm_dispatch_kernel,
        out_shape=(
            jax.ShapeDtypeStruct((TOK, D), F32),
            jax.ShapeDtypeStruct((NT, SROWS, 128), BF),
        ),
        in_specs=[vmem()] * 4,
        out_specs=(vmem(), vmem()),
        compiler_params=params(32),
        cost_estimate=pl.CostEstimate(flops=1 << 30, bytes_accessed=4 << 20, transcendentals=0),
        interpret=INTERPRET,
        name="norm_dispatch",
    )(sums, hidden, gain, ids_t)


def gather_extra(block):
    rows = iota((CH * NT, 512), 0)
    cols = iota((CH * NT, 512), 1)
    match = (rows % NT == cols // 16) & (rows // NT == cols % 16)
    stacked = dot(jnp.where(match, 1.0, 0.0).astype(BF), block).astype(BF)
    return [stacked[c * NT : (c + 1) * NT, :] for c in range(CH)]


def merge_kernel(info_ref, own_ref, oth_ref, o_ref):
    zlo = info_ref[3]
    o_ref[zlo] = own_ref[...]
    o_ref[1 - zlo] = oth_ref[...]


def merge(info, own, other):
    return pl.pallas_call(
        merge_kernel,
        out_shape=jax.ShapeDtypeStruct((2,) + own.shape, BF),
        in_specs=[
            pl.BlockSpec(memory_space=pltpu.SMEM),
            vmem(),
            vmem(),
        ],
        out_specs=vmem(),
        cost_estimate=pl.CostEstimate(flops=1 << 33, bytes_accessed=1 << 20, transcendentals=0),
        interpret=INTERPRET,
        name="merge",
    )(info, own, other)


def unpack_kernel(src, w1_ref, w2_ref):
    for d in range(src.shape[0]):
        top = d * 96
        w1_ref[top : top + 64, :] = src[d, 0:64, 0:1024]
        w1_ref[top + 64 : top + 96, 0:512] = src[d, 0:32, 1024:1536]
        w1_ref[top + 64 : top + 96, 512:1024] = src[d, 32:64, 1024:1536]
        w2_ref[d * 32 : d * 32 + 32, :] = src[d, 64:96, :]


def unpack(weights):
    blocks = weights.shape[0]
    return pl.pallas_call(
        unpack_kernel,
        out_shape=(
            jax.ShapeDtypeStruct((blocks * 96, 2 * FFE), BF),
            jax.ShapeDtypeStruct((blocks * 32, D), BF),
        ),
        in_specs=[vmem()],
        out_specs=(vmem(), vmem()),
        compiler_params=params(20),
        interpret=INTERPRET,
        name="unpack",
    )(weights)


def expert_kernel(in_ref, up_ref, down_ref, o_ref, x, w1, w2, o, sems, out_sems):
    loads = [
        pltpu.make_async_copy(src.at[rows, :], dst.at[rows, :], sems.at[n])
        for n, (src, dst, rows) in enumerate(
            ((up_ref, w1, pl.ds(0, 768)), (up_ref, w1, pl.ds(768, 768)), (down_ref, w2, pl.ds(0, FFE)))
        )
    ]
    for copy in loads:
        copy.start()
    for c in range(CH):
        x[0:512, c * 128 : c * 128 + 128] = in_ref[:, c * SLOT : (c + 1) * SLOT, :].reshape(512, 128)
    chunks = gather_extra(in_ref[:, SLOT * CH : SROWS, :].reshape(512, 128))
    for c in range(CH):
        x[512:544, c * 128 : c * 128 + 128] = chunks[c]
    loads[0].wait()
    hidden = dot(x[:, 0:768], w1[0:768, :])
    loads[1].wait()
    hidden = hidden + dot(x[:, 768:1536], w1[768:1536, :])
    gate = hidden[:, :FFE]
    active = (gate / (1.0 + jnp.exp(-gate)) * hidden[:, FFE:]).astype(BF)
    loads[2].wait()
    place = iota((512, NT), 0)
    owner = place // 16 == iota((512, NT), 1)
    extra = jnp.zeros((512, 128), F32)
    sent = []
    for c in range(0, CH, 2):
        out = dot(active, w2[:, c * 128 : c * 128 + 256]).astype(BF)
        for n in range(2):
            cols = slice(n * 128, n * 128 + 128)
            o[:, (c + n) * SLOT : (c + n + 1) * SLOT, :] = out[0:512, cols].reshape(NT, SLOT, 128)
            match = jnp.where(owner & (place % 16 == c + n), 1.0, 0.0).astype(BF)
            extra = extra + dot(match, out[512:544, cols])
        rows = pl.ds(c * SLOT, 2 * SLOT)
        sent.append(pltpu.make_async_copy(o.at[:, rows, :], o_ref.at[:, rows, :], out_sems.at[c // 2]))
        sent[-1].start()
    o[:, SLOT * CH : SROWS, :] = extra.astype(BF).reshape(NT, 16, 128)
    rows = pl.ds(CH * SLOT, 16)
    sent.append(pltpu.make_async_copy(o.at[:, rows, :], o_ref.at[:, rows, :], out_sems.at[CH // 2]))
    sent[-1].start()
    for copy in sent:
        copy.wait()


def expert(slots, up, down):
    return pl.pallas_call(
        expert_kernel,
        out_shape=jax.ShapeDtypeStruct((NT, SROWS, 128), BF),
        in_specs=[vmem()] + [pl.BlockSpec(memory_space=pltpu.HBM)] * 2,
        out_specs=pl.BlockSpec(memory_space=pltpu.HBM),
        scratch_shapes=[
            pltpu.VMEM((544, D), BF),
            pltpu.VMEM(up.shape, BF),
            pltpu.VMEM(down.shape, BF),
            pltpu.VMEM((NT, SROWS, 128), BF),
            pltpu.SemaphoreType.DMA((3,)),
            pltpu.SemaphoreType.DMA((CH // 2 + 1,)),
        ],
        compiler_params=params(58),
        cost_estimate=pl.CostEstimate(
            flops=2 * 544 * 1536 * 1536, bytes_accessed=9 << 20, transcendentals=544 * 512
        ),
        interpret=INTERPRET,
        name="expert",
    )(slots, up, down)


def combine_kernel(in_ref, res_ref, ids_ref, gate_ref, o_ref):
    experts = iota((TOK, NT), 1)
    named = jnp.zeros((TOK, NT), F32)
    gates = jnp.zeros((TOK, NT), F32)
    for k in range(TOPK):
        match = ids_ref[:, k : k + 1] == experts
        named = named + jnp.where(match, 1.0, 0.0)
        gates = gates + jnp.where(match, gate_ref[:, k : k + 1], 0.0)
    before = jnp.where(iota((TOK, TOK), 1) < iota((TOK, TOK), 0), 1.0, 0.0).astype(BF)
    rank = dot(before, named.astype(BF))
    rank = jnp.where(named > 0.5, rank, -1.0)
    spread = jnp.where(iota((NT, 512), 0) == iota((NT, 512), 1) // SLOT, 1.0, 0.0).astype(BF)
    place = (iota((TOK, 512), 1) % SLOT).astype(F32)
    pick = dot(rank.astype(BF), spread) == place
    high = gates.astype(BF)
    low = (gates - high.astype(F32)).astype(BF)
    weights = jnp.concatenate(
        [jnp.where(pick, dot(part, spread), 0.0).astype(BF) for part in (high, low)], 0
    )
    late = rank == float(SLOT)
    late_weights = jnp.concatenate(
        [jnp.where(late, part.astype(F32), 0.0).astype(BF) for part in (high, low)], 0
    )
    chunks = gather_extra(in_ref[:, SLOT * CH : SROWS, :].reshape(512, 128))
    for c in range(CH):
        main = in_ref[:, c * SLOT : (c + 1) * SLOT, :].reshape(512, 128)
        both = dot(weights, main) + dot(late_weights, chunks[c])
        cols = slice(c * 128, c * 128 + 128)
        o_ref[:, cols] = (res_ref[:, cols] + (both[:TOK] + both[TOK:])).astype(BF)


def combine(returned, residual, ids, gates):
    return pl.pallas_call(
        combine_kernel,
        out_shape=jax.ShapeDtypeStruct((TOK, D), BF),
        in_specs=[vmem()] * 4,
        out_specs=vmem(),
        compiler_params=params(32),
        interpret=INTERPRET,
        name="combine",
    )(returned, residual, ids, gates)


def shards(
    hidden_in,
    rotated_queries,
    fresh_key_values,
    cached_key_values,
    cached_len,
    expert_ids,
    route_gates,
    output_weight,
    norm_gain,
    gate_up,
    down_weight,
):
    zlo = lax.axis_index("zlo").astype(jnp.int32)
    x = lax.axis_index("x").astype(jnp.int32)
    core = lax.axis_index("core").astype(jnp.int32)
    length = cached_len[0]
    info = jnp.stack([length, core, x, zlo])
    ids = expert_ids[0, 0, 0]
    gates = route_gates[0, 0, 0]

    send = pack(rotated_queries[0, 0, 0], fresh_key_values[0, 0, 0], cached_key_values[0])
    plane_weight = lax.all_gather(output_weight, ("x", "core"), axis=0, tiled=True)
    packed = prepare(gate_up[0], down_weight[0], send)
    own = lax.all_to_all(send, ("zhi", "core"), split_axis=0, concat_axis=0, tiled=True)
    packed, own = lax.optimization_barrier((packed, own))
    across = lax.ppermute(packed, "zlo", [(0, 1), (1, 0)])
    both = merge(info, packed, across)
    spread = jnp.broadcast_to(own[None, :, 96:], (4, HKV, 96, 128))
    pairs = lax.all_to_all(spread, "x", split_axis=0, concat_axis=0, tiled=True)
    pairs, plane_weight, both = lax.optimization_barrier((pairs, plane_weight, both))
    weights = lax.all_gather(both, "y", axis=0, tiled=True)
    kept, sent = attention(info, own, pairs)
    swapped = lax.ppermute(sent, "core", [(0, 1), (1, 0)])
    terms = group_sums(info, kept, swapped, plane_weight)
    sums = lax.all_to_all(terms, "zhi", split_axis=0, concat_axis=0, tiled=True)
    residual, outbound = norm_dispatch(sums, hidden_in[0, 0, 0], norm_gain[None], ids.T)
    slots = lax.all_to_all(outbound, TEN, split_axis=0, concat_axis=0, tiled=True)
    computed = expert(slots, *unpack(weights))
    returned = lax.all_to_all(computed, TEN, split_axis=0, concat_axis=0, tiled=True)
    hidden_out = combine(returned, residual, ids, gates)

    low_x = x % 2
    mine = lax.dynamic_slice_in_dim(pairs, (low_x * 2 + core) * 32, 32, 3)
    for_other = lax.dynamic_slice_in_dim(pairs, (low_x * 2 + 1 - core) * 32, 32, 3)
    theirs = lax.ppermute(for_other, "core", [(0, 1), (1, 0)])
    chosen = jnp.where(core == x // 2, mine, theirs).reshape(4, 4, 2, 96, 32)
    chosen = jnp.transpose(chosen, (1, 0, 2, 3, 4)).reshape(NT, 96, 32)
    old_rows = chosen[:, :CROWS].reshape(NT * CROWS, 32)
    new_rows = chosen[:, CROWS:].reshape(NT * TOK, 32)
    total = NT * CROWS + NT * TOK
    base = jnp.concatenate([old_rows, jnp.zeros((NT * TOK, 32), BF)], 0)
    base = jnp.where((jnp.arange(total, dtype=jnp.int32) < length)[:, None], base, jnp.zeros_like(base))
    cache_out = lax.dynamic_update_slice_in_dim(base, new_rows, length, 0)
    return hidden_out.reshape(1, 1, 1, TOK, D), cache_out[None]


def solution(mesh):
    dp, tensor = mesh.devices.shape
    fine = Mesh(mesh.devices.reshape(dp // 2, 2, 4, 4, 2), ("y", "zlo", "zhi", "x", "core"))
    ydp = ("y", "zlo")
    return jax.shard_map(
        shards,
        mesh=fine,
        in_specs=(
            P(ydp, TEN, None, None, None),
            P(ydp, TEN, None, None, None),
            P(ydp, TEN, None, None, None),
            P(ydp, TEN, None),
            P(ydp),
            P(ydp, TEN, None, None, None),
            P(ydp, TEN, None, None, None),
            P(TEN, None),
            P(),
            P(TEN, ydp, None),
            P(TEN, ydp, None),
        ),
        out_specs=(P(ydp, TEN, None, None, None), P(ydp, None, TEN)),
        check_vma=False,
    )
```
